128 devices in a mesh: head: 16 (over y, z), seq: 8 (over x, core).
Axes of the slice: x: 4, y: 4, z: 4, core: 2. Of those that a mesh axis runs over, the one named last changes fastest.
Arguments:
- query_rows: bfloat16 [2, 8192, 4096], P(None, ('seq', 'head')), may hold values from -6 to 6
- key_rows: bfloat16 [2, 8192, 4096], P(None, ('seq', 'head')), may hold values from -6 to 6
- value_rows: bfloat16 [2, 8192, 4096], P(None, ('seq', 'head')), may hold values from -6 to 6
- beta_raw: bfloat16 [2, 8192, 32], P(None, ('seq', 'head')), may hold values from -5 to 5
- gate_latent: bfloat16 [2, 8192, 128], P(None, ('seq', 'head')), may hold values from -3 to 3
- gate_up: bfloat16 [128, 4096], replicated, may hold values from -1 to 1
- dt_bias: float32 [2, 4096], replicated, may hold values from -13 to -1
- decay_log: float32 [32], replicated, may hold values from -0.5 to 0.5
- boundary: int32 [2, 8192], P(None, ('seq', 'head')), may hold values 0 or 1
- modality: int32 [2, 8192], P(None, ('seq', 'head')), may hold values from 0 to 1, as said below
- out_gate: bfloat16 [2, 8192, 4096], P(None, ('seq', 'head')), may hold values from -6 to 6
- norm_gain: float32 [4096], replicated, may hold values from 0.1 to 1.9
Outputs:
- mixed_out: bfloat16 [2, 8192, 4096], P(None, ('seq', 'head'))
The draws below stay inside these ranges and needn't reach their ends.
Inputs may be any that keep to these rules, and one draw needn't show every extreme that they name: `modality`: each sequence has runs of audio and runs of text; the value changes at a few positions.
All inputs are finite; a program needn't handle non-finite values. No bound on the sum of `boundary` on one device may be relied on, other than what follows from the above.
Results may differ from the reference program's by a relative error of at most 0.0049.
Values may be sent and summed in bfloat16 or wider, within the bound.
A program may use at most 128 MiB of HBM per device.

```python
import math
import jax
import jax.numpy as jnp
from jax import lax

H = 32
DK = 128
RANK = 128
BATCH = 2
BLOCK = 128
LENGTH = 8192
HD = 4096


def draw_gate_up(key, part):
    normal_raw = jax.random.normal(key, (RANK, H * DK), jnp.float32)
    return (jnp.clip(normal_raw, -3.0, 3.0) * (0.5 / math.sqrt(RANK))).astype(jnp.bfloat16)


def draw_dt_bias(key, part):
    key_pick, key_fast, key_slow, key_text = jax.random.split(jax.random.fold_in(key, 11), 4)
    columns = H * DK
    slow_share = 0.5
    selector = jax.random.uniform(key_pick, (columns,))
    fast_rate = jnp.exp(jax.random.uniform(key_fast, (columns,), minval=math.log(1.0 / 64.0), maxval=math.log(1.0 / 16.0)))
    slow_rate = jnp.exp(jax.random.uniform(key_slow, (columns,), minval=math.log(0.1), maxval=math.log(0.5))) / LENGTH
    rates = jnp.where(selector < slow_share, slow_rate, fast_rate)
    audio_row = jnp.log(jnp.expm1(rates))
    text_row = audio_row + jnp.log(jax.random.uniform(key_text, (columns,), minval=1.5, maxval=3.0))
    return jnp.stack([audio_row, text_row]).astype(jnp.float32)


def draw_modality(key, part):
    key_ticks, key_start = jax.random.split(jax.random.fold_in(key, 23))
    random_ticks = jax.random.randint(key_ticks, (BATCH, LENGTH), 0, LENGTH)
    switch_mask = (random_ticks < 16).astype(jnp.int32)
    midpoint = (lax.broadcasted_iota(jnp.int32, (BATCH, LENGTH), 1) == LENGTH // 2).astype(jnp.int32)
    opening = jax.random.randint(key_start, (BATCH, 1), 0, 2)
    return (jnp.cumsum(jnp.maximum(switch_mask, midpoint), axis=1) + opening) % 2


def place_ends(entries, rng, low, largest):
    longest = entries.shape.index(max(entries.shape))
    spots = []
    for shift in (0, 1):
        where = [jax.random.randint(jax.random.fold_in(rng, axis), (), 0, length) for axis, length in enumerate(entries.shape)]
        where[longest] = (where[longest] + shift) % entries.shape[longest]
        spots.append(tuple(where))
    return entries.at[spots[0]].set(low).at[spots[1]].set(largest)


def shard_levels(rng, dims, cuts, low, largest):
    loudness, own = 1.0, jax.random.fold_in(rng, 6)
    for position, parts in cuts:
        heights = jnp.exp(jax.random.uniform(jax.random.fold_in(own, position), (parts,), jnp.float32, low / len(cuts), largest / len(cuts)))
        loudness = loudness * jnp.repeat(heights, dims[position] // parts).reshape([-1 if axis == position else 1 for axis in range(len(dims))])
    return loudness


def gaussian(own_key, dims, spread, bound, cuts=(), kind=jnp.bfloat16):
    values = jax.random.normal(own_key, dims, jnp.float32) * spread
    if len(cuts) > 0:
        values = shard_levels(own_key, dims, cuts, -0.22, 0.18) * values
    return jnp.clip(values, min=-bound, max=bound).astype(kind)


def setup_inputs(seed: int = 0) -> dict:
    key_list = jax.random.split(jax.random.key(seed), 13)
    query_rows = gaussian(key_list[0], (BATCH, LENGTH, HD), 1.0, 6.0, ((1, 128),))
    key_rows = gaussian(key_list[1], (BATCH, LENGTH, HD), 1.0, 6.0, ((1, 128),))
    value_rows = gaussian(key_list[2], (BATCH, LENGTH, HD), 1.0, 6.0, ((1, 128),))
    beta_raw = gaussian(key_list[3], (BATCH, LENGTH, H), 1.0, 5.0, ((1, 128),))
    gate_latent = gaussian(key_list[4], (BATCH, LENGTH, RANK), 1.0, 3.0, ((1, 128),))
    gate_up = draw_gate_up(jax.random.fold_in(key_list[12], 71), 0)
    dt_bias = draw_dt_bias(jax.random.fold_in(key_list[12], 71), 0)
    decay_log = jnp.clip(jax.random.uniform(key_list[7], (H,), jnp.float32, -0.5, 0.5), -0.5, 0.5)
    boundary = place_ends((jax.random.randint(key_list[8], (BATCH, LENGTH), 0, LENGTH) < 2).astype(jnp.int32), jax.random.fold_in(key_list[8], 1), 0, 1)
    modality = draw_modality(jax.random.fold_in(key_list[12], 71), 0)
    out_gate = gaussian(key_list[10], (BATCH, LENGTH, HD), 1.0, 6.0, ((1, 128),))
    norm_gain = jnp.clip(1.0 + 0.18 * jax.random.normal(key_list[11], (HD,), jnp.float32), 0.1, 1.9)
    return dict(query_rows=query_rows, key_rows=key_rows, value_rows=value_rows, beta_raw=beta_raw, gate_latent=gate_latent, gate_up=gate_up, dt_bias=dt_bias, decay_log=decay_log, boundary=boundary, modality=modality, out_gate=out_gate, norm_gain=norm_gain)


exact_mode = lax.Precision.HIGHEST
norm_eps = 1e-06

def product(left_side, right_side):
    return jnp.matmul(left_side, right_side, precision=exact_mode)

def unit_rows(matrix):
    return matrix * lax.rsqrt(lax.optimization_barrier(jnp.sum(matrix * matrix, axis=-1, keepdims=True)) + norm_eps)

def invert_unit_lower(strict):
    length = strict.shape[-1]
    unit_mat = jnp.eye(length, dtype=jnp.float32)
    nil_power = -strict
    result = unit_mat + nil_power
    for repeat in range(1, length.bit_length() - 1):
        nil_power = product(nil_power, nil_power)
        result = product(result, unit_mat + nil_power)
    return result

def block_parts(query_block, key_block, value_block, beta_block, decay_block, mark_block):
    length = query_block.shape[-2]
    decay_sum = jnp.cumsum(decay_block, axis=-2)
    counts = jnp.cumsum(mark_block, axis=-1)
    alive_rows = (counts == 0).astype(jnp.float32)
    same_doc = (counts[..., :, None] == counts[..., None, :]).astype(jnp.float32)
    row_ids = lax.broadcasted_iota(jnp.int32, (length, length), 0)
    col_ids = lax.broadcasted_iota(jnp.int32, (length, length), 1)
    strict_low = (row_ids > col_ids).astype(jnp.float32)
    with_diag = (row_ids >= col_ids).astype(jnp.float32)
    growth = jnp.exp(decay_sum)
    key_grow = key_block * growth
    key_shrink = key_block * jnp.exp(-decay_sum)
    key_gram = jnp.einsum('...ik,...jk->...ij', key_grow, key_shrink, precision=exact_mode)
    strict = key_gram * strict_low * same_doc * beta_block[..., :, None]
    solver = invert_unit_lower(strict) * beta_block[..., None, :]
    weight_rows = product(solver, key_grow * alive_rows[..., :, None])
    pseudo_rows = product(solver, value_block)
    query_grow = query_block * growth
    mixing = jnp.einsum('...ik,...jk->...ij', query_grow, key_shrink, precision=exact_mode) * with_diag * same_doc
    query_live = query_grow * alive_rows[..., :, None]
    last_sum = decay_sum[..., -1:, :]
    key_tail = key_block * jnp.exp(last_sum - decay_sum) * same_doc[..., -1, :][..., :, None]
    carry_decay = jnp.exp(last_sum[..., 0, :]) * alive_rows[..., -1:]
    return (weight_rows, pseudo_rows, mixing, query_live, key_tail, carry_decay)

def reference(query_rows, key_rows, value_rows, beta_raw, gate_latent, gate_up, dt_bias, decay_log, boundary, modality, out_gate, norm_gain):
    seq_count, length, columns = query_rows.shape
    gate_pre = jnp.dot(gate_latent.reshape(-1, RANK), gate_up, preferred_element_type=jnp.float32)
    gate_pre = gate_pre.astype(jnp.bfloat16).reshape(seq_count, length, columns)
    gate_bias = jnp.where(modality[..., None] == 1, dt_bias[1], dt_bias[0])
    rate_scale = jnp.repeat(jnp.exp(decay_log), DK)
    log_decay = -rate_scale * jax.nn.softplus(gate_pre.astype(jnp.float32) + gate_bias)
    unit_query = unit_rows(query_rows.astype(jnp.float32).reshape(seq_count, length, H, DK)) * DK ** (-0.5)
    unit_key = unit_rows(key_rows.astype(jnp.float32).reshape(seq_count, length, H, DK))
    value_wide = value_rows.astype(jnp.float32).reshape(seq_count, length, H, DK)
    beta_gate = jax.nn.sigmoid(beta_raw.astype(jnp.float32))
    blocks = length // BLOCK

    def to_blocks(tensor):
        return tensor.reshape(seq_count, blocks, BLOCK, H, DK).transpose(1, 0, 3, 2, 4)
    beta_blocks = beta_gate.reshape(seq_count, blocks, BLOCK, H).transpose(1, 0, 3, 2)
    mark_blocks = jnp.broadcast_to(boundary.reshape(seq_count, blocks, 1, BLOCK).transpose(1, 0, 2, 3), (blocks, seq_count, H, BLOCK))

    def advance(carried, inputs):
        weight_rows, pseudo_rows, mixing, query_live, key_tail, carry_decay = block_parts(*inputs)
        fresh_rows = pseudo_rows - product(weight_rows, carried)
        core_out = product(query_live, carried) + product(mixing, fresh_rows)
        carried = carry_decay[..., :, None] * carried + jnp.einsum('...ck,...cv->...kv', key_tail, fresh_rows, precision=exact_mode)
        return (carried, core_out)
    zero_state = jnp.zeros((seq_count, H, DK, DK), jnp.float32)
    finish, cores = lax.scan(advance, zero_state, (to_blocks(unit_query), to_blocks(unit_key), to_blocks(value_wide), beta_blocks, to_blocks(log_decay.reshape(seq_count, length, H, DK)), mark_blocks))
    core_out = cores.transpose(1, 0, 3, 2, 4).reshape(seq_count, length, columns).astype(jnp.bfloat16)
    core_wide = core_out.astype(jnp.float32).reshape(seq_count, length, H, DK)
    normed = core_wide * lax.rsqrt(lax.optimization_barrier(jnp.mean(core_wide * core_wide, axis=-1, keepdims=True)) + norm_eps)
    mixed_out = normed.reshape(seq_count, length, columns) * norm_gain * jax.nn.sigmoid(out_gate.astype(jnp.float32))
    return mixed_out.astype(jnp.bfloat16)
```

```python
import functools

import jax
import jax.numpy as jnp
from jax import lax
from jax.experimental import pallas as pl
from jax.experimental.pallas import tpu as pltpu
from jax.sharding import PartitionSpec as P

H = 32
DK = 128
TOK = 64
C = 128
SPAN = 2048
GROUPS = 16
OWNERS = 32
NORM_EPS = 1e-6
MESH = pl.DeviceIdType.MESH
F32 = jnp.float32
BF16 = jnp.bfloat16
ANY = pl.BlockSpec(memory_space=pl.ANY)
VM = pl.BlockSpec(memory_space=pltpu.VMEM)


def place():
    group = lax.axis_index("head")
    seq = lax.axis_index("seq")
    core = lax.rem(seq, 2)
    return group, seq, core, group * 2 + core, core * GROUPS + group


def owner_id(owner, seq, core):
    return {"head": owner // 2, "seq": seq - core + lax.rem(owner, 2)}


def greet(seq, core, me):
    barrier = pltpu.get_barrier_semaphore()

    def one(step, carry):
        other = lax.rem(me + step, OWNERS)
        pl.semaphore_signal(
            barrier, inc=1, device_id=owner_id(other, seq, core), device_id_type=MESH
        )
        return carry

    lax.fori_loop(1, OWNERS, one, 0)
    return barrier


def entry_kernel(
    q_in, k_in, v_in, lat_in, aux_in, q_out, k_out, v_out, lat_out, aux_out, send, recv
):
    group, seq, core, me, blk = place()
    barrier = greet(seq, core, me)
    pl.semaphore_wait(barrier, OWNERS - 1)
    rows = pl.ds(pl.multiple_of(blk * TOK, TOK), TOK)

    def lat_send(step, carry):
        other = lax.rem(group + step, GROUPS)
        pltpu.make_async_remote_copy(
            lat_in, lat_out.at[:, rows, :], send.at[3], recv.at[3],
            device_id={"head": other, "seq": seq}, device_id_type=MESH,
        ).start()
        return carry

    lax.fori_loop(1, GROUPS, lat_send, 0)
    pltpu.make_async_copy(lat_in, lat_out.at[:, rows, :], recv.at[3]).start()

    def aux_send(step, carry):
        other = lax.rem(me + step, OWNERS)
        pltpu.make_async_remote_copy(
            aux_in.at[other], aux_out.at[blk], send.at[4], recv.at[4],
            device_id=owner_id(other, seq, core), device_id_type=MESH,
        ).start()
        return carry

    lax.fori_loop(1, OWNERS, aux_send, 0)
    pltpu.make_async_copy(aux_in.at[me], aux_out.at[blk], recv.at[4]).start()

    for slot, src, dst in ((0, k_in, k_out), (1, v_in, v_out), (2, q_in, q_out)):

        def piece_send(step, carry, slot=slot, src=src, dst=dst):
            other = lax.rem(me + step, OWNERS)
            cols = pl.ds(pl.multiple_of(other * DK, DK), DK)
            pltpu.make_async_remote_copy(
                src.at[:, :, cols], dst.at[:, rows, :], send.at[slot], recv.at[slot],
                device_id=owner_id(other, seq, core), device_id_type=MESH,
            ).start()
            return carry

        lax.fori_loop(1, OWNERS, piece_send, 0)
        own = pl.ds(pl.multiple_of(me * DK, DK), DK)
        pltpu.make_async_copy(src.at[:, :, own], dst.at[:, rows, :], recv.at[slot]).start()

    half = pl.ds(pl.multiple_of(core * 1024, 1024), 1024)
    mine = lat_out.at[:, half, :]
    pltpu.make_async_copy(mine, mine, recv.at[3]).wait()
    pass_on = pltpu.make_async_remote_copy(
        mine, mine, send.at[5], recv.at[5],
        device_id={"seq": seq + 1 - 2 * core}, device_id_type=MESH,
    )
    pass_on.start()
    for slot, dst in ((4, aux_out), (0, k_out), (1, v_out), (2, q_out)):
        pltpu.make_async_copy(dst, dst, recv.at[slot]).wait()
    pass_on.wait()
    sent = k_in.at[:, :, pl.ds(0, (OWNERS - 1) * DK)]
    for slot in (0, 1, 2):
        pltpu.make_async_copy(sent, sent, send.at[slot]).wait()
    lat_sent = lat_out.at[:, pl.ds(0, (GROUPS - 1) * TOK), :]
    pltpu.make_async_copy(lat_sent, lat_sent, send.at[3]).wait()
    aux_sent = aux_in.at[pl.ds(0, OWNERS - 1)]
    pltpu.make_async_copy(aux_sent, aux_sent, send.at[4]).wait()


def entry_exchange(q, k, v, lat, aux):
    wide = jax.ShapeDtypeStruct((2, SPAN, DK), BF16)
    return pl.pallas_call(
        entry_kernel,
        out_shape=(wide, wide, wide, wide, jax.ShapeDtypeStruct((OWNERS, 8, 128), BF16)),
        in_specs=[ANY] * 5,
        out_specs=(ANY,) * 5,
        scratch_shapes=[pltpu.SemaphoreType.DMA((6,)), pltpu.SemaphoreType.DMA((6,))],
        compiler_params=pltpu.CompilerParams(collective_id=0, has_side_effects=True),
        name="entry_exchange",
    )(q, k, v, lat, aux)


def halves(x):
    high = x.astype(BF16)
    return high, (x - high.astype(F32)).astype(BF16)


def fine_dot(left, right):
    lh, ll = halves(left)
    rh, rl = halves(right)
    return jnp.dot(
        jnp.concatenate([lh, ll, lh], axis=1),
        jnp.concatenate([rh, rh, rl], axis=0),
        preferred_element_type=F32,
    )


def fine_dot_nt(left, right):
    lh, ll = halves(left)
    rh, rl = halves(right)
    return lax.dot_general(
        jnp.concatenate([lh, ll, lh], axis=1),
        jnp.concatenate([rh, rh, rl], axis=1),
        (((1,), (1,)), ((), ())),
        preferred_element_type=F32,
    )


def softplus(x):
    u = jnp.exp(-jnp.abs(x))
    series = u * (1.0 - u * (0.5 - u * (1.0 / 3.0 - u * 0.25)))
    return jnp.maximum(x, 0.0) + jnp.where(u < 0.015625, series, jnp.log(1.0 + u))


def unit(x):
    x = x.astype(F32)
    return x * lax.rsqrt(jnp.sum(x * x, axis=-1, keepdims=True) + NORM_EPS)


def local_kernel(
    pairs, q_ref, k_ref, v_ref, lat_ref, aux_ref, up_ref, bias_ref, rate_ref,
    ol_ref, rh_ref, rl_ref, map_ref, state,
):
    step = pl.program_id(0)

    ri = lax.broadcasted_iota(jnp.int32, (C, C), 0)
    ci = lax.broadcasted_iota(jnp.int32, (C, C), 1)
    eye = ri == ci
    strict = ri > ci
    lower = ri >= ci
    tri = lower.astype(BF16)
    tri2 = jnp.concatenate([tri, tri], axis=1)
    upper = (ri <= ci).astype(BF16)
    up = up_ref[...]
    bias0 = bias_ref[0:1, :]
    bias1 = bias_ref[1:2, :]
    rate = -jnp.exp(rate_ref[...])

    @pl.when(step == 0)
    def _():
        state[...] = jnp.zeros_like(state)
        for chain in range(2):
            state[chain, :, 0:C] = eye.astype(F32)

    todo = []
    for j in range(pairs):
        rows = aux_ref[2 * j].astype(F32) + aux_ref[2 * j + 1].astype(F32)
        counts = jnp.dot(rows.astype(BF16), upper, preferred_element_type=F32)
        both = jnp.concatenate([jax.nn.sigmoid(rows), counts, rows], axis=0)
        both = jnp.concatenate([both, jnp.zeros((C - 24, C), F32)], axis=0)
        cols = both.T
        for chain in range(2):
            todo.append(
                dict(
                    j=j, chain=chain,
                    beta=cols[:, chain:chain + 1],
                    count_col=cols[:, 10 + chain:11 + chain],
                    kind=cols[:, 20 + chain:21 + chain],
                    count_row=counts[2 + chain:3 + chain, :],
                    count_last=counts[2 + chain:3 + chain, C - 1:C],
                )
            )
    for t in todo:
        at = pl.ds(t["j"] * C, C)
        chain = t["chain"]
        pre = jnp.dot(lat_ref[chain, at, :], up, preferred_element_type=F32)
        pre = pre.astype(BF16).astype(F32)
        bias = jnp.where(t["kind"] > 0.5, bias1, bias0)
        decay = rate * softplus(pre + bias)
        dh, dl = halves(decay)
        total = jnp.dot(tri2, jnp.concatenate([dh, dl], axis=0), preferred_element_type=F32)
        t["total"] = total
        t["growth"] = jnp.exp(total)
    for t in todo:
        at = pl.ds(t["j"] * C, C)
        chain = t["chain"]
        total, growth = t["total"], t["growth"]
        key = unit(k_ref[chain, at, :])
        query = unit(q_ref[chain, at, :]) * (DK ** -0.5)
        t["alive"] = (t["count_col"] < 0.5).astype(F32)
        same = t["count_col"] == t["count_row"]
        last = total[C - 1:C, :]
        key_grow = key * growth
        query_grow = query * growth
        key_shrink = key * jnp.exp(-total)
        tail_mask = (t["count_col"] == t["count_last"]).astype(F32)
        t["tail"] = key * jnp.exp(last - total) * tail_mask
        t["carry"] = jnp.exp(last) * (t["count_last"] < 0.5).astype(F32)
        gram = fine_dot_nt(jnp.concatenate([key_grow, query_grow], axis=0), key_shrink)
        t["mix"] = jnp.where(lower & same, gram[C:], 0.0)
        t["low"] = jnp.where(strict & same, gram[:C], 0.0) * t["beta"]
        t["query_live"] = query_grow * t["alive"]
        t["rhs"] = jnp.concatenate(
            [key_grow * (t["alive"] * t["beta"]), v_ref[chain, at, :].astype(F32) * t["beta"]],
            axis=1,
        )

    near = (ri // 16) == (ci // 16)
    for t in todo:
        t["d"] = jnp.where(near, t["low"], 0.0)
    for t in todo:
        t["d2"] = fine_dot(t["d"], t["d"])
    for t in todo:
        both = fine_dot(jnp.concatenate([t["d"], t["d2"]], axis=0), t["d2"])
        t["x"] = t["d2"] - t["d"] - both[:C]
        t["d4"] = both[C:]
    for t in todo:
        both = fine_dot(jnp.concatenate([t["x"], t["d4"]], axis=0), t["d4"])
        t["x"] = t["x"] + t["d4"] + both[:C]
        t["d8"] = both[C:]
    for t in todo:
        t["x"] = t["x"] + t["d8"] + fine_dot(t["x"], t["d8"])
    width = 16
    while width < C:
        part = ((ri // (2 * width)) == (ci // (2 * width))) & ((ri // width) != (ci // width))
        for t in todo:
            off = jnp.where(part, t["low"], 0.0)
            t["y"] = off + fine_dot(off, t["x"])
        for t in todo:
            t["x"] = t["x"] - (t["y"] + fine_dot(t["x"], t["y"]))
        width *= 2

    for t in todo:
        t["wu"] = t["rhs"] + fine_dot(t["x"], t["rhs"])
    for t in todo:
        wh, wl = halves(t["wu"])
        right = jnp.concatenate([wh, wh, wl], axis=0)
        mh, ml = halves(t["mix"])
        kh, kl = halves(t["tail"].T)
        left = jnp.concatenate(
            [jnp.concatenate([mh, ml, mh], axis=1), jnp.concatenate([kh, kl, kh], axis=1)], axis=0
        )
        both = jnp.dot(left, right, preferred_element_type=F32)
        t["pu"] = both[:C, C:]
        live = t["query_live"] - both[:C, :C]
        move = jnp.where(eye, t["carry"], 0.0) - both[C:, :C]
        t["left"] = jnp.concatenate([live, move], axis=0)
        t["offset"] = both[C:, C:]
    held = [state[0], state[1]]
    for t in todo:
        at = pl.ds(t["j"] * C, C)
        chain = t["chain"]
        both = fine_dot(t["left"], held[chain])
        ol_ref[chain, at, :] = t["pu"] + both[:C, C:]
        high, low = halves(both[:C, :C])
        rh_ref[chain, at, :] = high
        rl_ref[chain, at, :] = low
        held[chain] = jnp.concatenate([both[C:, :C], both[C:, C:] + t["offset"]], axis=1)
    state[0] = held[0]
    state[1] = held[1]
    map_ref[0] = held[0]
    map_ref[1] = held[1]


def local_work(q, k, v, lat, aux, up, bias, rate, pairs=2):
    steps = SPAN // (pairs * C)
    wide = pl.BlockSpec((2, pairs * C, DK), lambda i: (0, i, 0))
    whole = lambda *shape: pl.BlockSpec(shape, lambda i: (0,) * len(shape))
    return pl.pallas_call(
        functools.partial(local_kernel, pairs),
        grid=(steps,),
        out_shape=(
            jax.ShapeDtypeStruct((2, SPAN, DK), F32),
            jax.ShapeDtypeStruct((2, SPAN, DK), BF16),
            jax.ShapeDtypeStruct((2, SPAN, DK), BF16),
            jax.ShapeDtypeStruct((2, DK, 2 * DK), F32),
        ),
        in_specs=[
            wide, wide, wide, wide,
            pl.BlockSpec((2 * pairs, 8, 128), lambda i: (i, 0, 0)),
            whole(DK, DK), whole(2, DK), whole(1, DK),
        ],
        out_specs=(wide, wide, wide, whole(2, DK, 2 * DK)),
        scratch_shapes=[pltpu.VMEM((2, DK, 2 * DK), F32)],
        name="local_work",
    )(q, k, v, lat, aux, up, bias, rate)


def exit_kernel(
    ol_ref, rh_ref, rl_ref, map_ref, back_ref,
    first, second, moved, core_buf, sem_send, sem_recv, back_send, back_recv,
):
    group, seq, core, me, blk = place()
    x = seq // 2
    barrier = greet(seq, core, me)
    for away in (1, 2, 3):
        pl.semaphore_signal(
            barrier, inc=1, device_id={"seq": lax.rem(seq + 2 * away, 8)}, device_id_type=MESH
        )
    pl.semaphore_wait(barrier, OWNERS + 2)

    def send_to(src, dst, slot, to):
        return pltpu.make_async_remote_copy(
            src, dst, sem_send.at[slot], sem_recv.at[slot],
            device_id={"seq": 2 * to + core}, device_id_type=MESH,
        )

    for chain in range(2):
        moved[chain] = map_ref[chain, :, DK:]

    @pl.when(x == 0)
    def _():
        first[...] = jnp.zeros_like(first)
        send_to(moved, first, 0, 1).start()
        send_to(moved, first, 0, 1).wait_send()

    @pl.when(x == 2)
    def _():
        send_to(map_ref, second, 1, 3).start()

    @pl.when(x == 1)
    def _():
        send_to(moved, first, 0, 1).wait_recv()
        for chain in range(2):
            moved[chain] = map_ref[chain, :, DK:] + fine_dot(map_ref[chain, :, 0:DK], first[chain])
        send_to(moved, first, 0, 2).start()
        send_to(moved, first, 2, 3).start()
        send_to(moved, first, 0, 2).wait_send()
        send_to(moved, first, 2, 3).wait_send()

    @pl.when(x == 2)
    def _():
        send_to(map_ref, second, 1, 3).wait_send()
        send_to(moved, first, 0, 2).wait_recv()

    @pl.when(x == 3)
    def _():
        send_to(map_ref, second, 1, 3).wait_recv()
        send_to(moved, first, 2, 3).wait_recv()
        for chain in range(2):
            first[chain] = second[chain, :, DK:] + fine_dot(second[chain, :, 0:DK], first[chain])

    rights = []
    for chain in range(2):
        sh, sl = halves(first[chain])
        rights.append(jnp.concatenate([sh, sh, sl], axis=0))

    mine = pl.ds(pl.multiple_of(me * DK, DK), DK)

    def piece(step, carry):
        j = lax.rem(step + group, SPAN // C)
        at = pl.ds(pl.multiple_of(j * C, C), C)
        for chain in range(2):
            high = rh_ref[chain, at, :]
            left = jnp.concatenate([high, rl_ref[chain, at, :], high], axis=1)
            out = ol_ref[chain, at, :] + jnp.dot(left, rights[chain], preferred_element_type=F32)
            core_buf[chain, at, :] = out.astype(BF16)
        for part in range(2):
            b = 2 * j + part
            rows = pl.ds(pl.multiple_of(b * TOK, TOK), TOK)

            @pl.when(b != blk)
            def _():
                pltpu.make_async_remote_copy(
                    core_buf.at[:, rows, :], back_ref.at[:, :, mine], back_send, back_recv,
                    device_id={"head": lax.rem(b, GROUPS), "seq": seq - core + b // GROUPS},
                    device_id_type=MESH,
                ).start()

            @pl.when(b == blk)
            def _():
                pltpu.make_async_copy(
                    core_buf.at[:, rows, :], back_ref.at[:, :, mine], back_recv
                ).start()
        return carry

    lax.fori_loop(0, SPAN // C, piece, 0)
    pltpu.make_async_copy(back_ref, back_ref, back_recv).wait()
    sent = back_ref.at[:, :, pl.ds(0, (OWNERS - 1) * DK)]
    pltpu.make_async_copy(sent, sent, back_send).wait()


def exit_exchange(ol, rh, rl, maps):
    return pl.pallas_call(
        exit_kernel,
        out_shape=jax.ShapeDtypeStruct((2, TOK, H * DK), BF16),
        in_specs=[VM] * 4,
        out_specs=ANY,
        scratch_shapes=[
            pltpu.VMEM((2, DK, DK), F32),
            pltpu.VMEM((2, DK, 2 * DK), F32),
            pltpu.VMEM((2, DK, DK), F32),
            pltpu.VMEM((2, SPAN, DK), BF16),
            pltpu.SemaphoreType.DMA((3,)),
            pltpu.SemaphoreType.DMA((3,)),
            pltpu.SemaphoreType.DMA,
            pltpu.SemaphoreType.DMA,
        ],
        compiler_params=pltpu.CompilerParams(collective_id=1, has_side_effects=True),
        name="exit_exchange",
    )(ol, rh, rl, maps)


def gate_kernel(core_ref, gate_ref, gain_ref, out_ref):
    for b in range(2):
        for h in range(core_ref.shape[2] // DK):
            cols = slice(h * DK, (h + 1) * DK)
            wide = core_ref[b, :, cols].astype(F32)
            norm = lax.rsqrt(jnp.mean(wide * wide, axis=-1, keepdims=True) + NORM_EPS)
            gate = jax.nn.sigmoid(gate_ref[b, :, cols].astype(F32))
            out_ref[b, :, cols] = (wide * norm * gain_ref[0:1, cols] * gate).astype(BF16)


def norm_gate(core, gate, gain):
    width = 1024
    spec = pl.BlockSpec((2, TOK, width), lambda i: (0, 0, i))
    return pl.pallas_call(
        gate_kernel,
        grid=(H * DK // width,),
        out_shape=jax.ShapeDtypeStruct(core.shape, BF16),
        in_specs=[spec, spec, pl.BlockSpec((1, width), lambda i: (0, i))],
        out_specs=spec,
        name="norm_gate",
    )(core, gate, gain.reshape(1, -1))


def pack_small(beta_raw, boundary, modality):
    core_group = lax.axis_index("head")
    beta = beta_raw.astype(F32).transpose(2, 0, 1)
    mark = jnp.broadcast_to(boundary.astype(F32)[None], (OWNERS, 2, TOK))
    kind = jnp.broadcast_to(modality.astype(F32)[None], (OWNERS, 2, TOK))
    rows = jnp.concatenate([beta, mark, kind, jnp.zeros((OWNERS, 2, TOK), F32)], axis=1)
    odd = (lax.rem(core_group, 2) == 1).astype(F32)
    return jnp.concatenate([rows * (1.0 - odd), rows * odd], axis=2).astype(BF16)


def per_device(
    query_rows, key_rows, value_rows, beta_raw, gate_latent, gate_up, dt_bias, decay_log,
    boundary, modality, out_gate, norm_gain,
):
    me = lax.axis_index("head") * 2 + lax.rem(lax.axis_index("seq"), 2)
    aux = pack_small(beta_raw, boundary, modality)
    q, k, v, lat, aux = entry_exchange(query_rows, key_rows, value_rows, gate_latent, aux)
    up = lax.dynamic_slice_in_dim(gate_up, me * DK, DK, 1)
    bias = lax.dynamic_slice_in_dim(dt_bias, me * DK, DK, 1)
    rate = jnp.broadcast_to(lax.dynamic_slice_in_dim(decay_log, me, 1, 0)[None], (1, DK))
    ol, rh, rl, maps = local_work(q, k, v, lat, aux, up, bias, rate)
    back = exit_exchange(ol, rh, rl, maps)
    return norm_gate(back, out_gate, norm_gain)


def solution(mesh):
    rows = P(None, ("seq", "head"), None)
    flat = P(None, ("seq", "head"))
    return jax.shard_map(
        per_device,
        mesh=mesh,
        in_specs=(rows, rows, rows, rows, rows, P(), P(), P(), flat, flat, rows, P()),
        out_specs=rows,
        check_vma=False,
    )
```

```python
import jax
import jax.numpy as jnp
from jax import lax
from jax.experimental import pallas as pl
from jax.experimental.pallas import tpu as pltpu
from jax.sharding import PartitionSpec as P

H = 32
DK = 128
TOK = 64
C = 128
SPAN = 2048
BLOCKS = SPAN // C
GROUPS = 16
OWNERS = 32
NORM_EPS = 1e-6
MESH = pl.DeviceIdType.MESH
F32 = jnp.float32
BF16 = jnp.bfloat16
ANY = pl.BlockSpec(memory_space=pl.ANY)
VM = pl.BlockSpec(memory_space=pltpu.VMEM)
SM = pl.BlockSpec(memory_space=pltpu.SMEM)
LAT, AUX, PASS = 6, 7, 8


def halves(x):
    high = x.astype(BF16)
    return high, (x - high.astype(F32)).astype(BF16)


def left_of(pair):
    return jnp.concatenate([pair[0], pair[1], pair[0]], axis=1)


def right_of(pair):
    return jnp.concatenate([pair[0], pair[0], pair[1]], axis=0)


def dot(left, right):
    return jnp.dot(left, right, preferred_element_type=F32)


def fine(left, right):
    return dot(left_of(left), right_of(right))


def stack(*parts):
    return jnp.concatenate(parts, axis=0)


def softplus(x):
    u = jnp.exp(-jnp.abs(x))
    series = u * (1.0 - u * (0.5 - u * (1.0 / 3.0 - u * 0.25)))
    return jnp.maximum(x, 0.0) + jnp.where(u < 0.015625, series, jnp.log(1.0 + u))


def unit(x):
    x = x.astype(F32)
    return x * lax.rsqrt(jnp.sum(x * x, axis=-1, keepdims=True) + NORM_EPS)


def aligned(start, size):
    return pl.ds(pl.multiple_of(start, size), size)


def kernel(
    q_in, k_in, v_in, beta_in, mark_in, kind_in, lat_in, up_in, bias_in, rate_in, gate_in, gain_in,
    out_ref,
    kb, vb, qb, lb, auxb, aux_src, upb, biasb, gateb, scale,
    total, grow, shrink, keyg, tail, xb, wb, ub, mcb, ocb, right, cols, rows,
    maps, first, second, moved, core_buf, back,
    send, recv, pre_send, pre_recv, back_send, back_recv, here,
):
    group = lax.axis_index("head")
    seq = lax.axis_index("seq")
    core = lax.rem(seq, 2)
    x = seq // 2
    me = group * 2 + core
    blk = core * GROUPS + group

    def owner_id(owner):
        return {"head": owner // 2, "seq": seq - core + lax.rem(owner, 2)}

    barrier = pltpu.get_barrier_semaphore()

    def greet(step, carry):
        pl.semaphore_signal(
            barrier, inc=1, device_id=owner_id(lax.rem(me + step, OWNERS)), device_id_type=MESH
        )
        return carry

    lax.fori_loop(1, OWNERS, greet, 0)
    for away in (1, 2, 3):
        pl.semaphore_signal(
            barrier, inc=1, device_id={"seq": lax.rem(seq + 2 * away, 8)}, device_id_type=MESH
        )

    my_cols = aligned(me * DK, DK)
    my_rows = aligned(blk * TOK, TOK)
    local = (
        pltpu.make_async_copy(up_in.at[:, my_cols], upb, here.at[0]),
        pltpu.make_async_copy(bias_in.at[:, my_cols], biasb, here.at[1]),
        pltpu.make_async_copy(gate_in, gateb, here.at[2]),
    )
    for copy in local:
        copy.start()

    ri = lax.broadcasted_iota(jnp.int32, (C, C), 0)
    ci = lax.broadcasted_iota(jnp.int32, (C, C), 1)
    si = lax.broadcasted_iota(jnp.int32, (8 * OWNERS, H), 0)
    sj = lax.broadcasted_iota(jnp.int32, (8 * OWNERS, H), 1)
    select = ((si % 8 == 0) & (si // 8 == sj)).astype(BF16)
    part = lax.broadcasted_iota(jnp.int32, (8 * OWNERS, TOK), 0) % 8
    ti = lax.broadcasted_iota(jnp.int32, (TOK, C), 0)
    tj = lax.broadcasted_iota(jnp.int32, (TOK, C), 1)
    packed = jnp.zeros((8 * OWNERS, C), F32)
    for b in range(2):
        small = dot(select, beta_in[b])
        small = jnp.where(part == 1, mark_in[b:b + 1, :].astype(F32), small)
        small = jnp.where(part == 2, kind_in[b:b + 1, :].astype(F32), small)
        packed = packed + dot(small.astype(BF16), (tj == ti + b * TOK).astype(BF16))
    aux_src[...] = packed.reshape(OWNERS, 8, C).astype(BF16)

    pl.semaphore_wait(barrier, OWNERS + 2)

    def lat_send(step, carry):
        pltpu.make_async_remote_copy(
            lat_in, lb.at[:, my_rows, :], send.at[LAT], recv.at[LAT],
            device_id={"head": lax.rem(group + step, GROUPS), "seq": seq}, device_id_type=MESH,
        ).start()
        return carry

    lax.fori_loop(1, GROUPS, lat_send, 0)
    pltpu.make_async_copy(lat_in, lb.at[:, my_rows, :], recv.at[LAT]).start()

    def aux_send(step, carry):
        other = lax.rem(me + step, OWNERS)
        pltpu.make_async_remote_copy(
            aux_src.at[other], auxb.at[blk], send.at[AUX], recv.at[AUX],
            device_id=owner_id(other), device_id_type=MESH,
        ).start()
        return carry

    lax.fori_loop(1, OWNERS, aux_send, 0)
    pltpu.make_async_copy(aux_src.at[me], auxb.at[blk], recv.at[AUX]).start()

    def spread(slot, src, dst, chain):
        def one(step, carry):
            other = lax.rem(me + step, OWNERS)
            pltpu.make_async_remote_copy(
                src.at[chain, :, aligned(other * DK, DK)], dst.at[chain, my_rows, :],
                send.at[slot], recv.at[slot], device_id=owner_id(other), device_id_type=MESH,
            ).start()
            return carry

        lax.fori_loop(1, OWNERS, one, 0)
        pltpu.make_async_copy(
            src.at[chain, :, my_cols], dst.at[chain, my_rows, :], recv.at[slot]
        ).start()

    def arrived(slot, dst):
        pltpu.make_async_copy(dst, dst, recv.at[slot]).wait()

    spread(0, k_in, kb, 0)

    local[2].wait()

    def gates(step, carry):
        for inner in range(4):
            at = aligned((step * 4 + inner) * DK, DK)
            for chain in range(2):
                scale[chain, :, at] = gain_in[0:1, at] * jax.nn.sigmoid(
                    gateb[chain, :, at].astype(F32)
                )
        return carry

    lax.fori_loop(0, H // 4, gates, 0)

    half = lb.at[:, aligned(core * (SPAN // 2), SPAN // 2), :]
    arrived(LAT, half)
    pass_on = pltpu.make_async_remote_copy(
        half, half, send.at[PASS], recv.at[PASS],
        device_id={"seq": seq + 1 - 2 * core}, device_id_type=MESH,
    )
    pass_on.start()
    spread(1, k_in, kb, 1)
    spread(2, v_in, vb, 0)
    spread(3, v_in, vb, 1)
    spread(4, q_in, qb, 0)
    spread(5, q_in, qb, 1)

    eye = ri == ci
    strict = ri > ci
    lower = ri >= ci
    tri = lower.astype(BF16)
    tri2 = jnp.concatenate([tri, tri], axis=1)
    upper = (ri <= ci).astype(BF16)
    lane = lax.broadcasted_iota(jnp.int32, (8, C), 1)
    local[0].wait()
    local[1].wait()
    arrived(AUX, auxb)
    pass_on.wait()

    rate = -jnp.exp(jnp.full((1, DK), rate_in[me], F32))

    def decays(step, carry):
        for inner in range(2):
            j = step * 2 + inner
            at = aligned(j * C, C)
            one = auxb[2 * j].astype(F32)
            two = auxb[2 * j + 1].astype(F32)
            mine = stack(
                jnp.where(lane < TOK, one, pltpu.roll(two, TOK, 1)),
                jnp.where(lane < TOK, pltpu.roll(one, TOK, 1), two),
            )
            counts = dot(mine.astype(BF16), upper)
            tall = stack(jax.nn.sigmoid(mine), counts, mine, jnp.zeros((C - 48, C), F32)).T
            cols[j] = tall
            rows[j] = counts
            for chain in range(2):
                kind = tall[:, 34 + 8 * chain:35 + 8 * chain]
                pre = dot(lb[chain, at, :], upb[...]).astype(BF16).astype(F32)
                bias = jnp.where(kind > 0.5, biasb[1:2, :], biasb[0:1, :])
                decay = rate * softplus(pre + bias)
                dh, dl = halves(decay)
                total[chain, at, :] = dot(tri2, stack(dh, dl))
        return carry

    lax.fori_loop(0, BLOCKS // 2, decays, 0)

    near = (ri // 16) == (ci // 16)

    def key_stage(chain):
        def body(step, carry):
            todo = []
            for inner in range(4):
                j = step * 4 + inner
                at = aligned(j * C, C)
                beta = cols[j, :, 8 * chain:8 * chain + 1]
                count_col = cols[j, :, 17 + 8 * chain:18 + 8 * chain]
                count_row = rows[j, 8 * chain + 1:8 * chain + 2, :]
                count_last = count_row[:, C - 1:C]
                sums = total[chain, at, :]
                last = sums[C - 1:C, :]
                growth = jnp.exp(sums)
                grow[chain, at, :] = growth
                key = unit(kb[chain, at, :])
                key_grow = key * growth
                alive = (count_col < 0.5).astype(F32)
                keyg[chain, at, :] = key_grow * (alive * beta)
                shrunk = halves(key * jnp.exp(-sums))
                shrink[chain, at, :] = jnp.concatenate(shrunk, axis=1)
                mask = (count_col == count_last).astype(F32)
                moved_t = halves((key * jnp.exp(last - sums) * mask).T)
                tail[chain, at, :] = jnp.concatenate(moved_t, axis=1)
                gram = lax.dot_general(
                    left_of(halves(key_grow)),
                    jnp.concatenate([shrunk[0], shrunk[0], shrunk[1]], axis=1),
                    (((1,), (1,)), ((), ())), preferred_element_type=F32,
                )
                low = jnp.where(strict & (count_col == count_row), gram, 0.0) * beta
                d = jnp.where(near, low, 0.0)
                todo.append(dict(at=at, low=low, d=d, ds=halves(d)))
            for t in todo:
                t["d2"] = fine(t["ds"], t["ds"])
                t["d2s"] = halves(t["d2"])
            for t in todo:
                both = dot(stack(left_of(t["ds"]), left_of(t["d2s"])), right_of(t["d2s"]))
                t["x"] = t["d2"] - t["d"] - both[:C]
                t["d4"] = both[C:]
                t["xs"], t["d4s"] = halves(t["x"]), halves(t["d4"])
            for t in todo:
                both = dot(stack(left_of(t["xs"]), left_of(t["d4s"])), right_of(t["d4s"]))
                t["x"] = t["x"] + t["d4"] + both[:C]
                t["d8"] = both[C:]
                t["xs"], t["d8s"] = halves(t["x"]), halves(t["d8"])
            for t in todo:
                t["x"] = t["x"] + t["d8"] + fine(t["xs"], t["d8s"])
                t["xs"] = halves(t["x"])
            width = 16
            while width < C:
                part = ((ri // (2 * width)) == (ci // (2 * width))) & (
                    (ri // width) != (ci // width)
                )
                for t in todo:
                    off = jnp.where(part, t["low"], 0.0)
                    t["ys"] = off + fine(halves(off), t["xs"])
                for t in todo:
                    t["x"] = t["x"] - (t["ys"] + fine(t["xs"], halves(t["ys"])))
                    t["xs"] = halves(t["x"])
                width *= 2
            for t in todo:
                xb[chain, t["at"], :] = jnp.concatenate(t["xs"], axis=1)
            return carry

        lax.fori_loop(0, BLOCKS // 4, body, 0)

    def value_stage(chain):
        maps[chain, :, 0:DK] = eye.astype(F32)
        maps[chain, :, DK:] = jnp.zeros((DK, DK), F32)

        def body(step, carry):
            todo = []
            for inner in range(4):
                j = step * 4 + inner
                at = aligned(j * C, C)
                beta = cols[j, :, 8 * chain:8 * chain + 1]
                count_last = rows[j, 8 * chain + 1:8 * chain + 2, C - 1:C]
                rhs = jnp.concatenate(
                    [keyg[chain, at, :], vb[chain, at, :].astype(F32) * beta], axis=1
                )
                xs = xb[chain, at, :]
                wu = rhs + dot(jnp.concatenate([xs, xs[:, :C]], axis=1), right_of(halves(rhs)))
                pair = halves(wu)
                wb[chain, at, :] = jnp.concatenate([pair[0][:, :C], pair[1][:, :C]], axis=1)
                ub[chain, at, :] = wu[:, C:]
                ts = tail[chain, at, :]
                both = dot(jnp.concatenate([ts, ts[:, :C]], axis=1), right_of(pair))
                carry_row = jnp.exp(total[chain, at, :][C - 1:C, :]) * (count_last < 0.5).astype(F32)
                move = jnp.where(eye, carry_row, 0.0) - both[:, :C]
                todo.append(dict(at=at, move=halves(move), offset=both[:, C:]))
            held = maps[chain]
            for t in todo:
                pair = halves(held)
                mcb[chain, t["at"], :] = jnp.concatenate(
                    [pair[0][:, :C], pair[1][:, :C]], axis=1
                )
                ocb[chain, t["at"], :] = held[:, C:]
                both = fine(t["move"], pair)
                held = jnp.concatenate([both[:, :C], both[:, C:] + t["offset"]], axis=1)
            maps[chain] = held
            return carry

        lax.fori_loop(0, BLOCKS // 4, body, 0)

    arrived(0, kb.at[0])
    key_stage(0)
    arrived(1, kb.at[1])
    key_stage(1)
    arrived(2, vb.at[0])
    value_stage(0)
    arrived(3, vb.at[1])
    value_stage(1)

    def send_to(src, dst, slot, to):
        return pltpu.make_async_remote_copy(
            src, dst, pre_send.at[slot], pre_recv.at[slot],
            device_id={"seq": 2 * to + core}, device_id_type=MESH,
        )

    moved[...] = maps[:, :, DK:]

    @pl.when(x == 0)
    def _():
        first[...] = jnp.zeros_like(first)
        send_to(moved, first, 0, 1).start()
        send_to(moved, first, 0, 1).wait_send()

    @pl.when(x == 2)
    def _():
        send_to(maps, second, 1, 3).start()

    @pl.when(x == 1)
    def _():
        send_to(moved, first, 0, 1).wait_recv()
        for chain in range(2):
            moved[chain] = maps[chain, :, DK:] + fine(
                halves(maps[chain, :, 0:DK]), halves(first[chain])
            )
        send_to(moved, first, 2, 3).start()
        send_to(moved, first, 0, 2).start()
        send_to(moved, first, 0, 2).wait_send()
        send_to(moved, first, 2, 3).wait_send()

    @pl.when(x == 2)
    def _():
        send_to(maps, second, 1, 3).wait_send()
        send_to(moved, first, 0, 2).wait_recv()

    @pl.when(x == 3)
    def _():
        send_to(maps, second, 1, 3).wait_recv()
        send_to(moved, first, 2, 3).wait_recv()
        for chain in range(2):
            first[chain] = second[chain, :, DK:] + fine(
                halves(second[chain, :, 0:DK]), halves(first[chain])
            )

    def state_stage(chain):
        incoming = right_of(halves(first[chain]))

        def body(step, carry):
            todo = []
            for inner in range(4):
                j = step * 4 + inner
                at = aligned(j * C, C)
                mc = mcb[chain, at, :]
                state = ocb[chain, at, :] + dot(
                    jnp.concatenate([mc, mc[:, :C]], axis=1), incoming
                )
                todo.append((j, at, halves(state)))
            for j, at, pair in todo:
                ws = wb[chain, at, :]
                fresh = ub[chain, at, :] - dot(
                    jnp.concatenate([ws, ws[:, :C]], axis=1), right_of(pair)
                )
                fh, fl = halves(fresh)
                right[chain, j] = stack(pair[0], fh, pair[1], fl)
            return carry

        lax.fori_loop(0, BLOCKS // 4, body, 0)

    state_stage(0)
    state_stage(1)

    def query_stage(chain):
        def body(step, carry):
            p = lax.rem(step + group // 2, BLOCKS // 2)
            for inner in range(2):
                j = 2 * p + inner
                at = aligned(j * C, C)
                count_col = cols[j, :, 17 + 8 * chain:18 + 8 * chain]
                count_row = rows[j, 8 * chain + 1:8 * chain + 2, :]
                query = unit(qb[chain, at, :]) * (DK ** -0.5) * grow[chain, at, :]
                sh = shrink[chain, at, :]
                gram = lax.dot_general(
                    left_of(halves(query)), jnp.concatenate([sh[:, :C], sh], axis=1),
                    (((1,), (1,)), ((), ())), preferred_element_type=F32,
                )
                mix = jnp.where(lower & (count_col == count_row), gram, 0.0)
                live = query * (count_col < 0.5).astype(F32)
                pair = halves(jnp.concatenate([live, mix], axis=1))
                hold = right[chain, j]
                out = dot(left_of(pair), stack(hold[:2 * C], hold))
                core_buf[chain, at, :] = out.astype(BF16)
            for inner in range(4):
                b = 4 * p + inner
                rows_b = aligned(b * TOK, TOK)
                src = core_buf.at[chain, rows_b, :]
                dst = back.at[chain, :, my_cols]

                @pl.when(b != blk)
                def _():
                    pltpu.make_async_remote_copy(
                        src, dst, back_send.at[chain], back_recv.at[chain],
                        device_id={"head": lax.rem(b, GROUPS), "seq": seq - core + b // GROUPS},
                        device_id_type=MESH,
                    ).start()

                @pl.when(b == blk)
                def _():
                    pltpu.make_async_copy(src, dst, back_recv.at[chain]).start()

            return carry

        lax.fori_loop(0, BLOCKS // 2, body, 0)

    arrived(4, qb.at[0])
    query_stage(0)
    arrived(5, qb.at[1])
    query_stage(1)

    for chain in range(2):
        pltpu.make_async_copy(back.at[chain], back.at[chain], back_recv.at[chain]).wait()

        def finish(step, carry, chain=chain):
            for inner in range(4):
                at = aligned((step * 4 + inner) * DK, DK)
                wide = back[chain, :, at].astype(F32)
                norm = lax.rsqrt(jnp.mean(wide * wide, axis=-1, keepdims=True) + NORM_EPS)
                out_ref[chain, :, at] = (wide * norm * scale[chain, :, at]).astype(BF16)
            return carry

        lax.fori_loop(0, H // 4, finish, 0)

    many = (OWNERS - 1) * DK
    for slot in range(6):
        sent = k_in.at[0, :, pl.ds(0, many)]
        pltpu.make_async_copy(sent, sent, send.at[slot]).wait()
    for chain in range(2):
        sent = back.at[0, :, pl.ds(0, many)]
        pltpu.make_async_copy(sent, sent, back_send.at[chain]).wait()
    lat_sent = lb.at[:, pl.ds(0, (GROUPS - 1) * TOK), :]
    pltpu.make_async_copy(lat_sent, lat_sent, send.at[LAT]).wait()
    aux_sent = aux_src.at[pl.ds(0, OWNERS - 1)]
    pltpu.make_async_copy(aux_sent, aux_sent, send.at[AUX]).wait()


def per_device(
    query_rows, key_rows, value_rows, beta_raw, gate_latent, gate_up, dt_bias, decay_log,
    boundary, modality, out_gate, norm_gain,
):
    span = lambda width, dtype: pltpu.VMEM((2, SPAN, width), dtype)
    return pl.pallas_call(
        kernel,
        out_shape=jax.ShapeDtypeStruct((2, TOK, H * DK), BF16),
        in_specs=[ANY, ANY, ANY, VM, VM, VM, ANY, ANY, ANY, SM, ANY, VM],
        out_specs=VM,
        scratch_shapes=[
            span(DK, BF16), span(DK, BF16), span(DK, BF16), span(DK, BF16),
            pltpu.VMEM((OWNERS, 8, C), BF16),
            pltpu.VMEM((OWNERS, 8, C), BF16),
            pltpu.VMEM((DK, DK), BF16),
            pltpu.VMEM((2, DK), F32),
            pltpu.VMEM((2, TOK, H * DK), BF16),
            pltpu.VMEM((2, TOK, H * DK), F32),
            span(DK, F32),
            span(DK, F32),
            span(2 * DK, BF16),
            span(DK, F32),
            span(2 * DK, BF16),
            span(2 * DK, BF16),
            span(2 * DK, BF16),
            span(DK, F32),
            span(2 * DK, BF16),
            span(DK, F32),
            pltpu.VMEM((2, BLOCKS, 4 * C, DK), BF16),
            pltpu.VMEM((BLOCKS, C, C), F32),
            pltpu.VMEM((BLOCKS, 16, C), F32),
            pltpu.VMEM((2, DK, 2 * DK), F32),
            pltpu.VMEM((2, DK, DK), F32),
            pltpu.VMEM((2, DK, 2 * DK), F32),
            pltpu.VMEM((2, DK, DK), F32),
            span(DK, BF16),
            pltpu.VMEM((2, TOK, H * DK), BF16),
            pltpu.SemaphoreType.DMA((9,)),
            pltpu.SemaphoreType.DMA((9,)),
            pltpu.SemaphoreType.DMA((3,)),
            pltpu.SemaphoreType.DMA((3,)),
            pltpu.SemaphoreType.DMA((2,)),
            pltpu.SemaphoreType.DMA((2,)),
            pltpu.SemaphoreType.DMA((3,)),
        ],
        compiler_params=pltpu.CompilerParams(
            collective_id=0, has_side_effects=True, vmem_limit_bytes=60 * 1024 * 1024
        ),
        name="delta_attention",
    )(
        query_rows, key_rows, value_rows, beta_raw.transpose(0, 2, 1), boundary, modality, gate_latent, gate_up, dt_bias, decay_log,
        out_gate, norm_gain.reshape(1, -1),
    )


def solution(mesh):
    rows = P(None, ("seq", "head"), None)
    flat = P(None, ("seq", "head"))
    return jax.shard_map(
        per_device,
        mesh=mesh,
        in_specs=(rows, rows, rows, rows, rows, P(), P(), P(), flat, flat, rows, P()),
        out_specs=rows,
        check_vma=False,
    )
```

```python
import jax
import jax.numpy as jnp
from jax import lax
from jax.experimental import pallas as pl
from jax.experimental.pallas import tpu as pltpu
from jax.sharding import PartitionSpec as P

H = 32
DK = 128
TOK = 64
C = 128
SPAN = 2048
BLOCKS = SPAN // C
GROUPS = 16
OWNERS = 32
NORM_EPS = 1e-6
MESH = pl.DeviceIdType.MESH
F32 = jnp.float32
BF16 = jnp.bfloat16
ANY = pl.BlockSpec(memory_space=pl.ANY)
VM = pl.BlockSpec(memory_space=pltpu.VMEM)
SM = pl.BlockSpec(memory_space=pltpu.SMEM)
LAT, AUX, PASS = 6, 7, 8
KEY_STEP = 8


def halves(x):
    high = x.astype(BF16)
    return high, (x - high.astype(F32)).astype(BF16)


def left_of(pair):
    return jnp.concatenate([pair[0], pair[1], pair[0]], axis=1)


def right_of(pair):
    return jnp.concatenate([pair[0], pair[0], pair[1]], axis=0)


def dot(left, right):
    return jnp.dot(left, right, preferred_element_type=F32)


def fine(left, right):
    return dot(left_of(left), right_of(right))


def stack(*parts):
    return jnp.concatenate(parts, axis=0)


def softplus(x):
    u = jnp.exp(-jnp.abs(x))
    series = u * (1.0 - u * (0.5 - u * (1.0 / 3.0 - u * 0.25)))
    return jnp.maximum(x, 0.0) + jnp.where(u < 0.015625, series, jnp.log(1.0 + u))


def unit(x):
    x = x.astype(F32)
    return x * lax.rsqrt(jnp.sum(x * x, axis=-1, keepdims=True) + NORM_EPS)


def aligned(start, size):
    return pl.ds(pl.multiple_of(start, size), size)


def kernel(
    q_in, k_in, v_in, beta_in, mark_in, kind_in, lat_in, up_in, bias_in, rate_in, gate_in, gain_in,
    out_ref,
    kb, vb, qb, lb, auxb, aux_src, upb, biasb, gateb, scale,
    total, grow, shrink, keyg, tail, xb, wb, ub, mcb, ocb, right, cols, rows,
    maps, first, gathered, leftb, core_buf, back,
    send, recv, pre_send, pre_recv, back_send, back_recv, here,
):
    group = lax.axis_index("head")
    seq = lax.axis_index("seq")
    core = lax.rem(seq, 2)
    x = seq // 2
    me = group * 2 + core
    blk = core * GROUPS + group

    def owner_id(owner):
        return {"head": owner // 2, "seq": seq - core + lax.rem(owner, 2)}

    barrier = pltpu.get_barrier_semaphore()

    def greet(step, carry):
        pl.semaphore_signal(
            barrier, inc=1, device_id=owner_id(lax.rem(me + step, OWNERS)), device_id_type=MESH
        )
        return carry

    lax.fori_loop(1, OWNERS, greet, 0)
    for away in (1, 2, 3):
        pl.semaphore_signal(
            barrier, inc=1, device_id={"seq": lax.rem(seq + 2 * away, 8)}, device_id_type=MESH
        )

    my_cols = aligned(me * DK, DK)
    my_rows = aligned(blk * TOK, TOK)
    local = (
        pltpu.make_async_copy(up_in.at[:, my_cols], upb, here.at[0]),
        pltpu.make_async_copy(bias_in.at[:, my_cols], biasb, here.at[1]),
        pltpu.make_async_copy(gate_in, gateb, here.at[2]),
    )
    for copy in local:
        copy.start()

    ri = lax.broadcasted_iota(jnp.int32, (C, C), 0)
    ci = lax.broadcasted_iota(jnp.int32, (C, C), 1)
    si = lax.broadcasted_iota(jnp.int32, (8 * OWNERS, H), 0)
    sj = lax.broadcasted_iota(jnp.int32, (8 * OWNERS, H), 1)
    select = ((si % 8 == 0) & (si // 8 == sj)).astype(BF16)
    part = lax.broadcasted_iota(jnp.int32, (8 * OWNERS, TOK), 0) % 8
    ti = lax.broadcasted_iota(jnp.int32, (TOK, C), 0)
    tj = lax.broadcasted_iota(jnp.int32, (TOK, C), 1)
    packed = jnp.zeros((8 * OWNERS, C), F32)
    for b in range(2):
        small = dot(select, beta_in[b])
        small = jnp.where(part == 1, mark_in[b:b + 1, :].astype(F32), small)
        small = jnp.where(part == 2, kind_in[b:b + 1, :].astype(F32), small)
        packed = packed + dot(small.astype(BF16), (tj == ti + b * TOK).astype(BF16))
    aux_src[...] = packed.reshape(OWNERS, 8, C).astype(BF16)

    pl.semaphore_wait(barrier, OWNERS + 2)

    def lat_send(step, carry):
        pltpu.make_async_remote_copy(
            lat_in, lb.at[:, my_rows, :], send.at[LAT], recv.at[LAT],
            device_id={"head": lax.rem(group + step, GROUPS), "seq": seq}, device_id_type=MESH,
        ).start()
        return carry

    lax.fori_loop(1, GROUPS, lat_send, 0)
    pltpu.make_async_copy(lat_in, lb.at[:, my_rows, :], recv.at[LAT]).start()

    def aux_send(step, carry):
        other = lax.rem(me + step, OWNERS)
        pltpu.make_async_remote_copy(
            aux_src.at[other], auxb.at[blk], send.at[AUX], recv.at[AUX],
            device_id=owner_id(other), device_id_type=MESH,
        ).start()
        return carry

    lax.fori_loop(1, OWNERS, aux_send, 0)
    pltpu.make_async_copy(aux_src.at[me], auxb.at[blk], recv.at[AUX]).start()

    def spread(slot, src, dst, chain):
        def one(step, carry):
            other = lax.rem(me + step, OWNERS)
            pltpu.make_async_remote_copy(
                src.at[chain, :, aligned(other * DK, DK)], dst.at[chain, my_rows, :],
                send.at[slot], recv.at[slot], device_id=owner_id(other), device_id_type=MESH,
            ).start()
            return carry

        lax.fori_loop(1, OWNERS, one, 0)
        pltpu.make_async_copy(
            src.at[chain, :, my_cols], dst.at[chain, my_rows, :], recv.at[slot]
        ).start()

    def arrived(slot, dst):
        pltpu.make_async_copy(dst, dst, recv.at[slot]).wait()

    spread(0, k_in, kb, 0)

    local[2].wait()

    def gates(step, carry):
        for inner in range(4):
            at = aligned((step * 4 + inner) * DK, DK)
            for chain in range(2):
                scale[chain, :, at] = gain_in[0:1, at] * jax.nn.sigmoid(
                    gateb[chain, :, at].astype(F32)
                )
        return carry

    lax.fori_loop(0, H // 4, gates, 0)

    half = lb.at[:, aligned(core * (SPAN // 2), SPAN // 2), :]
    arrived(LAT, half)
    pass_on = pltpu.make_async_remote_copy(
        half, half, send.at[PASS], recv.at[PASS],
        device_id={"seq": seq + 1 - 2 * core}, device_id_type=MESH,
    )
    pass_on.start()
    spread(1, k_in, kb, 1)
    spread(2, v_in, vb, 0)
    spread(3, v_in, vb, 1)
    spread(4, q_in, qb, 0)
    spread(5, q_in, qb, 1)

    eye = ri == ci
    strict = ri > ci
    lower = ri >= ci
    tri = lower.astype(BF16)
    tri2 = jnp.concatenate([tri, tri], axis=1)
    upper = (ri <= ci).astype(BF16)
    lane = lax.broadcasted_iota(jnp.int32, (8, C), 1)
    local[0].wait()
    local[1].wait()
    arrived(AUX, auxb)
    pass_on.wait()

    rate = -jnp.exp(jnp.full((1, DK), rate_in[me], F32))

    def decays(step, carry):
        for inner in range(4):
            j = step * 4 + inner
            at = aligned(j * C, C)
            one = auxb[2 * j].astype(F32)
            two = auxb[2 * j + 1].astype(F32)
            mine = stack(
                jnp.where(lane < TOK, one, pltpu.roll(two, TOK, 1)),
                jnp.where(lane < TOK, pltpu.roll(one, TOK, 1), two),
            )
            counts = dot(mine.astype(BF16), upper)
            tall = stack(jax.nn.sigmoid(mine), counts, mine, jnp.zeros((C - 48, C), F32)).T
            cols[j] = tall
            rows[j] = counts
            for chain in range(2):
                kind = tall[:, 34 + 8 * chain:35 + 8 * chain]
                pre = dot(lb[chain, at, :], upb[...]).astype(BF16).astype(F32)
                bias = jnp.where(kind > 0.5, biasb[1:2, :], biasb[0:1, :])
                decay = rate * softplus(pre + bias)
                dh, dl = halves(decay)
                total[chain, at, :] = dot(tri2, stack(dh, dl))
        return carry

    lax.fori_loop(0, BLOCKS // 4, decays, 0)

    near = (ri // 16) == (ci // 16)

    def key_stage(chain):
        def body(step, carry):
            todo = []
            for inner in range(KEY_STEP):
                j = step * KEY_STEP + inner
                at = aligned(j * C, C)
                beta = cols[j, :, 8 * chain:8 * chain + 1]
                count_col = cols[j, :, 17 + 8 * chain:18 + 8 * chain]
                count_row = rows[j, 8 * chain + 1:8 * chain + 2, :]
                count_last = count_row[:, C - 1:C]
                sums = total[chain, at, :]
                last = sums[C - 1:C, :]
                growth = jnp.exp(sums)
                grow[chain, at, :] = growth
                key = unit(kb[chain, at, :])
                key_grow = key * growth
                alive = (count_col < 0.5).astype(F32)
                keyg[chain, at, :] = key_grow * (alive * beta)
                shrunk = halves(key * jnp.exp(-sums))
                shrink[chain, at, :] = jnp.concatenate(shrunk, axis=1)
                mask = (count_col == count_last).astype(F32)
                moved_t = halves((key * jnp.exp(last - sums) * mask).T)
                tail[chain, at, :] = jnp.concatenate(moved_t, axis=1)
                gram = lax.dot_general(
                    key_grow.astype(BF16), shrunk[0],
                    (((1,), (1,)), ((), ())), preferred_element_type=F32,
                )
                low = jnp.where(strict & (count_col == count_row), gram, 0.0) * beta
                d = jnp.where(near, low, 0.0)
                todo.append(dict(at=at, low=low, d=d, db=d.astype(BF16)))
            for t in todo:
                t["d2"] = dot(t["db"], t["db"])
                t["d2b"] = t["d2"].astype(BF16)
            for t in todo:
                both = dot(stack(t["db"], t["d2b"]), t["d2b"])
                t["x"] = t["d2"] - t["d"] - both[:C]
                t["d4"] = both[C:]
            for t in todo:
                d4b = t["d4"].astype(BF16)
                both = dot(stack(t["x"].astype(BF16), d4b), d4b)
                t["x"] = t["x"] + t["d4"] + both[:C]
                t["d8"] = both[C:]
            for t in todo:
                t["x"] = t["x"] + t["d8"] + dot(t["x"].astype(BF16), t["d8"].astype(BF16))
            width = 16
            while width < C:
                part = ((ri // (2 * width)) == (ci // (2 * width))) & (
                    (ri // width) != (ci // width)
                )
                for t in todo:
                    t["off"] = jnp.where(part, t["low"], 0.0)
                    t["xs"] = t["x"].astype(BF16)
                    t["y"] = t["off"] + dot(t["off"].astype(BF16), t["xs"])
                for t in todo:
                    t["x"] = t["x"] - (t["y"] + dot(t["xs"], t["y"].astype(BF16)))
                width *= 2
            for t in todo:
                xb[chain, t["at"], :] = t["x"].astype(BF16)
            return carry

        lax.fori_loop(0, BLOCKS // KEY_STEP, body, 0)

    def value_stage(chain):
        maps[chain, :, 0:DK] = eye.astype(F32)
        maps[chain, :, DK:] = jnp.zeros((DK, DK), F32)

        def body(step, carry):
            todo = []
            for inner in range(4):
                j = step * 4 + inner
                at = aligned(j * C, C)
                beta = cols[j, :, 8 * chain:8 * chain + 1]
                count_last = rows[j, 8 * chain + 1:8 * chain + 2, C - 1:C]
                rhs = jnp.concatenate(
                    [keyg[chain, at, :], vb[chain, at, :].astype(F32) * beta], axis=1
                )
                wu = rhs + dot(xb[chain, at, :], rhs.astype(BF16))
                pair = halves(wu)
                wb[chain, at, :] = jnp.concatenate([pair[0][:, :C], pair[1][:, :C]], axis=1)
                ub[chain, at, :] = wu[:, C:]
                ts = tail[chain, at, :]
                both = dot(jnp.concatenate([ts, ts[:, :C]], axis=1), right_of(pair))
                carry_row = jnp.exp(total[chain, at, :][C - 1:C, :]) * (count_last < 0.5).astype(F32)
                move = jnp.where(eye, carry_row, 0.0) - both[:, :C]
                todo.append((at, move, both[:, C:]))

            def chained(move, offset, pair):
                both = fine(move, pair)
                return jnp.concatenate([both[:, :C], both[:, C:] + offset], axis=1)

            def keep(at, pair, offset):
                mcb[chain, at, :] = jnp.concatenate([pair[0][:, :C], pair[1][:, :C]], axis=1)
                ocb[chain, at, :] = offset

            one = halves(jnp.concatenate(todo[0][1:], axis=1))
            two = chained(halves(todo[1][1]), todo[1][2], one)
            rest = chained(
                halves(todo[3][1]), todo[3][2], halves(jnp.concatenate(todo[2][1:], axis=1))
            )
            two_s = halves(two)
            three = chained(halves(todo[2][1]), todo[2][2], two_s)
            four = chained(halves(rest[:, :C]), rest[:, C:], two_s)
            four_m = halves(four[:, :C])
            keep(todo[1][0], one, todo[0][2])
            keep(todo[2][0], two_s, two[:, C:])
            keep(todo[3][0], halves(three[:, :C]), three[:, C:])
            keep(todo[0][0], four_m, four[:, C:])
            maps[chain] = chained(four_m, four[:, C:], halves(maps[chain]))
            return carry

        lax.fori_loop(0, BLOCKS // 4, body, 0)

    def map_copy(chain, src_x, to):
        cut = pl.ds(DK, DK) if src_x == 0 else pl.ds(0, 2 * DK)
        return pltpu.make_async_remote_copy(
            maps.at[chain, :, cut], gathered.at[src_x, chain, :, cut],
            pre_send.at[chain, to - 1], pre_recv.at[chain, src_x],
            device_id={"seq": 2 * to + core}, device_id_type=MESH,
        )

    def map_sends(chain, wait):
        for src_x in range(3):

            @pl.when(x == src_x)
            def _():
                for to in range(src_x + 1, 4):
                    copy = map_copy(chain, src_x, to)
                    if wait:
                        copy.wait_send()
                    else:
                        copy.start()

    arrived(0, kb.at[0])
    key_stage(0)
    arrived(1, kb.at[1])
    key_stage(1)
    arrived(2, vb.at[0])
    value_stage(0)
    map_sends(0, False)
    arrived(3, vb.at[1])
    value_stage(1)
    map_sends(1, False)

    def query_parts(chain, j):
        at = aligned(j * C, C)
        count_col = cols[j, :, 17 + 8 * chain:18 + 8 * chain]
        count_row = rows[j, 8 * chain + 1:8 * chain + 2, :]
        query = unit(qb[chain, at, :]) * (DK ** -0.5) * grow[chain, at, :]
        sh = shrink[chain, at, :]
        gram = lax.dot_general(
            left_of(halves(query)), jnp.concatenate([sh[:, :C], sh], axis=1),
            (((1,), (1,)), ((), ())), preferred_element_type=F32,
        )
        mix = jnp.where(lower & (count_col == count_row), gram, 0.0)
        live = query * (count_col < 0.5).astype(F32)
        return halves(jnp.concatenate([live, mix], axis=1))

    def query_stage(step, carry):
        for inner in range(4):
            j = step * 4 + inner
            leftb[aligned(j * C, C), :] = jnp.concatenate(query_parts(0, j), axis=1)
        return carry

    arrived(4, qb.at[0])
    lax.fori_loop(0, BLOCKS // 4, query_stage, 0)

    @pl.when(x == 0)
    def _():
        first[...] = jnp.zeros_like(first)

    for src_x in range(3):

        @pl.when(x > src_x)
        def _():
            for chain in range(2):
                map_copy(chain, src_x, src_x + 1).wait_recv()
                if src_x == 0:
                    first[chain] = gathered[0, chain, :, DK:]
                else:
                    first[chain] = gathered[src_x, chain, :, DK:] + fine(
                        halves(gathered[src_x, chain, :, 0:DK]), halves(first[chain])
                    )

    def state_stage(step, carry):
        for chain in range(2):
            now = first[chain]
            now_s = halves(now)
            incoming = right_of(now_s)

            def moved(at):
                mc = mcb[chain, at, :]
                return ocb[chain, at, :] + dot(
                    jnp.concatenate([mc, mc[:, :C]], axis=1), incoming
                )

            for inner in range(4):
                j = step * 4 + inner
                at = aligned(j * C, C)
                pair = now_s if inner == 0 else halves(moved(at))
                ws = wb[chain, at, :]
                fresh = ub[chain, at, :] - dot(
                    jnp.concatenate([ws, ws[:, :C]], axis=1), right_of(pair)
                )
                fh, fl = halves(fresh)
                right[chain, j] = stack(pair[0], fh, pair[1], fl)
            first[chain] = moved(aligned(step * 4 * C, C))
        return carry

    lax.fori_loop(0, BLOCKS // 4, state_stage, 0)

    def output_stage(chain):
        def body(step, carry):
            p = lax.rem(step + group // 4, BLOCKS // 4)
            for inner in range(4):
                j = 4 * p + inner
                at = aligned(j * C, C)
                if chain == 0:
                    ls = leftb[at, :]
                    left = jnp.concatenate([ls, ls[:, :2 * C]], axis=1)
                else:
                    left = left_of(query_parts(chain, j))
                hold = right[chain, j]
                out = dot(left, stack(hold[:2 * C], hold))
                core_buf[chain, at, :] = out.astype(BF16)
            for inner in range(8):
                b = 8 * p + inner
                src = core_buf.at[chain, aligned(b * TOK, TOK), :]
                dst = back.at[chain, :, my_cols]

                @pl.when(b != blk)
                def _():
                    pltpu.make_async_remote_copy(
                        src, dst, back_send.at[chain], back_recv.at[chain],
                        device_id={"head": lax.rem(b, GROUPS), "seq": seq - core + b // GROUPS},
                        device_id_type=MESH,
                    ).start()

                @pl.when(b == blk)
                def _():
                    pltpu.make_async_copy(src, dst, back_recv.at[chain]).start()

            return carry

        lax.fori_loop(0, BLOCKS // 4, body, 0)

    output_stage(0)
    arrived(5, qb.at[1])
    output_stage(1)

    for chain in range(2):
        pltpu.make_async_copy(back.at[chain], back.at[chain], back_recv.at[chain]).wait()

        def finish(step, carry, chain=chain):
            for inner in range(8):
                at = aligned((step * 8 + inner) * DK, DK)
                wide = back[chain, :, at].astype(F32)
                norm = lax.rsqrt(jnp.mean(wide * wide, axis=-1, keepdims=True) + NORM_EPS)
                out_ref[chain, :, at] = (wide * norm * scale[chain, :, at]).astype(BF16)
            return carry

        lax.fori_loop(0, H // 8, finish, 0)

    map_sends(0, True)
    map_sends(1, True)

    many = (OWNERS - 1) * DK
    for slot in range(6):
        sent = k_in.at[0, :, pl.ds(0, many)]
        pltpu.make_async_copy(sent, sent, send.at[slot]).wait()
    for chain in range(2):
        sent = back.at[0, :, pl.ds(0, many)]
        pltpu.make_async_copy(sent, sent, back_send.at[chain]).wait()
    lat_sent = lb.at[:, pl.ds(0, (GROUPS - 1) * TOK), :]
    pltpu.make_async_copy(lat_sent, lat_sent, send.at[LAT]).wait()
    aux_sent = aux_src.at[pl.ds(0, OWNERS - 1)]
    pltpu.make_async_copy(aux_sent, aux_sent, send.at[AUX]).wait()


def per_device(
    query_rows, key_rows, value_rows, beta_raw, gate_latent, gate_up, dt_bias, decay_log,
    boundary, modality, out_gate, norm_gain,
):
    span = lambda width, dtype: pltpu.VMEM((2, SPAN, width), dtype)
    return pl.pallas_call(
        kernel,
        out_shape=jax.ShapeDtypeStruct((2, TOK, H * DK), BF16),
        in_specs=[ANY, ANY, ANY, VM, VM, VM, ANY, ANY, ANY, SM, ANY, VM],
        out_specs=VM,
        scratch_shapes=[
            span(DK, BF16), span(DK, BF16), span(DK, BF16), span(DK, BF16),
            pltpu.VMEM((OWNERS, 8, C), BF16),
            pltpu.VMEM((OWNERS, 8, C), BF16),
            pltpu.VMEM((DK, DK), BF16),
            pltpu.VMEM((2, DK), F32),
            pltpu.VMEM((2, TOK, H * DK), BF16),
            pltpu.VMEM((2, TOK, H * DK), F32),
            span(DK, F32),
            span(DK, F32),
            span(2 * DK, BF16),
            span(DK, F32),
            span(2 * DK, BF16),
            span(DK, BF16),
            span(2 * DK, BF16),
            span(DK, F32),
            span(2 * DK, BF16),
            span(DK, F32),
            pltpu.VMEM((2, BLOCKS, 4 * C, DK), BF16),
            pltpu.VMEM((BLOCKS, C, C), F32),
            pltpu.VMEM((BLOCKS, 16, C), F32),
            pltpu.VMEM((2, DK, 2 * DK), F32),
            pltpu.VMEM((2, DK, DK), F32),
            pltpu.VMEM((3, 2, DK, 2 * DK), F32),
            pltpu.VMEM((SPAN, 4 * C), BF16),
            span(DK, BF16),
            pltpu.VMEM((2, TOK, H * DK), BF16),
            pltpu.SemaphoreType.DMA((9,)),
            pltpu.SemaphoreType.DMA((9,)),
            pltpu.SemaphoreType.DMA((2, 3)),
            pltpu.SemaphoreType.DMA((2, 3)),
            pltpu.SemaphoreType.DMA((2,)),
            pltpu.SemaphoreType.DMA((2,)),
            pltpu.SemaphoreType.DMA((3,)),
        ],
        compiler_params=pltpu.CompilerParams(
            collective_id=0, has_side_effects=True, vmem_limit_bytes=60 * 1024 * 1024
        ),
        name="delta_attention",
    )(
        query_rows, key_rows, value_rows, beta_raw.transpose(0, 2, 1), boundary, modality, gate_latent, gate_up, dt_bias, decay_log,
        out_gate, norm_gain.reshape(1, -1),
    )


def solution(mesh):
    rows = P(None, ("seq", "head"), None)
    flat = P(None, ("seq", "head"))
    return jax.shard_map(
        per_device,
        mesh=mesh,
        in_specs=(rows, rows, rows, rows, rows, P(), P(), P(), flat, flat, rows, P()),
        out_specs=rows,
        check_vma=False,
    )
```

```python
import functools

import jax
import jax.numpy as jnp
from jax import lax
from jax.experimental import pallas as pl
from jax.experimental.pallas import tpu as pltpu
from jax.sharding import PartitionSpec as P

H = 32
DK = 128
TOK = 64
C = 128
SPAN = 2048
BLOCKS = SPAN // C
GROUPS = 16
OWNERS = 32
NORM_EPS = 1e-6
MESH = pl.DeviceIdType.MESH
F32 = jnp.float32
BF16 = jnp.bfloat16
ANY = pl.BlockSpec(memory_space=pl.ANY)
VM = pl.BlockSpec(memory_space=pltpu.VMEM)
SM = pl.BlockSpec(memory_space=pltpu.SMEM)
LAT, AUX, PASS = 6, 7, 8
KEY_STEP = 8


def halves(x):
    high = x.astype(BF16)
    return high, (x - high.astype(F32)).astype(BF16)


def left_of(pair):
    return jnp.concatenate([pair[0], pair[1], pair[0]], axis=1)


def right_of(pair):
    return jnp.concatenate([pair[0], pair[0], pair[1]], axis=0)


def dot(left, right):
    return jnp.dot(left, right, preferred_element_type=F32)


def fine(left, right):
    return dot(left_of(left), right_of(right))


def stack(*parts):
    return jnp.concatenate(parts, axis=0)


def softplus(x):
    u = jnp.exp(-jnp.abs(x))
    series = u * (1.0 - u * (0.5 - u * (1.0 / 3.0 - u * 0.25)))
    return jnp.maximum(x, 0.0) + jnp.where(u < 0.015625, series, jnp.log(1.0 + u))


def unit(x):
    x = x.astype(F32)
    return x * lax.rsqrt(jnp.sum(x * x, axis=-1, keepdims=True) + NORM_EPS)


def aligned(start, size):
    return pl.ds(pl.multiple_of(start, size), size)


def kernel(
    q_in, k_in, v_in, beta_in, mark_in, kind_in, lat_in, up_in, bias_in, rate_in, gate_in, gain_in,
    out_ref,
    kb, vb, qb, lb, auxb, aux_src, upb, biasb, gateb, scale,
    total, grow, shrink, keyg, tail, xb, wb, ub, mcb, ocb, right, cols, rows,
    maps, first, gathered, states, leftb, core_buf, back,
    send, recv, pre_send, pre_recv, back_send, back_recv, here,
):
    group = lax.axis_index("head")
    seq = lax.axis_index("seq")
    core = lax.rem(seq, 2)
    x = seq // 2
    me = group * 2 + core
    blk = core * GROUPS + group

    def owner_id(owner):
        return {"head": owner // 2, "seq": seq - core + lax.rem(owner, 2)}

    barrier = pltpu.get_barrier_semaphore()

    def greet(step, carry):
        pl.semaphore_signal(
            barrier, inc=1, device_id=owner_id(lax.rem(me + step, OWNERS)), device_id_type=MESH
        )
        return carry

    lax.fori_loop(1, OWNERS, greet, 0)
    for away in (1, 2, 3):
        pl.semaphore_signal(
            barrier, inc=1, device_id={"seq": lax.rem(seq + 2 * away, 8)}, device_id_type=MESH
        )

    my_cols = aligned(me * DK, DK)
    my_rows = aligned(blk * TOK, TOK)
    local = (
        pltpu.make_async_copy(up_in.at[:, my_cols], upb, here.at[0]),
        pltpu.make_async_copy(bias_in.at[:, my_cols], biasb, here.at[1]),
        pltpu.make_async_copy(gate_in, gateb, here.at[2]),
    )
    for copy in local:
        copy.start()

    ri = lax.broadcasted_iota(jnp.int32, (C, C), 0)
    ci = lax.broadcasted_iota(jnp.int32, (C, C), 1)
    si = lax.broadcasted_iota(jnp.int32, (8 * OWNERS, H), 0)
    sj = lax.broadcasted_iota(jnp.int32, (8 * OWNERS, H), 1)
    select = ((si % 8 == 0) & (si // 8 == sj)).astype(BF16)
    part = lax.broadcasted_iota(jnp.int32, (8 * OWNERS, TOK), 0) % 8
    ti = lax.broadcasted_iota(jnp.int32, (TOK, C), 0)
    tj = lax.broadcasted_iota(jnp.int32, (TOK, C), 1)
    packed = jnp.zeros((8 * OWNERS, C), F32)
    for b in range(2):
        small = dot(select, beta_in[b])
        small = jnp.where(part == 1, mark_in[b:b + 1, :].astype(F32), small)
        small = jnp.where(part == 2, kind_in[b:b + 1, :].astype(F32), small)
        packed = packed + dot(small.astype(BF16), (tj == ti + b * TOK).astype(BF16))
    aux_src[...] = packed.reshape(OWNERS, 8, C).astype(BF16)

    pl.semaphore_wait(barrier, OWNERS + 2)

    def lat_send(step, carry):
        pltpu.make_async_remote_copy(
            lat_in, lb.at[:, my_rows, :], send.at[LAT], recv.at[LAT],
            device_id={"head": lax.rem(group + 5 * step, GROUPS), "seq": seq}, device_id_type=MESH,
        ).start()
        return carry

    lax.fori_loop(1, GROUPS, lat_send, 0)
    pltpu.make_async_copy(lat_in, lb.at[:, my_rows, :], recv.at[LAT]).start()

    def aux_send(step, carry):
        other = lax.rem(me + step, OWNERS)
        pltpu.make_async_remote_copy(
            aux_src.at[other], auxb.at[blk], send.at[AUX], recv.at[AUX],
            device_id=owner_id(other), device_id_type=MESH,
        ).start()
        return carry

    lax.fori_loop(1, OWNERS, aux_send, 0)
    pltpu.make_async_copy(aux_src.at[me], auxb.at[blk], recv.at[AUX]).start()

    def spread(slot, src, dst, chain):
        def one(step, carry):
            other = lax.rem(me + 5 * step, OWNERS)
            pltpu.make_async_remote_copy(
                src.at[chain, :, aligned(other * DK, DK)], dst.at[chain, my_rows, :],
                send.at[slot], recv.at[slot], device_id=owner_id(other), device_id_type=MESH,
            ).start()
            return carry

        lax.fori_loop(1, OWNERS, one, 0)
        pltpu.make_async_copy(
            src.at[chain, :, my_cols], dst.at[chain, my_rows, :], recv.at[slot]
        ).start()

    def arrived(slot, dst):
        pltpu.make_async_copy(dst, dst, recv.at[slot]).wait()

    spread(0, k_in, kb, 0)

    local[2].wait()

    def gates(step, carry):
        for inner in range(4):
            at = aligned((step * 4 + inner) * DK, DK)
            for chain in range(2):
                scale[chain, :, at] = gain_in[0:1, at] * jax.nn.sigmoid(
                    gateb[chain, :, at].astype(F32)
                )
        return carry

    lax.fori_loop(0, H // 4, gates, 0)

    half = lb.at[:, aligned(core * (SPAN // 2), SPAN // 2), :]
    arrived(LAT, half)
    pass_on = pltpu.make_async_remote_copy(
        half, half, send.at[PASS], recv.at[PASS],
        device_id={"seq": seq + 1 - 2 * core}, device_id_type=MESH,
    )
    pass_on.start()
    spread(1, k_in, kb, 1)
    spread(2, v_in, vb, 0)
    spread(3, v_in, vb, 1)
    spread(4, q_in, qb, 0)
    spread(5, q_in, qb, 1)

    eye = ri == ci
    strict = ri > ci
    lower = ri >= ci
    tri = lower.astype(BF16)
    tri2 = jnp.concatenate([tri, tri], axis=1)
    upper = (ri <= ci).astype(BF16)
    lane = lax.broadcasted_iota(jnp.int32, (8, C), 1)
    local[0].wait()
    local[1].wait()
    arrived(AUX, auxb)

    rate = -jnp.exp(jnp.full((1, DK), rate_in[me], F32))

    def decays(step, start):
        for inner in range(4):
            j = lax.rem(start + step * 4 + inner, BLOCKS)
            at = aligned(j * C, C)
            one = auxb[2 * j].astype(F32)
            two = auxb[2 * j + 1].astype(F32)
            mine = stack(
                jnp.where(lane < TOK, one, pltpu.roll(two, TOK, 1)),
                jnp.where(lane < TOK, pltpu.roll(one, TOK, 1), two),
            )
            counts = dot(mine.astype(BF16), upper)
            tall = stack(jax.nn.sigmoid(mine), counts, mine, jnp.zeros((C - 48, C), F32)).T
            cols[j] = tall
            rows[j] = counts
            for chain in range(2):
                kind = tall[:, 34 + 8 * chain:35 + 8 * chain]
                pre = dot(lb[chain, at, :], upb[...]).astype(BF16).astype(F32)
                bias = jnp.where(kind > 0.5, biasb[1:2, :], biasb[0:1, :])
                decay = rate * softplus(pre + bias)
                dh, dl = halves(decay)
                total[chain, at, :] = dot(tri2, stack(dh, dl))
        return start

    lax.fori_loop(0, BLOCKS // 8, decays, core * (BLOCKS // 2))
    pass_on.wait()
    lax.fori_loop(0, BLOCKS // 8, decays, (1 - core) * (BLOCKS // 2))

    near = ((ri // 16) == (ci // 16)).astype(BF16)
    eye_wide = eye.astype(F32)
    eye_low = eye.astype(BF16)
    parts = []
    for width in (16, 32, 64):
        same_pair = (ri // (2 * width)) == (ci // (2 * width))
        parts.append((same_pair & ((ri // width) != (ci // width))).astype(BF16))

    def key_stage(chain):
        def body(step, carry):
            todo = []
            for inner in range(KEY_STEP):
                j = step * KEY_STEP + inner
                at = aligned(j * C, C)
                beta = cols[j, :, 8 * chain:8 * chain + 1]
                count_col = cols[j, :, 17 + 8 * chain:18 + 8 * chain]
                count_row = rows[j, 8 * chain + 1:8 * chain + 2, :]
                count_last = count_row[:, C - 1:C]
                sums = total[chain, at, :]
                last = sums[C - 1:C, :]
                growth = jnp.exp(sums)
                grow[chain, at, :] = growth
                key = unit(kb[chain, at, :])
                key_grow = key * growth
                alive = (count_col < 0.5).astype(F32)
                keyg[chain, at, :] = key_grow * (alive * beta)
                shrunk = halves(key * jnp.exp(-sums))
                shrink[chain, at, :] = jnp.concatenate(shrunk, axis=1)
                mask = (count_col == count_last).astype(F32)
                moved_t = halves((key * jnp.exp(last - sums) * mask).T)
                tail[chain, at, :] = jnp.concatenate(moved_t, axis=1)
                gram = lax.dot_general(
                    key_grow.astype(BF16), shrunk[0],
                    (((1,), (1,)), ((), ())), preferred_element_type=F32,
                )
                low = jnp.where(strict & (count_col == count_row), gram, 0.0) * beta
                low = low.astype(BF16)
                todo.append(dict(at=at, low=low, d=low * near))
            for t in todo:
                t["d2"] = dot(t["d"], t["d"]).astype(BF16)
            for t in todo:
                start = eye_low - t["d"]
                both = dot(stack(start, t["d2"]), t["d2"])
                t["t"] = start.astype(F32) + both[:C]
                t["d4"] = both[C:].astype(BF16)
            for t in todo:
                both = dot(stack(t["t"].astype(BF16), t["d4"]), t["d4"])
                t["t"] = t["t"] + both[:C]
                t["d8"] = both[C:].astype(BF16)
            for t in todo:
                t["t"] = t["t"] + dot(t["t"].astype(BF16), t["d8"])
            for part in parts:
                for t in todo:
                    t["tb"] = t["t"].astype(BF16)
                    t["y"] = dot(t["low"] * part, t["tb"]).astype(BF16)
                for t in todo:
                    t["t"] = t["t"] - dot(t["tb"], t["y"])
            for t in todo:
                xb[chain, t["at"], :] = (t["t"] - eye_wide).astype(BF16)
            return carry

        lax.fori_loop(0, BLOCKS // KEY_STEP, body, 0)

    def value_stage(chain):
        maps[chain, :, 0:DK] = eye.astype(F32)
        maps[chain, :, DK:] = jnp.zeros((DK, DK), F32)

        def body(step, carry):
            todo = []
            for inner in range(8):
                j = step * 8 + inner
                at = aligned(j * C, C)
                beta = cols[j, :, 8 * chain:8 * chain + 1]
                count_last = rows[j, 8 * chain + 1:8 * chain + 2, C - 1:C]
                rhs = jnp.concatenate(
                    [keyg[chain, at, :], vb[chain, at, :].astype(F32) * beta], axis=1
                )
                wu = rhs + dot(xb[chain, at, :], rhs.astype(BF16))
                pair = halves(wu)
                wb[chain, at, :] = jnp.concatenate([pair[0][:, :C], pair[1][:, :C]], axis=1)
                ub[chain, at, :] = wu[:, C:]
                ts = tail[chain, at, :]
                both = dot(jnp.concatenate([ts, ts[:, :C]], axis=1), right_of(pair))
                carry_row = jnp.exp(total[chain, at, :][C - 1:C, :]) * (count_last < 0.5).astype(F32)
                move = jnp.where(eye, carry_row, 0.0) - both[:, :C]
                todo.append((at, move, both[:, C:]))

            def chained(move, offset, pair):
                both = fine(move, pair)
                return jnp.concatenate([both[:, :C], both[:, C:] + offset], axis=1)

            def keep(at, pair, offset):
                mcb[chain, at, :] = jnp.concatenate([pair[0][:, :C], pair[1][:, :C]], axis=1)
                ocb[chain, at, :] = offset

            past = []
            for four_of in (todo[:4], todo[4:]):
                one = halves(jnp.concatenate(four_of[0][1:], axis=1))
                two = chained(halves(four_of[1][1]), four_of[1][2], one)
                rest = chained(
                    halves(four_of[3][1]), four_of[3][2], halves(jnp.concatenate(four_of[2][1:], axis=1))
                )
                two_s = halves(two)
                three = chained(halves(four_of[2][1]), four_of[2][2], two_s)
                four = chained(halves(rest[:, :C]), rest[:, C:], two_s)
                four_m = halves(four[:, :C])
                keep(four_of[1][0], one, four_of[0][2])
                keep(four_of[2][0], two_s, two[:, C:])
                keep(four_of[3][0], halves(three[:, :C]), three[:, C:])
                keep(four_of[0][0], four_m, four[:, C:])
                past.append((four_m, four[:, C:]))
            held = maps[chain]
            for move, offset in past:
                held = chained(move, offset, halves(held))
            maps[chain] = held
            return carry

        lax.fori_loop(0, BLOCKS // 8, body, 0)

    def map_copy(chain, src_x, to):
        cut = pl.ds(DK, DK) if src_x == 0 else pl.ds(0, 2 * DK)
        return pltpu.make_async_remote_copy(
            maps.at[chain, :, cut], gathered.at[src_x, chain, :, cut],
            pre_send.at[chain, to - 1], pre_recv.at[chain, src_x],
            device_id={"seq": 2 * to + core}, device_id_type=MESH,
        )

    def map_sends(chain, wait):
        for src_x in range(3):

            @pl.when(x == src_x)
            def _():
                for to in range(src_x + 1, 4):
                    copy = map_copy(chain, src_x, to)
                    if wait:
                        copy.wait_send()
                    else:
                        copy.start()

    arrived(0, kb.at[0])
    key_stage(0)
    arrived(1, kb.at[1])
    key_stage(1)
    arrived(2, vb.at[0])
    value_stage(0)
    map_sends(0, False)
    arrived(3, vb.at[1])
    value_stage(1)
    map_sends(1, False)

    def query_parts(chain, j):
        at = aligned(j * C, C)
        count_col = cols[j, :, 17 + 8 * chain:18 + 8 * chain]
        count_row = rows[j, 8 * chain + 1:8 * chain + 2, :]
        query = unit(qb[chain, at, :]) * (DK ** -0.5) * grow[chain, at, :]
        sh = shrink[chain, at, :]
        gram = lax.dot_general(
            left_of(halves(query)), jnp.concatenate([sh[:, :C], sh], axis=1),
            (((1,), (1,)), ((), ())), preferred_element_type=F32,
        )
        mix = jnp.where(lower & (count_col == count_row), gram, 0.0)
        live = query * (count_col < 0.5).astype(F32)
        return halves(jnp.concatenate([live, mix], axis=1))

    def query_stage(step, carry, chain):
        for inner in range(4):
            j = step * 4 + inner
            leftb[aligned(j * C, C), :] = jnp.concatenate(query_parts(chain, j), axis=1)
        return carry

    arrived(4, qb.at[0])
    lax.fori_loop(0, BLOCKS // 4, functools.partial(query_stage, chain=0), 0)

    @pl.when(x == 0)
    def _():
        first[...] = jnp.zeros_like(first)

    for src_x in range(3):

        @pl.when(x > src_x)
        def _():
            for chain in range(2):
                map_copy(chain, src_x, src_x + 1).wait_recv()
                if src_x == 0:
                    first[chain] = gathered[0, chain, :, DK:]
                else:
                    first[chain] = gathered[src_x, chain, :, DK:] + fine(
                        halves(gathered[src_x, chain, :, 0:DK]), halves(first[chain])
                    )

    def moved(chain, at, incoming):
        mc = mcb[chain, at, :]
        return ocb[chain, at, :] + dot(jnp.concatenate([mc, mc[:, :C]], axis=1), incoming)

    now = [first[0], first[1]]
    for four in range(BLOCKS // 4):
        for chain in range(2):
            incoming = right_of(halves(now[chain]))
            states[chain, four] = incoming
            if four < BLOCKS // 4 - 1:
                now[chain] = moved(chain, pl.ds(four * 4 * C, C), incoming)

    def state_stage(chain):
        def body(step, carry):
            todo = []
            for inner in range(8):
                j = step * 8 + inner
                at = aligned(j * C, C)
                incoming = states[chain, step * 2 + inner // 4]
                if inner % 4 == 0:
                    todo.append((j, at, incoming))
                else:
                    todo.append((j, at, right_of(halves(moved(chain, at, incoming)))))
            for j, at, incoming in todo:
                ws = wb[chain, at, :]
                fresh = ub[chain, at, :] - dot(jnp.concatenate([ws, ws[:, :C]], axis=1), incoming)
                fh, fl = halves(fresh)
                right[chain, j] = stack(incoming[C:2 * C], fh, incoming[2 * C:], fl)
            return carry

        lax.fori_loop(0, BLOCKS // 8, body, 0)

    def output_stage(chain):
        def body(step, own):
            p = lax.rem(step + blk // 8, BLOCKS // 4)
            for inner in range(4):
                j = 4 * p + inner
                at = aligned(j * C, C)
                ls = leftb[at, :]
                hold = right[chain, j]
                out = dot(
                    jnp.concatenate([ls, ls[:, :2 * C]], axis=1), stack(hold[:2 * C], hold)
                )
                core_buf[chain, at, :] = out.astype(BF16)
            for inner in range(8):
                b = 8 * p + lax.rem(blk + inner, 8)
                src = core_buf.at[chain, aligned(b * TOK, TOK), :]
                dst = back.at[chain, :, my_cols]
                if own and inner == 0:
                    pltpu.make_async_copy(src, dst, back_recv.at[chain]).start()
                else:
                    pltpu.make_async_remote_copy(
                        src, dst, back_send.at[chain], back_recv.at[chain],
                        device_id={"head": lax.rem(b, GROUPS), "seq": seq - core + b // GROUPS},
                        device_id_type=MESH,
                    ).start()

        body(0, True)

        def others(step, carry):
            body(step, False)
            return carry

        lax.fori_loop(1, BLOCKS // 4, others, 0)

    state_stage(0)
    output_stage(0)
    state_stage(1)
    arrived(5, qb.at[1])
    lax.fori_loop(0, BLOCKS // 4, functools.partial(query_stage, chain=1), 0)
    output_stage(1)

    for chain in range(2):
        pltpu.make_async_copy(back.at[chain], back.at[chain], back_recv.at[chain]).wait()

        def finish(step, carry, chain=chain):
            for inner in range(8):
                at = aligned((step * 8 + inner) * DK, DK)
                wide = back[chain, :, at].astype(F32)
                norm = lax.rsqrt(jnp.mean(wide * wide, axis=-1, keepdims=True) + NORM_EPS)
                out_ref[chain, :, at] = (wide * norm * scale[chain, :, at]).astype(BF16)
            return carry

        lax.fori_loop(0, H // 8, finish, 0)

    map_sends(0, True)
    map_sends(1, True)

    many = (OWNERS - 1) * DK
    for slot in range(6):
        sent = k_in.at[0, :, pl.ds(0, many)]
        pltpu.make_async_copy(sent, sent, send.at[slot]).wait()
    for chain in range(2):
        sent = back.at[0, :, pl.ds(0, many)]
        pltpu.make_async_copy(sent, sent, back_send.at[chain]).wait()
    lat_sent = lb.at[:, pl.ds(0, (GROUPS - 1) * TOK), :]
    pltpu.make_async_copy(lat_sent, lat_sent, send.at[LAT]).wait()
    aux_sent = aux_src.at[pl.ds(0, OWNERS - 1)]
    pltpu.make_async_copy(aux_sent, aux_sent, send.at[AUX]).wait()


def per_device(
    query_rows, key_rows, value_rows, beta_raw, gate_latent, gate_up, dt_bias, decay_log,
    boundary, modality, out_gate, norm_gain,
):
    span = lambda width, dtype: pltpu.VMEM((2, SPAN, width), dtype)
    return pl.pallas_call(
        kernel,
        out_shape=jax.ShapeDtypeStruct((2, TOK, H * DK), BF16),
        in_specs=[ANY, ANY, ANY, VM, VM, VM, ANY, ANY, ANY, SM, ANY, VM],
        out_specs=VM,
        scratch_shapes=[
            span(DK, BF16), span(DK, BF16), span(DK, BF16), span(DK, BF16),
            pltpu.VMEM((OWNERS, 8, C), BF16),
            pltpu.VMEM((OWNERS, 8, C), BF16),
            pltpu.VMEM((DK, DK), BF16),
            pltpu.VMEM((2, DK), F32),
            pltpu.VMEM((2, TOK, H * DK), BF16),
            pltpu.VMEM((2, TOK, H * DK), F32),
            span(DK, F32),
            span(DK, F32),
            span(2 * DK, BF16),
            span(DK, F32),
            span(2 * DK, BF16),
            span(DK, BF16),
            span(2 * DK, BF16),
            span(DK, F32),
            span(2 * DK, BF16),
            span(DK, F32),
            pltpu.VMEM((2, BLOCKS, 4 * C, DK), BF16),
            pltpu.VMEM((BLOCKS, C, C), F32),
            pltpu.VMEM((BLOCKS, 16, C), F32),
            pltpu.VMEM((2, DK, 2 * DK), F32),
            pltpu.VMEM((2, DK, DK), F32),
            pltpu.VMEM((3, 2, DK, 2 * DK), F32),
            pltpu.VMEM((2, BLOCKS // 4, 3 * C, DK), BF16),
            pltpu.VMEM((SPAN, 4 * C), BF16),
            span(DK, BF16),
            pltpu.VMEM((2, TOK, H * DK), BF16),
            pltpu.SemaphoreType.DMA((9,)),
            pltpu.SemaphoreType.DMA((9,)),
            pltpu.SemaphoreType.DMA((2, 3)),
            pltpu.SemaphoreType.DMA((2, 3)),
            pltpu.SemaphoreType.DMA((2,)),
            pltpu.SemaphoreType.DMA((2,)),
            pltpu.SemaphoreType.DMA((3,)),
        ],
        compiler_params=pltpu.CompilerParams(
            collective_id=0, has_side_effects=True, vmem_limit_bytes=60 * 1024 * 1024
        ),
        name="delta_attention",
    )(
        query_rows, key_rows, value_rows, beta_raw.transpose(0, 2, 1), boundary, modality, gate_latent, gate_up, dt_bias, decay_log,
        out_gate, norm_gain.reshape(1, -1),
    )


def solution(mesh):
    rows = P(None, ("seq", "head"), None)
    flat = P(None, ("seq", "head"))
    return jax.shard_map(
        per_device,
        mesh=mesh,
        in_specs=(rows, rows, rows, rows, rows, P(), P(), P(), flat, flat, rows, P()),
        out_specs=rows,
        check_vma=False,
    )
```

```python
import jax
import jax.numpy as jnp
from jax import lax
from jax.experimental import pallas as pl
from jax.experimental.pallas import tpu as pltpu
from jax.sharding import PartitionSpec as P

H = 32
DK = 128
TOK = 64
C = 128
SPAN = 2048
BLOCKS = SPAN // C
GROUPS = 16
OWNERS = 32
NORM_EPS = 1e-6
MESH = pl.DeviceIdType.MESH
F32 = jnp.float32
BF16 = jnp.bfloat16
ANY = pl.BlockSpec(memory_space=pl.ANY)
VM = pl.BlockSpec(memory_space=pltpu.VMEM)
SM = pl.BlockSpec(memory_space=pltpu.SMEM)
LAT, AUX, PASS = 6, 7, 8
KEY_STEP = 8


def halves(x):
    high = x.astype(BF16)
    return high, (x - high.astype(F32)).astype(BF16)


def left_of(pair):
    return jnp.concatenate([pair[0], pair[1], pair[0]], axis=1)


def right_of(pair):
    return jnp.concatenate([pair[0], pair[0], pair[1]], axis=0)


def dot(left, right):
    return jnp.dot(left, right, preferred_element_type=F32)


def fine(left, right):
    return dot(left_of(left), right_of(right))


def stack(*parts):
    return jnp.concatenate(parts, axis=0)


def softplus(x):
    u = jnp.exp(-jnp.abs(x))
    series = u * (1.0 - u * (0.5 - u * (1.0 / 3.0 - u * 0.25)))
    return jnp.maximum(x, 0.0) + jnp.where(u < 0.015625, series, jnp.log(1.0 + u))


def unit(x):
    x = x.astype(F32)
    return x * lax.rsqrt(jnp.sum(x * x, axis=-1, keepdims=True) + NORM_EPS)


def aligned(start, size):
    return pl.ds(pl.multiple_of(start, size), size)


def kernel(
    q_in, k_in, v_in, beta_hbm, mark_hbm, kind_hbm, lat_in, up_in, bias_in, rate_in, gate_in,
    gain_hbm,
    out_ref,
    beta_in, mark_in, kind_in, gain_in, kb, vb, qb, lb, auxb, aux_src, upb, biasb, gateb, scale,
    total, grow, shrink, keyg, tail, xb, wb, ub, mcb, ocb, right, cols, rows,
    maps, first, gathered, states, leftb, core_buf, back,
    send, recv, pre_send, pre_recv, back_send, back_recv, here,
):
    group = lax.axis_index("head")
    seq = lax.axis_index("seq")
    core = lax.rem(seq, 2)
    x = seq // 2
    me = group * 2 + core
    blk = core * GROUPS + group

    def owner_id(owner):
        return {"head": owner // 2, "seq": seq - core + lax.rem(owner, 2)}

    small = (
        pltpu.make_async_copy(beta_hbm, beta_in, here.at[3]),
        pltpu.make_async_copy(mark_hbm, mark_in, here.at[4]),
        pltpu.make_async_copy(kind_hbm, kind_in, here.at[5]),
        pltpu.make_async_copy(gain_hbm, gain_in, here.at[6]),
    )
    for copy in small:
        copy.start()

    barrier = pltpu.get_barrier_semaphore()

    def greet(step, carry):
        pl.semaphore_signal(
            barrier, inc=1, device_id=owner_id(lax.rem(me + step, OWNERS)), device_id_type=MESH
        )
        return carry

    lax.fori_loop(1, OWNERS, greet, 0)
    for away in (1, 2, 3):
        pl.semaphore_signal(
            barrier, inc=1, device_id={"seq": lax.rem(seq + 2 * away, 8)}, device_id_type=MESH
        )

    my_cols = aligned(me * DK, DK)
    my_rows = aligned(blk * TOK, TOK)
    local = (
        pltpu.make_async_copy(up_in.at[:, my_cols], upb, here.at[0]),
        pltpu.make_async_copy(bias_in.at[:, my_cols], biasb, here.at[1]),
        pltpu.make_async_copy(gate_in, gateb, here.at[2]),
    )
    for copy in local:
        copy.start()

    ri = lax.broadcasted_iota(jnp.int32, (C, C), 0)
    ci = lax.broadcasted_iota(jnp.int32, (C, C), 1)
    si = lax.broadcasted_iota(jnp.int32, (8 * OWNERS, H), 0)
    sj = lax.broadcasted_iota(jnp.int32, (8 * OWNERS, H), 1)
    select = ((si % 8 == 0) & (si // 8 == sj)).astype(BF16)
    part = lax.broadcasted_iota(jnp.int32, (8 * OWNERS, TOK), 0) % 8
    ti = lax.broadcasted_iota(jnp.int32, (TOK, C), 0)
    tj = lax.broadcasted_iota(jnp.int32, (TOK, C), 1)
    packed = jnp.zeros((8 * OWNERS, C), F32)
    for copy in small:
        copy.wait()
    for b in range(2):
        tiny = dot(select, beta_in[b])
        tiny = jnp.where(part == 1, mark_in[b:b + 1, :].astype(F32), tiny)
        tiny = jnp.where(part == 2, kind_in[b:b + 1, :].astype(F32), tiny)
        packed = packed + dot(tiny.astype(BF16), (tj == ti + b * TOK).astype(BF16))
    aux_src[...] = packed.reshape(OWNERS, 8, C).astype(BF16)

    pl.semaphore_wait(barrier, OWNERS + 2)

    def lat_send(step, carry):
        pltpu.make_async_remote_copy(
            lat_in, lb.at[:, my_rows, :], send.at[LAT], recv.at[LAT],
            device_id={"head": lax.rem(group + 5 * step, GROUPS), "seq": seq}, device_id_type=MESH,
        ).start()
        return carry

    lax.fori_loop(1, GROUPS, lat_send, 0)
    pltpu.make_async_copy(lat_in, lb.at[:, my_rows, :], recv.at[LAT]).start()

    def aux_send(step, carry):
        other = lax.rem(me + step, OWNERS)
        pltpu.make_async_remote_copy(
            aux_src.at[other], auxb.at[blk], send.at[AUX], recv.at[AUX],
            device_id=owner_id(other), device_id_type=MESH,
        ).start()
        return carry

    lax.fori_loop(1, OWNERS, aux_send, 0)
    pltpu.make_async_copy(aux_src.at[me], auxb.at[blk], recv.at[AUX]).start()

    def spread(slot, src, dst, chain):
        def one(step, carry):
            other = lax.rem(me + 5 * step, OWNERS)
            pltpu.make_async_remote_copy(
                src.at[chain, :, aligned(other * DK, DK)], dst.at[chain, my_rows, :],
                send.at[slot], recv.at[slot], device_id=owner_id(other), device_id_type=MESH,
            ).start()
            return carry

        lax.fori_loop(1, OWNERS, one, 0)
        pltpu.make_async_copy(
            src.at[chain, :, my_cols], dst.at[chain, my_rows, :], recv.at[slot]
        ).start()

    def arrived(slot, dst):
        pltpu.make_async_copy(dst, dst, recv.at[slot]).wait()

    spread(0, k_in, kb, 0)

    local[2].wait()

    def gates(step, carry):
        for inner in range(4):
            at = aligned((step * 4 + inner) * DK, DK)
            for chain in range(2):
                scale[chain, :, at] = gain_in[0:1, at] * jax.nn.sigmoid(
                    gateb[chain, :, at].astype(F32)
                )
        return carry

    lax.fori_loop(0, H // 4, gates, 0)

    half = lb.at[:, aligned(core * (SPAN // 2), SPAN // 2), :]
    arrived(LAT, half)
    pass_on = pltpu.make_async_remote_copy(
        half, half, send.at[PASS], recv.at[PASS],
        device_id={"seq": seq + 1 - 2 * core}, device_id_type=MESH,
    )
    pass_on.start()
    spread(1, k_in, kb, 1)
    spread(2, v_in, vb, 0)
    spread(3, v_in, vb, 1)
    spread(4, q_in, qb, 0)
    spread(5, q_in, qb, 1)

    eye = ri == ci
    strict = ri > ci
    lower = ri >= ci
    tri = lower.astype(BF16)
    tri2 = jnp.concatenate([tri, tri], axis=1)
    upper = (ri <= ci).astype(BF16)
    lane = lax.broadcasted_iota(jnp.int32, (8, C), 1)
    local[0].wait()
    local[1].wait()
    arrived(AUX, auxb)

    rate = -jnp.exp(jnp.full((1, DK), rate_in[me], F32))

    def decays(step, start):
        for inner in range(4):
            j = lax.rem(start + step * 4 + inner, BLOCKS)
            at = aligned(j * C, C)
            one = auxb[2 * j].astype(F32)
            two = auxb[2 * j + 1].astype(F32)
            mine = stack(
                jnp.where(lane < TOK, one, pltpu.roll(two, TOK, 1)),
                jnp.where(lane < TOK, pltpu.roll(one, TOK, 1), two),
            )
            counts = dot(mine.astype(BF16), upper)
            tall = stack(jax.nn.sigmoid(mine), counts, mine, jnp.zeros((C - 48, C), F32)).T
            cols[j] = tall
            rows[j] = counts
            for chain in range(2):
                kind = tall[:, 34 + 8 * chain:35 + 8 * chain]
                pre = dot(lb[chain, at, :], upb[...]).astype(BF16).astype(F32)
                bias = jnp.where(kind > 0.5, biasb[1:2, :], biasb[0:1, :])
                decay = rate * softplus(pre + bias)
                dh, dl = halves(decay)
                total[chain, at, :] = dot(tri2, stack(dh, dl))
        return start

    lax.fori_loop(0, BLOCKS // 8, decays, core * (BLOCKS // 2))
    pass_on.wait()
    lax.fori_loop(0, BLOCKS // 8, decays, (1 - core) * (BLOCKS // 2))

    near = ((ri // 16) == (ci // 16)).astype(BF16)
    eye_wide = eye.astype(F32)
    eye_low = eye.astype(BF16)
    parts = []
    for width in (16, 32, 64):
        same_pair = (ri // (2 * width)) == (ci // (2 * width))
        parts.append((same_pair & ((ri // width) != (ci // width))).astype(BF16))

    def key_stage(chain):
        def body(step, carry):
            todo = []
            for inner in range(KEY_STEP):
                j = step * KEY_STEP + inner
                at = aligned(j * C, C)
                beta = cols[j, :, 8 * chain:8 * chain + 1]
                count_col = cols[j, :, 17 + 8 * chain:18 + 8 * chain]
                count_row = rows[j, 8 * chain + 1:8 * chain + 2, :]
                count_last = count_row[:, C - 1:C]
                sums = total[chain, at, :]
                last = sums[C - 1:C, :]
                growth = jnp.exp(sums)
                grow[chain, at, :] = growth
                key = unit(kb[chain, at, :])
                key_grow = key * growth
                alive = (count_col < 0.5).astype(F32)
                keyg[chain, at, :] = key_grow * (alive * beta)
                shrunk = halves(key * jnp.exp(-sums))
                shrink[chain, at, :] = jnp.concatenate(shrunk, axis=1)
                mask = (count_col == count_last).astype(F32)
                moved_t = halves((key * jnp.exp(last - sums) * mask).T)
                tail[chain, at, :] = jnp.concatenate(moved_t, axis=1)
                gram = lax.dot_general(
                    key_grow.astype(BF16), shrunk[0],
                    (((1,), (1,)), ((), ())), preferred_element_type=F32,
                )
                low = jnp.where(strict & (count_col == count_row), gram, 0.0) * beta
                low = low.astype(BF16)
                todo.append(dict(at=at, low=low, d=low * near))
            for t in todo:
                t["d2"] = dot(t["d"], t["d"]).astype(BF16)
            for t in todo:
                start = eye_low - t["d"]
                both = dot(stack(start, t["d2"]), t["d2"])
                t["t"] = start.astype(F32) + both[:C]
                t["d4"] = both[C:].astype(BF16)
            for t in todo:
                both = dot(stack(t["t"].astype(BF16), t["d4"]), t["d4"])
                t["t"] = t["t"] + both[:C]
                t["d8"] = both[C:].astype(BF16)
            for t in todo:
                t["t"] = t["t"] + dot(t["t"].astype(BF16), t["d8"])
            for part in parts:
                for t in todo:
                    t["tb"] = t["t"].astype(BF16)
                    t["y"] = dot(t["low"] * part, t["tb"]).astype(BF16)
                for t in todo:
                    t["t"] = t["t"] - dot(t["tb"], t["y"])
            for t in todo:
                xb[chain, t["at"], :] = (t["t"] - eye_wide).astype(BF16)
            return carry

        lax.fori_loop(0, BLOCKS // KEY_STEP, body, 0)

    def value_stage(chain):
        maps[chain, :, 0:DK] = eye.astype(F32)
        maps[chain, :, DK:] = jnp.zeros((DK, DK), F32)

        def body(step, carry):
            todo = []
            for inner in range(8):
                j = step * 8 + inner
                at = aligned(j * C, C)
                beta = cols[j, :, 8 * chain:8 * chain + 1]
                count_last = rows[j, 8 * chain + 1:8 * chain + 2, C - 1:C]
                rhs = jnp.concatenate(
                    [keyg[chain, at, :], vb[chain, at, :].astype(F32) * beta], axis=1
                )
                wu = rhs + dot(xb[chain, at, :], rhs.astype(BF16))
                pair = halves(wu)
                wb[chain, at, :] = jnp.concatenate([pair[0][:, :C], pair[1][:, :C]], axis=1)
                ub[chain, at, :] = wu[:, C:]
                ts = tail[chain, at, :]
                both = dot(jnp.concatenate([ts, ts[:, :C]], axis=1), right_of(pair))
                carry_row = jnp.exp(total[chain, at, :][C - 1:C, :]) * (count_last < 0.5).astype(F32)
                move = jnp.where(eye, carry_row, 0.0) - both[:, :C]
                todo.append((at, move, both[:, C:]))

            def chained(move, offset, pair):
                both = fine(move, pair)
                return jnp.concatenate([both[:, :C], both[:, C:] + offset], axis=1)

            def keep(at, pair, offset):
                mcb[chain, at, :] = jnp.concatenate([pair[0][:, :C], pair[1][:, :C]], axis=1)
                ocb[chain, at, :] = offset

            past = []
            for four_of in (todo[:4], todo[4:]):
                one = halves(jnp.concatenate(four_of[0][1:], axis=1))
                two = chained(halves(four_of[1][1]), four_of[1][2], one)
                rest = chained(
                    halves(four_of[3][1]), four_of[3][2], halves(jnp.concatenate(four_of[2][1:], axis=1))
                )
                two_s = halves(two)
                three = chained(halves(four_of[2][1]), four_of[2][2], two_s)
                four = chained(halves(rest[:, :C]), rest[:, C:], two_s)
                four_m = halves(four[:, :C])
                keep(four_of[1][0], one, four_of[0][2])
                keep(four_of[2][0], two_s, two[:, C:])
                keep(four_of[3][0], halves(three[:, :C]), three[:, C:])
                keep(four_of[0][0], four_m, four[:, C:])
                past.append((four_m, four[:, C:]))
            held = maps[chain]
            for move, offset in past:
                held = chained(move, offset, halves(held))
            maps[chain] = held
            return carry

        lax.fori_loop(0, BLOCKS // 8, body, 0)

    def map_copy(chain, src_x, to):
        cut = pl.ds(DK, DK) if src_x == 0 else pl.ds(0, 2 * DK)
        return pltpu.make_async_remote_copy(
            maps.at[chain, :, cut], gathered.at[src_x, chain, :, cut],
            pre_send.at[chain, to - 1], pre_recv.at[chain, src_x],
            device_id={"seq": 2 * to + core}, device_id_type=MESH,
        )

    def map_sends(chain, wait):
        for src_x in range(3):

            @pl.when(x == src_x)
            def _():
                for to in range(src_x + 1, 4):
                    copy = map_copy(chain, src_x, to)
                    if wait:
                        copy.wait_send()
                    else:
                        copy.start()

    arrived(0, kb.at[0])
    key_stage(0)
    arrived(1, kb.at[1])
    key_stage(1)
    arrived(2, vb.at[0])
    value_stage(0)
    map_sends(0, False)
    arrived(3, vb.at[1])
    value_stage(1)
    map_sends(1, False)

    def query_parts(chain, j):
        at = aligned(j * C, C)
        count_col = cols[j, :, 17 + 8 * chain:18 + 8 * chain]
        count_row = rows[j, 8 * chain + 1:8 * chain + 2, :]
        query = unit(qb[chain, at, :]) * (DK ** -0.5) * grow[chain, at, :]
        sh = shrink[chain, at, :]
        gram = lax.dot_general(
            left_of(halves(query)), jnp.concatenate([sh[:, :C], sh], axis=1),
            (((1,), (1,)), ((), ())), preferred_element_type=F32,
        )
        mix = jnp.where(lower & (count_col == count_row), gram, 0.0)
        live = query * (count_col < 0.5).astype(F32)
        return halves(jnp.concatenate([live, mix], axis=1))

    def query_stage(step, carry):
        for inner in range(4):
            j = step * 4 + inner
            leftb[aligned(j * C, C), :] = jnp.concatenate(query_parts(0, j), axis=1)
        return carry

    arrived(4, qb.at[0])
    lax.fori_loop(0, BLOCKS // 4, query_stage, 0)

    def incoming_state(chain):
        @pl.when(x == 0)
        def _():
            first[chain] = jnp.zeros((DK, DK), F32)

        for src_x in range(3):

            @pl.when(x > src_x)
            def _():
                map_copy(chain, src_x, src_x + 1).wait_recv()
                if src_x == 0:
                    first[chain] = gathered[0, chain, :, DK:]
                else:
                    first[chain] = gathered[src_x, chain, :, DK:] + fine(
                        halves(gathered[src_x, chain, :, 0:DK]), halves(first[chain])
                    )

    def moved(chain, at, incoming):
        mc = mcb[chain, at, :]
        return ocb[chain, at, :] + dot(jnp.concatenate([mc, mc[:, :C]], axis=1), incoming)

    def state_stage(chain):
        now = first[chain]
        for four in range(BLOCKS // 4):
            incoming = right_of(halves(now))
            states[chain, four] = incoming
            if four < BLOCKS // 4 - 1:
                now = moved(chain, pl.ds(four * 4 * C, C), incoming)

        def body(step, carry):
            todo = []
            for inner in range(8):
                j = step * 8 + inner
                at = aligned(j * C, C)
                incoming = states[chain, step * 2 + inner // 4]
                if inner % 4 == 0:
                    todo.append((j, at, incoming))
                else:
                    todo.append((j, at, right_of(halves(moved(chain, at, incoming)))))
            for j, at, incoming in todo:
                ws = wb[chain, at, :]
                fresh = ub[chain, at, :] - dot(jnp.concatenate([ws, ws[:, :C]], axis=1), incoming)
                fh, fl = halves(fresh)
                right[chain, j] = stack(incoming[C:2 * C], fh, incoming[2 * C:], fl)
            return carry

        lax.fori_loop(0, BLOCKS // 8, body, 0)

    def output_stage(chain):
        def body(step, own):
            p = lax.rem(step + blk // 8, BLOCKS // 4)
            for inner in range(4):
                j = 4 * p + inner
                at = aligned(j * C, C)
                if chain == 0:
                    ls = leftb[at, :]
                    left = jnp.concatenate([ls, ls[:, :2 * C]], axis=1)
                else:
                    left = left_of(query_parts(chain, j))
                hold = right[chain, j]
                out = dot(left, stack(hold[:2 * C], hold))
                core_buf[chain, at, :] = out.astype(BF16)
            for inner in range(8):
                b = 8 * p + lax.rem(blk + inner, 8)
                src = core_buf.at[chain, aligned(b * TOK, TOK), :]
                dst = back.at[chain, :, my_cols]
                if own and inner == 0:
                    pltpu.make_async_copy(src, dst, back_recv.at[chain]).start()
                else:
                    pltpu.make_async_remote_copy(
                        src, dst, back_send.at[chain], back_recv.at[chain],
                        device_id={"head": lax.rem(b, GROUPS), "seq": seq - core + b // GROUPS},
                        device_id_type=MESH,
                    ).start()

        body(0, True)

        def others(step, carry):
            body(step, False)
            return carry

        lax.fori_loop(1, BLOCKS // 4, others, 0)

    incoming_state(0)
    state_stage(0)
    output_stage(0)
    incoming_state(1)
    state_stage(1)
    arrived(5, qb.at[1])
    output_stage(1)

    for chain in range(2):
        pltpu.make_async_copy(back.at[chain], back.at[chain], back_recv.at[chain]).wait()

        def finish(step, carry, chain=chain):
            for inner in range(8):
                at = aligned((step * 8 + inner) * DK, DK)
                wide = back[chain, :, at].astype(F32)
                norm = lax.rsqrt(jnp.mean(wide * wide, axis=-1, keepdims=True) + NORM_EPS)
                out_ref[chain, :, at] = (wide * norm * scale[chain, :, at]).astype(BF16)
            return carry

        lax.fori_loop(0, H // 8, finish, 0)

    map_sends(0, True)
    map_sends(1, True)

    many = (OWNERS - 1) * DK
    for slot in range(6):
        sent = k_in.at[0, :, pl.ds(0, many)]
        pltpu.make_async_copy(sent, sent, send.at[slot]).wait()
    for chain in range(2):
        sent = back.at[0, :, pl.ds(0, many)]
        pltpu.make_async_copy(sent, sent, back_send.at[chain]).wait()
    lat_sent = lb.at[:, pl.ds(0, (GROUPS - 1) * TOK), :]
    pltpu.make_async_copy(lat_sent, lat_sent, send.at[LAT]).wait()
    aux_sent = aux_src.at[pl.ds(0, OWNERS - 1)]
    pltpu.make_async_copy(aux_sent, aux_sent, send.at[AUX]).wait()


def per_device(
    query_rows, key_rows, value_rows, beta_raw, gate_latent, gate_up, dt_bias, decay_log,
    boundary, modality, out_gate, norm_gain,
):
    span = lambda width, dtype: pltpu.VMEM((2, SPAN, width), dtype)
    return pl.pallas_call(
        kernel,
        out_shape=jax.ShapeDtypeStruct((2, TOK, H * DK), BF16),
        in_specs=[ANY, ANY, ANY, ANY, ANY, ANY, ANY, ANY, ANY, SM, ANY, ANY],
        out_specs=VM,
        scratch_shapes=[
            pltpu.VMEM((2, H, TOK), BF16),
            pltpu.VMEM((2, TOK), jnp.int32),
            pltpu.VMEM((2, TOK), jnp.int32),
            pltpu.VMEM((1, H * DK), F32),
            span(DK, BF16), span(DK, BF16), span(DK, BF16), span(DK, BF16),
            pltpu.VMEM((OWNERS, 8, C), BF16),
            pltpu.VMEM((OWNERS, 8, C), BF16),
            pltpu.VMEM((DK, DK), BF16),
            pltpu.VMEM((2, DK), F32),
            pltpu.VMEM((2, TOK, H * DK), BF16),
            pltpu.VMEM((2, TOK, H * DK), F32),
            span(DK, F32),
            span(DK, F32),
            span(2 * DK, BF16),
            span(DK, F32),
            span(2 * DK, BF16),
            span(DK, BF16),
            span(2 * DK, BF16),
            span(DK, F32),
            span(2 * DK, BF16),
            span(DK, F32),
            pltpu.VMEM((2, BLOCKS, 4 * C, DK), BF16),
            pltpu.VMEM((BLOCKS, C, C), F32),
            pltpu.VMEM((BLOCKS, 16, C), F32),
            pltpu.VMEM((2, DK, 2 * DK), F32),
            pltpu.VMEM((2, DK, DK), F32),
            pltpu.VMEM((3, 2, DK, 2 * DK), F32),
            pltpu.VMEM((2, BLOCKS // 4, 3 * C, DK), BF16),
            pltpu.VMEM((SPAN, 4 * C), BF16),
            span(DK, BF16),
            pltpu.VMEM((2, TOK, H * DK), BF16),
            pltpu.SemaphoreType.DMA((9,)),
            pltpu.SemaphoreType.DMA((9,)),
            pltpu.SemaphoreType.DMA((2, 3)),
            pltpu.SemaphoreType.DMA((2, 3)),
            pltpu.SemaphoreType.DMA((2,)),
            pltpu.SemaphoreType.DMA((2,)),
            pltpu.SemaphoreType.DMA((7,)),
        ],
        compiler_params=pltpu.CompilerParams(
            collective_id=0, has_side_effects=True, vmem_limit_bytes=60 * 1024 * 1024
        ),
        name="delta_attention",
    )(
        query_rows, key_rows, value_rows, beta_raw.transpose(0, 2, 1), boundary, modality, gate_latent, gate_up, dt_bias, decay_log,
        out_gate, norm_gain.reshape(1, -1),
    )


def solution(mesh):
    rows = P(None, ("seq", "head"), None)
    flat = P(None, ("seq", "head"))
    return jax.shard_map(
        per_device,
        mesh=mesh,
        in_specs=(rows, rows, rows, rows, rows, P(), P(), P(), flat, flat, rows, P()),
        out_specs=rows,
        check_vma=False,
    )
```

```python
import jax
import jax.numpy as jnp
from jax import lax
from jax.experimental import pallas as pl
from jax.experimental.pallas import tpu as pltpu
from jax.sharding import PartitionSpec as P

H = 32
DK = 128
TOK = 64
C = 128
SPAN = 2048
BLOCKS = SPAN // C
GROUPS = 16
OWNERS = 32
NORM_EPS = 1e-6
MESH = pl.DeviceIdType.MESH
F32 = jnp.float32
BF16 = jnp.bfloat16
ANY = pl.BlockSpec(memory_space=pl.ANY)
VM = pl.BlockSpec(memory_space=pltpu.VMEM)
SM = pl.BlockSpec(memory_space=pltpu.SMEM)
LAT, AUX, PASS = 6, 8, 9
KEY_STEP = 8


def halves(x):
    high = x.astype(BF16)
    return high, (x - high.astype(F32)).astype(BF16)


def left_of(pair):
    return jnp.concatenate([pair[0], pair[1], pair[0]], axis=1)


def right_of(pair):
    return jnp.concatenate([pair[0], pair[0], pair[1]], axis=0)


def dot(left, right):
    return jnp.dot(left, right, preferred_element_type=F32)


def fine(left, right):
    return dot(left_of(left), right_of(right))


def stack(*parts):
    return jnp.concatenate(parts, axis=0)


def softplus(x):
    u = jnp.exp(-jnp.abs(x))
    series = u * (1.0 - u * (0.5 - u * (1.0 / 3.0)))
    return jnp.maximum(x, 0.0) + jnp.where(u < 0.0078125, series, jnp.log(1.0 + u))


def unit(x):
    x = x.astype(F32)
    return x * lax.rsqrt(jnp.sum(x * x, axis=-1, keepdims=True) + NORM_EPS)


def aligned(start, size):
    return pl.ds(pl.multiple_of(start, size), size)


def kernel(
    q_in, k_in, v_in, beta_hbm, mark_hbm, kind_hbm, lat_in, up_in, bias_in, rate_in, gate_in,
    gain_hbm,
    out_ref,
    beta_in, mark_in, kind_in, gain_in, kb, vb, qb, lb, auxb, aux_src, upb, biasb, gateb, scale,
    total, grow, shrink, keyg, tail, xb, wb, ub, mcb, ocb, right, cols, rows,
    maps, first, maps_out, gathered, states, leftb, core_buf, back,
    send, recv, pre_send, pre_recv, back_send, back_recv, here,
):
    group = lax.axis_index("head")
    seq = lax.axis_index("seq")
    core = lax.rem(seq, 2)
    x = seq // 2
    me = group * 2 + core
    blk = core * GROUPS + group

    def owner_id(owner):
        return {"head": owner // 2, "seq": seq - core + lax.rem(owner, 2)}

    small = (
        pltpu.make_async_copy(beta_hbm, beta_in, here.at[3]),
        pltpu.make_async_copy(mark_hbm, mark_in, here.at[4]),
        pltpu.make_async_copy(kind_hbm, kind_in, here.at[5]),
        pltpu.make_async_copy(gain_hbm, gain_in, here.at[6]),
    )
    for copy in small:
        copy.start()

    barrier = pltpu.get_barrier_semaphore()

    def greet(step, carry):
        pl.semaphore_signal(
            barrier, inc=1, device_id=owner_id(lax.rem(me + step, OWNERS)), device_id_type=MESH
        )
        return carry

    lax.fori_loop(1, OWNERS, greet, 0)
    for away in (1, 2, 3):
        pl.semaphore_signal(
            barrier, inc=1, device_id={"seq": lax.rem(seq + 2 * away, 8)}, device_id_type=MESH
        )

    my_cols = aligned(me * DK, DK)
    my_rows = aligned(blk * TOK, TOK)
    local = (
        pltpu.make_async_copy(up_in.at[:, my_cols], upb, here.at[0]),
        pltpu.make_async_copy(bias_in.at[:, my_cols], biasb, here.at[1]),
        pltpu.make_async_copy(gate_in, gateb, here.at[2]),
    )
    for copy in local:
        copy.start()

    ri = lax.broadcasted_iota(jnp.int32, (C, C), 0)
    ci = lax.broadcasted_iota(jnp.int32, (C, C), 1)
    si = lax.broadcasted_iota(jnp.int32, (8 * OWNERS, H), 0)
    sj = lax.broadcasted_iota(jnp.int32, (8 * OWNERS, H), 1)
    select = ((si % 8 == 0) & (si // 8 == sj)).astype(BF16)
    part = lax.broadcasted_iota(jnp.int32, (8 * OWNERS, TOK), 0) % 8
    ti = lax.broadcasted_iota(jnp.int32, (TOK, C), 0)
    tj = lax.broadcasted_iota(jnp.int32, (TOK, C), 1)
    packed = jnp.zeros((8 * OWNERS, C), F32)
    for copy in small:
        copy.wait()
    for b in range(2):
        tiny = dot(select, beta_in[b])
        tiny = jnp.where(part == 1, mark_in[b:b + 1, :].astype(F32), tiny)
        tiny = jnp.where(part == 2, kind_in[b:b + 1, :].astype(F32), tiny)
        packed = packed + dot(tiny.astype(BF16), (tj == ti + b * TOK).astype(BF16))
    aux_src[...] = packed.reshape(OWNERS, 8, C).astype(BF16)

    pl.semaphore_wait(barrier, OWNERS + 2)

    def lat_spread(chain):
        def one(step, carry):
            pltpu.make_async_remote_copy(
                lat_in.at[chain], lb.at[chain, my_rows, :], send.at[LAT + chain],
                recv.at[LAT + chain],
                device_id={"head": lax.rem(group + 5 * step, GROUPS), "seq": seq},
                device_id_type=MESH,
            ).start()
            return carry

        lax.fori_loop(1, GROUPS, one, 0)
        pltpu.make_async_copy(
            lat_in.at[chain], lb.at[chain, my_rows, :], recv.at[LAT + chain]
        ).start()

    lat_spread(0)

    def aux_send(step, carry):
        other = lax.rem(me + step, OWNERS)
        pltpu.make_async_remote_copy(
            aux_src.at[other], auxb.at[blk], send.at[AUX], recv.at[AUX],
            device_id=owner_id(other), device_id_type=MESH,
        ).start()
        return carry

    lax.fori_loop(1, OWNERS, aux_send, 0)
    pltpu.make_async_copy(aux_src.at[me], auxb.at[blk], recv.at[AUX]).start()
    lat_spread(1)

    def spread(slot, src, dst, chain):
        def one(step, carry):
            other = lax.rem(me + 5 * step, OWNERS)
            pltpu.make_async_remote_copy(
                src.at[chain, :, aligned(other * DK, DK)], dst.at[chain, my_rows, :],
                send.at[slot], recv.at[slot], device_id=owner_id(other), device_id_type=MESH,
            ).start()
            return carry

        lax.fori_loop(1, OWNERS, one, 0)
        pltpu.make_async_copy(
            src.at[chain, :, my_cols], dst.at[chain, my_rows, :], recv.at[slot]
        ).start()

    def arrived(slot, dst):
        pltpu.make_async_copy(dst, dst, recv.at[slot]).wait()

    spread(0, k_in, kb, 0)

    local[2].wait()

    def gates(step, carry):
        for inner in range(4):
            at = aligned((step * 4 + inner) * DK, DK)
            for chain in range(2):
                scale[chain, :, at] = gain_in[0:1, at] * jax.nn.sigmoid(
                    gateb[chain, :, at].astype(F32)
                )
        return carry

    lax.fori_loop(0, H // 4, gates, 0)

    pass_on = []
    for chain in range(2):
        half = lb.at[chain, aligned(core * (SPAN // 2), SPAN // 2), :]
        arrived(LAT + chain, half)
        pass_on.append(
            pltpu.make_async_remote_copy(
                half, half, send.at[PASS + chain], recv.at[PASS + chain],
                device_id={"seq": seq + 1 - 2 * core}, device_id_type=MESH,
            )
        )
        pass_on[chain].start()
    spread(1, k_in, kb, 1)
    spread(2, v_in, vb, 0)
    spread(3, v_in, vb, 1)
    spread(4, q_in, qb, 0)
    spread(5, q_in, qb, 1)

    eye = ri == ci
    strict = ri > ci
    lower = ri >= ci
    tri = lower.astype(BF16)
    tri2 = jnp.concatenate([tri, tri], axis=1)
    upper = (ri <= ci).astype(BF16)
    lane = lax.broadcasted_iota(jnp.int32, (8, C), 1)
    local[0].wait()
    local[1].wait()
    arrived(AUX, auxb)

    rate = -jnp.exp(jnp.full((1, DK), rate_in[me], F32))

    def small_rows(step, carry):
        for inner in range(4):
            j = step * 4 + inner
            one = auxb[2 * j].astype(F32)
            two = auxb[2 * j + 1].astype(F32)
            mine = stack(
                jnp.where(lane < TOK, one, pltpu.roll(two, TOK, 1)),
                jnp.where(lane < TOK, pltpu.roll(one, TOK, 1), two),
            )
            counts = dot(mine.astype(BF16), upper)
            cols[j] = stack(jax.nn.sigmoid(mine), counts, mine, jnp.zeros((C - 48, C), F32)).T
            rows[j] = counts
        return carry

    def decay_stage(chain, half_core):
        for inner in range(BLOCKS // 2):
            j = half_core * (BLOCKS // 2) + inner
            at = aligned(j * C, C)
            kind = cols[j, :, 34 + 8 * chain:35 + 8 * chain]
            pre = dot(lb[chain, at, :], upb[...]).astype(BF16).astype(F32)
            bias = jnp.where(kind > 0.5, biasb[1:2, :], biasb[0:1, :])
            dh, dl = halves(rate * softplus(pre + bias))
            total[chain, at, :] = dot(tri2, stack(dh, dl))

    lax.fori_loop(0, BLOCKS // 4, small_rows, 0)
    for chain in range(2):
        decay_stage(chain, core)
        pass_on[chain].wait()
        decay_stage(chain, 1 - core)

    near = ((ri // 16) == (ci // 16)).astype(BF16)
    eye_wide = eye.astype(F32)
    eye_low = eye.astype(BF16)
    parts = []
    for width in (16, 32, 64):
        same_pair = (ri // (2 * width)) == (ci // (2 * width))
        parts.append((same_pair & ((ri // width) != (ci // width))).astype(BF16))

    def key_stage(chain):
        def body(step, carry):
            todo = []
            for inner in range(KEY_STEP):
                j = step * KEY_STEP + inner
                at = aligned(j * C, C)
                beta = cols[j, :, 8 * chain:8 * chain + 1]
                count_col = cols[j, :, 17 + 8 * chain:18 + 8 * chain]
                count_row = rows[j, 8 * chain + 1:8 * chain + 2, :]
                count_last = count_row[:, C - 1:C]
                sums = total[chain, at, :]
                last = sums[C - 1:C, :]
                growth = jnp.exp(sums)
                grow[chain, at, :] = growth
                key = unit(kb[chain, at, :])
                key_grow = key * growth
                alive = (count_col < 0.5).astype(F32)
                keyg[chain, at, :] = key_grow * (alive * beta)
                shrunk = halves(key * jnp.exp(-sums))
                shrink[chain, at, :] = jnp.concatenate(shrunk, axis=1)
                mask = (count_col == count_last).astype(F32)
                moved_t = halves((key * jnp.exp(last - sums) * mask).T)
                tail[chain, at, :] = jnp.concatenate(moved_t, axis=1)
                gram = lax.dot_general(
                    key_grow.astype(BF16), shrunk[0],
                    (((1,), (1,)), ((), ())), preferred_element_type=F32,
                )
                low = jnp.where(strict & (count_col == count_row), gram, 0.0) * beta
                low = low.astype(BF16)
                todo.append(dict(at=at, low=low, d=low * near))
            for t in todo:
                t["d2"] = dot(t["d"], t["d"]).astype(BF16)
            for t in todo:
                start = eye_low - t["d"]
                both = dot(stack(start, t["d2"]), t["d2"])
                t["t"] = start.astype(F32) + both[:C]
                t["d4"] = both[C:].astype(BF16)
            for t in todo:
                both = dot(stack(t["t"].astype(BF16), t["d4"]), t["d4"])
                t["t"] = t["t"] + both[:C]
                t["d8"] = both[C:].astype(BF16)
            for t in todo:
                t["t"] = t["t"] + dot(t["t"].astype(BF16), t["d8"])
            for part in parts:
                for t in todo:
                    t["tb"] = t["t"].astype(BF16)
                    t["y"] = dot(t["low"] * part, t["tb"]).astype(BF16)
                for t in todo:
                    t["t"] = t["t"] - dot(t["tb"], t["y"])
            for t in todo:
                xb[chain, t["at"], :] = (t["t"] - eye_wide).astype(BF16)
            return carry

        lax.fori_loop(0, BLOCKS // KEY_STEP, body, 0)

    def value_stage(chain):
        maps[chain, :, 0:DK] = eye.astype(F32)
        maps[chain, :, DK:] = jnp.zeros((DK, DK), F32)

        def body(step, carry):
            todo = []
            for inner in range(8):
                j = step * 8 + inner
                at = aligned(j * C, C)
                beta = cols[j, :, 8 * chain:8 * chain + 1]
                count_last = rows[j, 8 * chain + 1:8 * chain + 2, C - 1:C]
                rhs = jnp.concatenate(
                    [keyg[chain, at, :], vb[chain, at, :].astype(F32) * beta], axis=1
                )
                wu = rhs + dot(xb[chain, at, :], rhs.astype(BF16))
                pair = halves(wu)
                wb[chain, at, :] = jnp.concatenate([pair[0][:, :C], pair[1][:, :C]], axis=1)
                ub[chain, at, :] = wu[:, C:]
                ts = tail[chain, at, :]
                both = dot(jnp.concatenate([ts, ts[:, :C]], axis=1), right_of(pair))
                carry_row = jnp.exp(total[chain, at, :][C - 1:C, :]) * (count_last < 0.5).astype(F32)
                move = jnp.where(eye, carry_row, 0.0) - both[:, :C]
                todo.append((at, move, both[:, C:]))

            def chained(move, offset, pair):
                both = fine(move, pair)
                return jnp.concatenate([both[:, :C], both[:, C:] + offset], axis=1)

            def keep(at, pair, offset):
                mcb[chain, at, :] = jnp.concatenate([pair[0][:, :C], pair[1][:, :C]], axis=1)
                ocb[chain, at, :] = offset

            past = []
            for four_of in (todo[:4], todo[4:]):
                one = halves(jnp.concatenate(four_of[0][1:], axis=1))
                two = chained(halves(four_of[1][1]), four_of[1][2], one)
                rest = chained(
                    halves(four_of[3][1]), four_of[3][2], halves(jnp.concatenate(four_of[2][1:], axis=1))
                )
                two_s = halves(two)
                three = chained(halves(four_of[2][1]), four_of[2][2], two_s)
                four = chained(halves(rest[:, :C]), rest[:, C:], two_s)
                four_m = halves(four[:, :C])
                keep(four_of[1][0], one, four_of[0][2])
                keep(four_of[2][0], two_s, two[:, C:])
                keep(four_of[3][0], halves(three[:, :C]), three[:, C:])
                keep(four_of[0][0], four_m, four[:, C:])
                past.append((four_m, four[:, C:]))
            held = maps[chain]
            for move, offset in past:
                held = chained(move, offset, halves(held))
            maps[chain] = held
            return carry

        lax.fori_loop(0, BLOCKS // 8, body, 0)

    def map_copy(chain, src_x, to):
        cut = pl.ds(DK, DK) if src_x == 0 else pl.ds(0, 2 * DK)
        return pltpu.make_async_remote_copy(
            maps_out.at[chain, :, cut], gathered.at[src_x, chain, :, cut],
            pre_send.at[chain, to - 1], pre_recv.at[chain, src_x],
            device_id={"seq": 2 * to + core}, device_id_type=MESH,
        )

    def map_sends(chain, wait):
        for src_x in range(3):

            @pl.when(x == src_x)
            def _():
                for to in range(src_x + 1, 4):
                    copy = map_copy(chain, src_x, to)
                    if wait:
                        copy.wait_send()
                    else:
                        copy.start()

    arrived(0, kb.at[0])
    key_stage(0)
    arrived(1, kb.at[1])
    key_stage(1)
    arrived(2, vb.at[0])
    value_stage(0)
    maps_out[0] = maps[0].astype(BF16)
    map_sends(0, False)
    arrived(3, vb.at[1])
    value_stage(1)
    maps_out[1] = maps[1].astype(BF16)
    map_sends(1, False)

    def query_parts(chain, j):
        at = aligned(j * C, C)
        count_col = cols[j, :, 17 + 8 * chain:18 + 8 * chain]
        count_row = rows[j, 8 * chain + 1:8 * chain + 2, :]
        query = unit(qb[chain, at, :]) * (DK ** -0.5) * grow[chain, at, :]
        sh = shrink[chain, at, :]
        gram = lax.dot_general(
            left_of(halves(query)), jnp.concatenate([sh[:, :C], sh], axis=1),
            (((1,), (1,)), ((), ())), preferred_element_type=F32,
        )
        mix = jnp.where(lower & (count_col == count_row), gram, 0.0)
        live = query * (count_col < 0.5).astype(F32)
        return halves(jnp.concatenate([live, mix], axis=1))

    def query_stage(step, carry):
        for inner in range(4):
            j = step * 4 + inner
            leftb[aligned(j * C, C), :] = jnp.concatenate(query_parts(0, j), axis=1)
        return carry

    arrived(4, qb.at[0])
    lax.fori_loop(0, BLOCKS // 4, query_stage, 0)

    def incoming_state(chain):
        @pl.when(x == 0)
        def _():
            first[chain] = jnp.zeros((DK, DK), F32)

        for src_x in range(3):

            @pl.when(x > src_x)
            def _():
                map_copy(chain, src_x, src_x + 1).wait_recv()
                if src_x == 0:
                    first[chain] = gathered[0, chain, :, DK:].astype(F32)
                else:
                    move = gathered[src_x, chain, :, 0:DK]
                    first[chain] = gathered[src_x, chain, :, DK:].astype(F32) + dot(
                        jnp.concatenate([move, move], axis=1), stack(*halves(first[chain]))
                    )

    def moved(chain, at, incoming):
        mc = mcb[chain, at, :]
        return ocb[chain, at, :] + dot(jnp.concatenate([mc, mc[:, :C]], axis=1), incoming)

    def state_stage(chain):
        now = first[chain]
        for four in range(BLOCKS // 4):
            incoming = right_of(halves(now))
            states[chain, four] = incoming
            if four < BLOCKS // 4 - 1:
                now = moved(chain, pl.ds(four * 4 * C, C), incoming)

        def body(step, carry):
            todo = []
            for inner in range(8):
                j = step * 8 + inner
                at = aligned(j * C, C)
                incoming = states[chain, step * 2 + inner // 4]
                if inner % 4 == 0:
                    todo.append((j, at, incoming))
                else:
                    todo.append((j, at, right_of(halves(moved(chain, at, incoming)))))
            for j, at, incoming in todo:
                ws = wb[chain, at, :]
                fresh = ub[chain, at, :] - dot(jnp.concatenate([ws, ws[:, :C]], axis=1), incoming)
                fh, fl = halves(fresh)
                right[chain, j] = stack(incoming[C:2 * C], fh, incoming[2 * C:], fl)
            return carry

        lax.fori_loop(0, BLOCKS // 8, body, 0)

    def output_stage(chain):
        def body(step, own):
            p = lax.rem(step + blk // 8, BLOCKS // 4)
            for inner in range(4):
                j = 4 * p + inner
                at = aligned(j * C, C)
                if chain == 0:
                    ls = leftb[at, :]
                    left = jnp.concatenate([ls, ls[:, :2 * C]], axis=1)
                else:
                    left = left_of(query_parts(chain, j))
                hold = right[chain, j]
                out = dot(left, stack(hold[:2 * C], hold))
                core_buf[chain, at, :] = out.astype(BF16)
            for inner in range(8):
                b = 8 * p + lax.rem(blk + inner, 8)
                src = core_buf.at[chain, aligned(b * TOK, TOK), :]
                dst = back.at[chain, :, my_cols]
                if own and inner == 0:
                    pltpu.make_async_copy(src, dst, back_recv.at[chain]).start()
                else:
                    pltpu.make_async_remote_copy(
                        src, dst, back_send.at[chain], back_recv.at[chain],
                        device_id={"head": lax.rem(b, GROUPS), "seq": seq - core + b // GROUPS},
                        device_id_type=MESH,
                    ).start()

        body(0, True)

        def others(step, carry):
            body(step, False)
            return carry

        lax.fori_loop(1, BLOCKS // 4, others, 0)

    incoming_state(0)
    state_stage(0)
    output_stage(0)
    incoming_state(1)
    state_stage(1)
    arrived(5, qb.at[1])
    output_stage(1)

    for chain in range(2):
        pltpu.make_async_copy(back.at[chain], back.at[chain], back_recv.at[chain]).wait()

        def finish(step, carry, chain=chain):
            for inner in range(8):
                at = aligned((step * 8 + inner) * DK, DK)
                wide = back[chain, :, at].astype(F32)
                norm = lax.rsqrt(jnp.mean(wide * wide, axis=-1, keepdims=True) + NORM_EPS)
                out_ref[chain, :, at] = (wide * norm * scale[chain, :, at]).astype(BF16)
            return carry

        lax.fori_loop(0, H // 8, finish, 0)

    map_sends(0, True)
    map_sends(1, True)

    many = (OWNERS - 1) * DK
    for slot in range(6):
        sent = k_in.at[0, :, pl.ds(0, many)]
        pltpu.make_async_copy(sent, sent, send.at[slot]).wait()
    for chain in range(2):
        sent = back.at[0, :, pl.ds(0, many)]
        pltpu.make_async_copy(sent, sent, back_send.at[chain]).wait()
    for chain in range(2):
        lat_sent = lb.at[chain, pl.ds(0, (GROUPS - 1) * TOK), :]
        pltpu.make_async_copy(lat_sent, lat_sent, send.at[LAT + chain]).wait()
    aux_sent = aux_src.at[pl.ds(0, OWNERS - 1)]
    pltpu.make_async_copy(aux_sent, aux_sent, send.at[AUX]).wait()


def per_device(
    query_rows, key_rows, value_rows, beta_raw, gate_latent, gate_up, dt_bias, decay_log,
    boundary, modality, out_gate, norm_gain,
):
    span = lambda width, dtype: pltpu.VMEM((2, SPAN, width), dtype)
    return pl.pallas_call(
        kernel,
        out_shape=pltpu.VMEM((2, TOK, H * DK), BF16),
        in_specs=[ANY, ANY, ANY, ANY, ANY, ANY, ANY, ANY, ANY, SM, ANY, ANY],
        out_specs=VM,
        scratch_shapes=[
            pltpu.VMEM((2, H, TOK), BF16),
            pltpu.VMEM((2, TOK), jnp.int32),
            pltpu.VMEM((2, TOK), jnp.int32),
            pltpu.VMEM((1, H * DK), F32),
            span(DK, BF16), span(DK, BF16), span(DK, BF16), span(DK, BF16),
            pltpu.VMEM((OWNERS, 8, C), BF16),
            pltpu.VMEM((OWNERS, 8, C), BF16),
            pltpu.VMEM((DK, DK), BF16),
            pltpu.VMEM((2, DK), F32),
            pltpu.VMEM((2, TOK, H * DK), BF16),
            pltpu.VMEM((2, TOK, H * DK), F32),
            span(DK, F32),
            span(DK, F32),
            span(2 * DK, BF16),
            span(DK, F32),
            span(2 * DK, BF16),
            span(DK, BF16),
            span(2 * DK, BF16),
            span(DK, F32),
            span(2 * DK, BF16),
            span(DK, F32),
            pltpu.VMEM((2, BLOCKS, 4 * C, DK), BF16),
            pltpu.VMEM((BLOCKS, C, C), F32),
            pltpu.VMEM((BLOCKS, 16, C), F32),
            pltpu.VMEM((2, DK, 2 * DK), F32),
            pltpu.VMEM((2, DK, DK), F32),
            pltpu.VMEM((2, DK, 2 * DK), BF16),
            pltpu.VMEM((3, 2, DK, 2 * DK), BF16),
            pltpu.VMEM((2, BLOCKS // 4, 3 * C, DK), BF16),
            pltpu.VMEM((SPAN, 4 * C), BF16),
            span(DK, BF16),
            pltpu.VMEM((2, TOK, H * DK), BF16),
            pltpu.SemaphoreType.DMA((11,)),
            pltpu.SemaphoreType.DMA((11,)),
            pltpu.SemaphoreType.DMA((2, 3)),
            pltpu.SemaphoreType.DMA((2, 3)),
            pltpu.SemaphoreType.DMA((2,)),
            pltpu.SemaphoreType.DMA((2,)),
            pltpu.SemaphoreType.DMA((7,)),
        ],
        compiler_params=pltpu.CompilerParams(
            collective_id=0, has_side_effects=True, vmem_limit_bytes=60 * 1024 * 1024
        ),
        name="delta_attention",
    )(
        query_rows, key_rows, value_rows, beta_raw.transpose(0, 2, 1), boundary, modality, gate_latent, gate_up, dt_bias, decay_log,
        out_gate, norm_gain.reshape(1, -1),
    )


def solution(mesh):
    rows = P(None, ("seq", "head"), None)
    flat = P(None, ("seq", "head"))
    return jax.shard_map(
        per_device,
        mesh=mesh,
        in_specs=(rows, rows, rows, rows, rows, P(), P(), P(), flat, flat, rows, P()),
        out_specs=rows,
        check_vma=False,
    )
```

```python
import jax
import jax.numpy as jnp
from jax import lax
from jax.experimental import pallas as pl
from jax.experimental.pallas import tpu as pltpu
from jax.sharding import PartitionSpec as P

H = 32
DK = 128
TOK = 64
C = 128
SPAN = 2048
BLOCKS = SPAN // C
GROUPS = 16
OWNERS = 32
NORM_EPS = 1e-6
MESH = pl.DeviceIdType.MESH
F32 = jnp.float32
BF16 = jnp.bfloat16
ANY = pl.BlockSpec(memory_space=pl.ANY)
VM = pl.BlockSpec(memory_space=pltpu.VMEM)
SM = pl.BlockSpec(memory_space=pltpu.SMEM)
LAT, AUX, PASS = 6, 8, 9
KEY_STEP = 8


def halves(x):
    high = x.astype(BF16)
    return high, (x - high.astype(F32)).astype(BF16)


def left_of(pair):
    return jnp.concatenate([pair[0], pair[1], pair[0]], axis=1)


def right_of(pair):
    return jnp.concatenate([pair[0], pair[0], pair[1]], axis=0)


def dot(left, right):
    return jnp.dot(left, right, preferred_element_type=F32)


def fine(left, right):
    return dot(left_of(left), right_of(right))


def stack(*parts):
    return jnp.concatenate(parts, axis=0)


def softplus(x):
    u = jnp.exp(-jnp.abs(x))
    series = u * (1.0 - u * (0.5 - u * (1.0 / 3.0)))
    return jnp.maximum(x, 0.0) + jnp.where(u < 0.0078125, series, jnp.log(1.0 + u))


def unit(x):
    x = x.astype(F32)
    return x * lax.rsqrt(jnp.sum(x * x, axis=-1, keepdims=True) + NORM_EPS)


def aligned(start, size):
    return pl.ds(pl.multiple_of(start, size), size)


def kernel(
    q_in, k_in, v_in, beta_hbm, mark_hbm, kind_hbm, lat_in, up_in, bias_in, rate_in, gate_in,
    gain_hbm,
    out_ref,
    beta_in, mark_in, kind_in, gain_in, kb, vb, qb, lb, auxb, aux_src, upb, biasb, gateb, scale,
    total, grow, shrink, keyg, tail, xb, wb, ub, mcb, ocb, right, cols, rows,
    maps, first, maps_out, gathered, states, core_buf, back,
    send, recv, pre_send, pre_recv, back_send, back_recv, here,
):
    group = lax.axis_index("head")
    seq = lax.axis_index("seq")
    core = lax.rem(seq, 2)
    x = seq // 2
    me = group * 2 + core
    blk = core * GROUPS + group

    def owner_id(owner):
        return {"head": owner // 2, "seq": seq - core + lax.rem(owner, 2)}

    small = (
        pltpu.make_async_copy(beta_hbm, beta_in, here.at[3]),
        pltpu.make_async_copy(mark_hbm, mark_in, here.at[4]),
        pltpu.make_async_copy(kind_hbm, kind_in, here.at[5]),
        pltpu.make_async_copy(gain_hbm, gain_in, here.at[6]),
    )
    for copy in small:
        copy.start()

    barrier = pltpu.get_barrier_semaphore()

    def greet(step, carry):
        pl.semaphore_signal(
            barrier, inc=1, device_id=owner_id(lax.rem(me + 21 * step, OWNERS)), device_id_type=MESH
        )
        return carry

    lax.fori_loop(1, OWNERS, greet, 0)
    for away in (1, 2, 3):
        pl.semaphore_signal(
            barrier, inc=1, device_id={"seq": lax.rem(seq + 2 * away, 8)}, device_id_type=MESH
        )

    my_cols = aligned(me * DK, DK)
    my_rows = aligned(blk * TOK, TOK)
    local = (
        pltpu.make_async_copy(up_in.at[:, my_cols], upb, here.at[0]),
        pltpu.make_async_copy(bias_in.at[:, my_cols], biasb, here.at[1]),
        pltpu.make_async_copy(gate_in, gateb, here.at[2]),
    )
    for copy in local:
        copy.start()

    pl.semaphore_wait(barrier, OWNERS + 2)

    def lat_spread(chain):
        def one(step, carry):
            pltpu.make_async_remote_copy(
                lat_in.at[chain], lb.at[chain, my_rows, :], send.at[LAT + chain],
                recv.at[LAT + chain],
                device_id={"head": lax.rem(group + 5 * step, GROUPS), "seq": seq},
                device_id_type=MESH,
            ).start()
            return carry

        lax.fori_loop(1, GROUPS, one, 0)
        pltpu.make_async_copy(
            lat_in.at[chain], lb.at[chain, my_rows, :], recv.at[LAT + chain]
        ).start()

    lat_spread(0)

    ri = lax.broadcasted_iota(jnp.int32, (C, C), 0)
    ci = lax.broadcasted_iota(jnp.int32, (C, C), 1)
    si = lax.broadcasted_iota(jnp.int32, (8 * OWNERS, H), 0)
    sj = lax.broadcasted_iota(jnp.int32, (8 * OWNERS, H), 1)
    select = ((si % 8 == 0) & (si // 8 == sj)).astype(BF16)
    part = lax.broadcasted_iota(jnp.int32, (8 * OWNERS, TOK), 0) % 8
    ti = lax.broadcasted_iota(jnp.int32, (TOK, C), 0)
    tj = lax.broadcasted_iota(jnp.int32, (TOK, C), 1)
    packed = jnp.zeros((8 * OWNERS, C), F32)
    for copy in small:
        copy.wait()
    for b in range(2):
        tiny = dot(select, beta_in[b])
        tiny = jnp.where(part == 1, mark_in[b:b + 1, :].astype(F32), tiny)
        tiny = jnp.where(part == 2, kind_in[b:b + 1, :].astype(F32), tiny)
        packed = packed + dot(tiny.astype(BF16), (tj == ti + b * TOK).astype(BF16))
    aux_src[...] = packed.reshape(OWNERS, 8, C).astype(BF16)

    def aux_send(step, carry):
        other = lax.rem(me + step, OWNERS)
        pltpu.make_async_remote_copy(
            aux_src.at[other], auxb.at[blk], send.at[AUX], recv.at[AUX],
            device_id=owner_id(other), device_id_type=MESH,
        ).start()
        return carry

    lax.fori_loop(1, OWNERS, aux_send, 0)
    pltpu.make_async_copy(aux_src.at[me], auxb.at[blk], recv.at[AUX]).start()
    lat_spread(1)

    def spread(slot, src, dst, chain):
        def one(step, carry):
            other = lax.rem(me + 5 * step, OWNERS)
            pltpu.make_async_remote_copy(
                src.at[chain, :, aligned(other * DK, DK)], dst.at[chain, my_rows, :],
                send.at[slot], recv.at[slot], device_id=owner_id(other), device_id_type=MESH,
            ).start()
            return carry

        lax.fori_loop(1, OWNERS, one, 0)
        pltpu.make_async_copy(
            src.at[chain, :, my_cols], dst.at[chain, my_rows, :], recv.at[slot]
        ).start()

    def arrived(slot, dst):
        pltpu.make_async_copy(dst, dst, recv.at[slot]).wait()

    spread(0, k_in, kb, 0)

    local[2].wait()

    def gates(step, carry):
        for inner in range(4):
            at = aligned((step * 4 + inner) * DK, DK)
            for chain in range(2):
                scale[chain, :, at] = gain_in[0:1, at] * jax.nn.sigmoid(
                    gateb[chain, :, at].astype(F32)
                )
        return carry

    lax.fori_loop(0, H // 4, gates, 0)

    pass_on = []
    for chain in range(2):
        half = lb.at[chain, aligned(core * (SPAN // 2), SPAN // 2), :]
        arrived(LAT + chain, half)
        pass_on.append(
            pltpu.make_async_remote_copy(
                half, half, send.at[PASS + chain], recv.at[PASS + chain],
                device_id={"seq": seq + 1 - 2 * core}, device_id_type=MESH,
            )
        )
        pass_on[chain].start()
    spread(1, k_in, kb, 1)
    spread(2, v_in, vb, 0)
    spread(3, v_in, vb, 1)
    spread(4, q_in, qb, 0)
    spread(5, q_in, qb, 1)

    eye = ri == ci
    strict = ri > ci
    lower = ri >= ci
    tri = lower.astype(BF16)
    tri2 = jnp.concatenate([tri, tri], axis=1)
    upper = (ri <= ci).astype(BF16)
    lane = lax.broadcasted_iota(jnp.int32, (8, C), 1)
    local[0].wait()
    local[1].wait()
    arrived(AUX, auxb)

    rate = -jnp.exp(jnp.full((1, DK), rate_in[me], F32))

    def small_rows(step, carry):
        for inner in range(4):
            j = step * 4 + inner
            one = auxb[2 * j].astype(F32)
            two = auxb[2 * j + 1].astype(F32)
            mine = stack(
                jnp.where(lane < TOK, one, pltpu.roll(two, TOK, 1)),
                jnp.where(lane < TOK, pltpu.roll(one, TOK, 1), two),
            )
            counts = dot(mine.astype(BF16), upper)
            cols[j] = stack(jax.nn.sigmoid(mine), counts, mine, jnp.zeros((C - 48, C), F32)).T
            rows[j] = counts
        return carry

    def decay_stage(chain, half_core):
        for inner in range(BLOCKS // 2):
            j = half_core * (BLOCKS // 2) + inner
            at = aligned(j * C, C)
            kind = cols[j, :, 34 + 8 * chain:35 + 8 * chain]
            pre = dot(lb[chain, at, :], upb[...]).astype(BF16).astype(F32)
            bias = jnp.where(kind > 0.5, biasb[1:2, :], biasb[0:1, :])
            dh, dl = halves(rate * softplus(pre + bias))
            total[chain, at, :] = dot(tri2, stack(dh, dl))

    lax.fori_loop(0, BLOCKS // 4, small_rows, 0)
    for chain in range(2):
        decay_stage(chain, core)
        pass_on[chain].wait()
        decay_stage(chain, 1 - core)

    near = ((ri // 16) == (ci // 16)).astype(BF16)
    eye_wide = eye.astype(F32)
    eye_low = eye.astype(BF16)
    parts = []
    for width in (16, 32, 64):
        same_pair = (ri // (2 * width)) == (ci // (2 * width))
        parts.append((same_pair & ((ri // width) != (ci // width))).astype(BF16))

    def key_stage(chain):
        def body(step, carry):
            todo = []
            for inner in range(KEY_STEP):
                j = step * KEY_STEP + inner
                at = aligned(j * C, C)
                beta = cols[j, :, 8 * chain:8 * chain + 1]
                count_col = cols[j, :, 17 + 8 * chain:18 + 8 * chain]
                count_row = rows[j, 8 * chain + 1:8 * chain + 2, :]
                count_last = count_row[:, C - 1:C]
                sums = total[chain, at, :]
                last = sums[C - 1:C, :]
                growth = jnp.exp(sums)
                grow[chain, at, :] = growth
                key = unit(kb[chain, at, :])
                key_grow = key * growth
                alive = (count_col < 0.5).astype(F32)
                keyg[chain, at, :] = key_grow * (alive * beta)
                shrunk = halves(key * jnp.exp(-sums))
                shrink[chain, at, :] = jnp.concatenate(shrunk, axis=1)
                mask = (count_col == count_last).astype(F32)
                moved_t = halves((key * jnp.exp(last - sums) * mask).T)
                tail[chain, at, :] = jnp.concatenate(moved_t, axis=1)
                gram = lax.dot_general(
                    key_grow.astype(BF16), shrunk[0],
                    (((1,), (1,)), ((), ())), preferred_element_type=F32,
                )
                low = jnp.where(strict & (count_col == count_row), gram, 0.0) * beta
                low = low.astype(BF16)
                todo.append(dict(at=at, low=low, d=low * near))
            for t in todo:
                t["d2"] = dot(t["d"], t["d"]).astype(BF16)
            for t in todo:
                start = eye_low - t["d"]
                both = dot(stack(start, t["d2"]), t["d2"])
                t["t"] = start.astype(F32) + both[:C]
                t["d4"] = both[C:].astype(BF16)
            for t in todo:
                both = dot(stack(t["t"].astype(BF16), t["d4"]), t["d4"])
                t["t"] = t["t"] + both[:C]
                t["d8"] = both[C:].astype(BF16)
            for t in todo:
                t["t"] = t["t"] + dot(t["t"].astype(BF16), t["d8"])
            for part in parts:
                for t in todo:
                    t["tb"] = t["t"].astype(BF16)
                    t["y"] = dot(t["low"] * part, t["tb"]).astype(BF16)
                for t in todo:
                    t["t"] = t["t"] - dot(t["tb"], t["y"])
            for t in todo:
                xb[chain, t["at"], :] = (t["t"] - eye_wide).astype(BF16)
            return carry

        lax.fori_loop(0, BLOCKS // KEY_STEP, body, 0)

    def value_stage(chain):
        maps[chain, :, 0:DK] = eye.astype(F32)
        maps[chain, :, DK:] = jnp.zeros((DK, DK), F32)

        def body(step, carry):
            todo = []
            for inner in range(8):
                j = step * 8 + inner
                at = aligned(j * C, C)
                beta = cols[j, :, 8 * chain:8 * chain + 1]
                count_last = rows[j, 8 * chain + 1:8 * chain + 2, C - 1:C]
                rhs = jnp.concatenate(
                    [keyg[chain, at, :], vb[chain, at, :].astype(F32) * beta], axis=1
                )
                wu = rhs + dot(xb[chain, at, :], rhs.astype(BF16))
                pair = halves(wu)
                wb[chain, at, :] = jnp.concatenate([pair[0][:, :C], pair[1][:, :C]], axis=1)
                ub[chain, at, :] = wu[:, C:]
                ts = tail[chain, at, :]
                both = dot(jnp.concatenate([ts, ts[:, :C]], axis=1), right_of(pair))
                carry_row = jnp.exp(total[chain, at, :][C - 1:C, :]) * (count_last < 0.5).astype(F32)
                move = jnp.where(eye, carry_row, 0.0) - both[:, :C]
                todo.append((at, move, both[:, C:]))

            def chained(move, offset, pair):
                both = fine(move, pair)
                return jnp.concatenate([both[:, :C], both[:, C:] + offset], axis=1)

            def keep(at, pair, offset):
                mcb[chain, at, :] = jnp.concatenate([pair[0][:, :C], pair[1][:, :C]], axis=1)
                ocb[chain, at, :] = offset

            past = []
            for four_of in (todo[:4], todo[4:]):
                one = halves(jnp.concatenate(four_of[0][1:], axis=1))
                two = chained(halves(four_of[1][1]), four_of[1][2], one)
                rest = chained(
                    halves(four_of[3][1]), four_of[3][2], halves(jnp.concatenate(four_of[2][1:], axis=1))
                )
                two_s = halves(two)
                three = chained(halves(four_of[2][1]), four_of[2][2], two_s)
                four = chained(halves(rest[:, :C]), rest[:, C:], two_s)
                four_m = halves(four[:, :C])
                keep(four_of[1][0], one, four_of[0][2])
                keep(four_of[2][0], two_s, two[:, C:])
                keep(four_of[3][0], halves(three[:, :C]), three[:, C:])
                keep(four_of[0][0], four_m, four[:, C:])
                past.append((four_m, four[:, C:]))
            held = maps[chain]
            for move, offset in past:
                held = chained(move, offset, halves(held))
            maps[chain] = held
            return carry

        lax.fori_loop(0, BLOCKS // 8, body, 0)

    def map_copy(chain, src_x, to):
        cut = pl.ds(DK, DK) if src_x == 0 else pl.ds(0, 2 * DK)
        return pltpu.make_async_remote_copy(
            maps_out.at[chain, :, cut], gathered.at[src_x, chain, :, cut],
            pre_send.at[chain, to - 1], pre_recv.at[chain, src_x],
            device_id={"seq": 2 * to + core}, device_id_type=MESH,
        )

    def map_sends(chain, wait):
        for src_x in range(3):

            @pl.when(x == src_x)
            def _():
                for to in range(src_x + 1, 4):
                    copy = map_copy(chain, src_x, to)
                    if wait:
                        copy.wait_send()
                    else:
                        copy.start()

    arrived(0, kb.at[0])
    key_stage(0)
    arrived(1, kb.at[1])
    key_stage(1)
    arrived(2, vb.at[0])
    value_stage(0)
    maps_out[0] = maps[0].astype(BF16)
    map_sends(0, False)
    arrived(3, vb.at[1])
    value_stage(1)
    maps_out[1] = maps[1].astype(BF16)
    map_sends(1, False)

    def query_parts(chain, j):
        at = aligned(j * C, C)
        count_col = cols[j, :, 17 + 8 * chain:18 + 8 * chain]
        count_row = rows[j, 8 * chain + 1:8 * chain + 2, :]
        query = unit(qb[chain, at, :]) * (DK ** -0.5) * grow[chain, at, :]
        sh = shrink[chain, at, :]
        gram = lax.dot_general(
            left_of(halves(query)), jnp.concatenate([sh[:, :C], sh], axis=1),
            (((1,), (1,)), ((), ())), preferred_element_type=F32,
        )
        mix = jnp.where(lower & (count_col == count_row), gram, 0.0)
        live = query * (count_col < 0.5).astype(F32)
        return halves(jnp.concatenate([live, mix], axis=1))

    def incoming_state(chain):
        @pl.when(x == 0)
        def _():
            first[chain] = jnp.zeros((DK, DK), F32)

        for src_x in range(3):

            @pl.when(x > src_x)
            def _():
                map_copy(chain, src_x, src_x + 1).wait_recv()
                if src_x == 0:
                    first[chain] = gathered[0, chain, :, DK:].astype(F32)
                else:
                    move = gathered[src_x, chain, :, 0:DK]
                    first[chain] = gathered[src_x, chain, :, DK:].astype(F32) + dot(
                        jnp.concatenate([move, move], axis=1), stack(*halves(first[chain]))
                    )

    def moved(chain, at, incoming):
        mc = mcb[chain, at, :]
        return ocb[chain, at, :] + dot(jnp.concatenate([mc, mc[:, :C]], axis=1), incoming)

    def state_stage(chain):
        now = first[chain]
        for four in range(BLOCKS // 4):
            incoming = right_of(halves(now))
            states[chain, four] = incoming
            if four < BLOCKS // 4 - 1:
                now = moved(chain, pl.ds(four * 4 * C, C), incoming)

        def body(step, carry):
            todo = []
            for inner in range(8):
                j = step * 8 + inner
                at = aligned(j * C, C)
                incoming = states[chain, step * 2 + inner // 4]
                if inner % 4 == 0:
                    todo.append((j, at, incoming))
                else:
                    todo.append((j, at, right_of(halves(moved(chain, at, incoming)))))
            for j, at, incoming in todo:
                ws = wb[chain, at, :]
                fresh = ub[chain, at, :] - dot(jnp.concatenate([ws, ws[:, :C]], axis=1), incoming)
                fh, fl = halves(fresh)
                right[chain, j] = stack(incoming[C:2 * C], fh, incoming[2 * C:], fl)
            return carry

        lax.fori_loop(0, BLOCKS // 8, body, 0)

    def output_stage(chain):
        def body(step, own):
            p = lax.rem(step + blk // 8, BLOCKS // 4)
            for inner in range(4):
                j = 4 * p + inner
                at = aligned(j * C, C)
                hold = right[chain, j]
                out = dot(left_of(query_parts(chain, j)), stack(hold[:2 * C], hold))
                core_buf[chain, at, :] = out.astype(BF16)
            for inner in range(8):
                b = 8 * p + lax.rem(blk + inner, 8)
                src = core_buf.at[chain, aligned(b * TOK, TOK), :]
                dst = back.at[chain, :, my_cols]
                if own and inner == 0:
                    pltpu.make_async_copy(src, dst, back_recv.at[chain, 0]).start()
                else:
                    pltpu.make_async_remote_copy(
                        src, dst, back_send.at[chain], back_recv.at[chain, step],
                        device_id={"head": lax.rem(b, GROUPS), "seq": seq - core + b // GROUPS},
                        device_id_type=MESH,
                    ).start()

        body(0, True)

        def others(step, carry):
            body(step, False)
            return carry

        lax.fori_loop(1, BLOCKS // 4, others, 0)

    incoming_state(0)
    state_stage(0)
    arrived(4, qb.at[0])
    output_stage(0)
    incoming_state(1)
    state_stage(1)
    arrived(5, qb.at[1])
    output_stage(1)

    for chain in range(2):

        def finish(step, carry, chain=chain):
            some = back.at[chain, :, pl.ds(0, 8 * DK)]
            pltpu.make_async_copy(some, some, back_recv.at[chain, step]).wait()
            q = lax.rem(blk // 8 + 4 - step, 4)
            base = lax.rem(q, 2) * 16 + q // 2
            for inner in range(8):
                at = aligned((base + 2 * inner) * DK, DK)
                wide = back[chain, :, at].astype(F32)
                norm = lax.rsqrt(jnp.mean(wide * wide, axis=-1, keepdims=True) + NORM_EPS)
                out_ref[chain, :, at] = (wide * norm * scale[chain, :, at]).astype(BF16)
            return carry

        lax.fori_loop(0, 4, finish, 0)

    map_sends(0, True)
    map_sends(1, True)

    many = (OWNERS - 1) * DK
    for slot in range(6):
        sent = k_in.at[0, :, pl.ds(0, many)]
        pltpu.make_async_copy(sent, sent, send.at[slot]).wait()
    for chain in range(2):
        sent = back.at[0, :, pl.ds(0, many)]
        pltpu.make_async_copy(sent, sent, back_send.at[chain]).wait()
    for chain in range(2):
        lat_sent = lb.at[chain, pl.ds(0, (GROUPS - 1) * TOK), :]
        pltpu.make_async_copy(lat_sent, lat_sent, send.at[LAT + chain]).wait()
    aux_sent = aux_src.at[pl.ds(0, OWNERS - 1)]
    pltpu.make_async_copy(aux_sent, aux_sent, send.at[AUX]).wait()


def per_device(
    query_rows, key_rows, value_rows, beta_raw, gate_latent, gate_up, dt_bias, decay_log,
    boundary, modality, out_gate, norm_gain,
):
    span = lambda width, dtype: pltpu.VMEM((2, SPAN, width), dtype)
    return pl.pallas_call(
        kernel,
        out_shape=pltpu.VMEM((2, TOK, H * DK), BF16),
        in_specs=[ANY, ANY, ANY, ANY, ANY, ANY, ANY, ANY, ANY, SM, ANY, ANY],
        out_specs=VM,
        scratch_shapes=[
            pltpu.VMEM((2, H, TOK), BF16),
            pltpu.VMEM((2, TOK), jnp.int32),
            pltpu.VMEM((2, TOK), jnp.int32),
            pltpu.VMEM((1, H * DK), F32),
            span(DK, BF16), span(DK, BF16), span(DK, BF16), span(DK, BF16),
            pltpu.VMEM((OWNERS, 8, C), BF16),
            pltpu.VMEM((OWNERS, 8, C), BF16),
            pltpu.VMEM((DK, DK), BF16),
            pltpu.VMEM((2, DK), F32),
            pltpu.VMEM((2, TOK, H * DK), BF16),
            pltpu.VMEM((2, TOK, H * DK), F32),
            span(DK, F32),
            span(DK, F32),
            span(2 * DK, BF16),
            span(DK, F32),
            span(2 * DK, BF16),
            span(DK, BF16),
            span(2 * DK, BF16),
            span(DK, F32),
            span(2 * DK, BF16),
            span(DK, F32),
            pltpu.VMEM((2, BLOCKS, 4 * C, DK), BF16),
            pltpu.VMEM((BLOCKS, C, C), F32),
            pltpu.VMEM((BLOCKS, 16, C), F32),
            pltpu.VMEM((2, DK, 2 * DK), F32),
            pltpu.VMEM((2, DK, DK), F32),
            pltpu.VMEM((2, DK, 2 * DK), BF16),
            pltpu.VMEM((3, 2, DK, 2 * DK), BF16),
            pltpu.VMEM((2, BLOCKS // 4, 3 * C, DK), BF16),
            span(DK, BF16),
            pltpu.VMEM((2, TOK, H * DK), BF16),
            pltpu.SemaphoreType.DMA((11,)),
            pltpu.SemaphoreType.DMA((11,)),
            pltpu.SemaphoreType.DMA((2, 3)),
            pltpu.SemaphoreType.DMA((2, 3)),
            pltpu.SemaphoreType.DMA((2,)),
            pltpu.SemaphoreType.DMA((2, 4)),
            pltpu.SemaphoreType.DMA((7,)),
        ],
        compiler_params=pltpu.CompilerParams(
            collective_id=0, has_side_effects=True, vmem_limit_bytes=60 * 1024 * 1024
        ),
        name="delta_attention",
    )(
        query_rows, key_rows, value_rows, beta_raw.transpose(0, 2, 1), boundary, modality, gate_latent, gate_up, dt_bias, decay_log,
        out_gate, norm_gain.reshape(1, -1),
    )


def solution(mesh):
    rows = P(None, ("seq", "head"), None)
    flat = P(None, ("seq", "head"))
    return jax.shard_map(
        per_device,
        mesh=mesh,
        in_specs=(rows, rows, rows, rows, rows, P(), P(), P(), flat, flat, rows, P()),
        out_specs=rows,
        check_vma=False,
    )
```

```python
import jax
import jax.numpy as jnp
from jax import lax
from jax.experimental import pallas as pl
from jax.experimental.pallas import tpu as pltpu
from jax.sharding import PartitionSpec as P

H = 32
DK = 128
TOK = 64
C = 128
SPAN = 2048
BLOCKS = SPAN // C
GROUPS = 16
OWNERS = 32
NORM_EPS = 1e-6
MESH = pl.DeviceIdType.MESH
F32 = jnp.float32
BF16 = jnp.bfloat16
ANY = pl.BlockSpec(memory_space=pl.ANY)
VM = pl.BlockSpec(memory_space=pltpu.VMEM)
SM = pl.BlockSpec(memory_space=pltpu.SMEM)
LAT, AUX, PASS = 6, 8, 9
KEY_STEP = 8


def halves(x):
    high = x.astype(BF16)
    return high, (x - high.astype(F32)).astype(BF16)


def left_of(pair):
    return jnp.concatenate([pair[0], pair[1], pair[0]], axis=1)


def right_of(pair):
    return jnp.concatenate([pair[0], pair[0], pair[1]], axis=0)


def dot(left, right):
    return jnp.dot(left, right, preferred_element_type=F32)


def fine(left, right):
    return dot(left_of(left), right_of(right))


def stack(*parts):
    return jnp.concatenate(parts, axis=0)


def softplus(x):
    u = jnp.exp(-jnp.abs(x))
    series = u * (1.0 - u * (0.5 - u * (1.0 / 3.0)))
    return jnp.maximum(x, 0.0) + jnp.where(u < 0.0078125, series, jnp.log(1.0 + u))


def unit(x):
    x = x.astype(F32)
    return x * lax.rsqrt(jnp.sum(x * x, axis=-1, keepdims=True) + NORM_EPS)


def aligned(start, size):
    return pl.ds(pl.multiple_of(start, size), size)


def kernel(
    q_in, k_in, v_in, beta_hbm, mark_hbm, kind_hbm, lat_in, up_in, bias_in, rate_in, gate_in,
    gain_hbm,
    out_ref,
    beta_in, mark_in, kind_in, gain_in, kb, vb, qb, lb, auxb, aux_src, upb, biasb, gateb, scale,
    total, grow, shrink, keyg, tail, xb, wb, ub, mcb, ocb, right, cols, rows,
    maps, first, maps_out, gathered, states, core_buf, back,
    send, recv, pre_send, pre_recv, back_send, back_recv, here,
):
    group = lax.axis_index("head")
    seq = lax.axis_index("seq")
    core = lax.rem(seq, 2)
    x = seq // 2
    me = group * 2 + core
    blk = core * GROUPS + group

    def owner_id(owner):
        return {"head": owner // 2, "seq": seq - core + lax.rem(owner, 2)}

    small = (
        pltpu.make_async_copy(beta_hbm, beta_in, here.at[3]),
        pltpu.make_async_copy(mark_hbm, mark_in, here.at[4]),
        pltpu.make_async_copy(kind_hbm, kind_in, here.at[5]),
        pltpu.make_async_copy(gain_hbm, gain_in, here.at[6]),
    )
    for copy in small:
        copy.start()

    barrier = pltpu.get_barrier_semaphore()

    def greet(step, carry):
        pl.semaphore_signal(
            barrier, inc=1, device_id=owner_id(lax.rem(me + 21 * step, OWNERS)), device_id_type=MESH
        )
        return carry

    lax.fori_loop(1, OWNERS, greet, 0)
    for away in (1, 2, 3):
        pl.semaphore_signal(
            barrier, inc=1, device_id={"seq": lax.rem(seq + 2 * away, 8)}, device_id_type=MESH
        )

    my_cols = aligned(me * DK, DK)
    my_rows = aligned(blk * TOK, TOK)
    local = (
        pltpu.make_async_copy(up_in.at[:, my_cols], upb, here.at[0]),
        pltpu.make_async_copy(bias_in.at[:, my_cols], biasb, here.at[1]),
        pltpu.make_async_copy(gate_in, gateb, here.at[2]),
    )
    for copy in local:
        copy.start()

    pl.semaphore_wait(barrier, OWNERS + 2)

    def lat_spread(chain):
        def one(step, carry):
            pltpu.make_async_remote_copy(
                lat_in.at[chain], lb.at[chain, my_rows, :], send.at[LAT + chain],
                recv.at[LAT + chain],
                device_id={"head": lax.rem(group + 5 * step, GROUPS), "seq": seq},
                device_id_type=MESH,
            ).start()
            return carry

        lax.fori_loop(1, GROUPS, one, 0)
        pltpu.make_async_copy(
            lat_in.at[chain], lb.at[chain, my_rows, :], recv.at[LAT + chain]
        ).start()

    lat_spread(0)

    ri = lax.broadcasted_iota(jnp.int32, (C, C), 0)
    ci = lax.broadcasted_iota(jnp.int32, (C, C), 1)
    si = lax.broadcasted_iota(jnp.int32, (8 * OWNERS, H), 0)
    sj = lax.broadcasted_iota(jnp.int32, (8 * OWNERS, H), 1)
    select = ((si % 8 == 0) & (si // 8 == sj)).astype(BF16)
    part = lax.broadcasted_iota(jnp.int32, (8 * OWNERS, TOK), 0) % 8
    ti = lax.broadcasted_iota(jnp.int32, (TOK, C), 0)
    tj = lax.broadcasted_iota(jnp.int32, (TOK, C), 1)
    packed = jnp.zeros((8 * OWNERS, C), F32)
    for copy in small:
        copy.wait()
    for b in range(2):
        tiny = dot(select, beta_in[b])
        tiny = jnp.where(part == 1, mark_in[b:b + 1, :].astype(F32), tiny)
        tiny = jnp.where(part == 2, kind_in[b:b + 1, :].astype(F32), tiny)
        packed = packed + dot(tiny.astype(BF16), (tj == ti + b * TOK).astype(BF16))
    aux_src[...] = packed.reshape(OWNERS, 8, C).astype(BF16)

    def aux_send(step, carry):
        other = lax.rem(me + step, OWNERS)
        pltpu.make_async_remote_copy(
            aux_src.at[other], auxb.at[blk], send.at[AUX], recv.at[AUX],
            device_id=owner_id(other), device_id_type=MESH,
        ).start()
        return carry

    lax.fori_loop(1, OWNERS, aux_send, 0)
    pltpu.make_async_copy(aux_src.at[me], auxb.at[blk], recv.at[AUX]).start()
    lat_spread(1)

    def spread(slot, src, dst, chain):
        def one(step, carry):
            other = lax.rem(me + 5 * step, OWNERS)
            pltpu.make_async_remote_copy(
                src.at[chain, :, aligned(other * DK, DK)], dst.at[chain, my_rows, :],
                send.at[slot], recv.at[slot], device_id=owner_id(other), device_id_type=MESH,
            ).start()
            return carry

        lax.fori_loop(1, OWNERS, one, 0)
        pltpu.make_async_copy(
            src.at[chain, :, my_cols], dst.at[chain, my_rows, :], recv.at[slot]
        ).start()

    def arrived(slot, dst):
        pltpu.make_async_copy(dst, dst, recv.at[slot]).wait()

    spread(0, k_in, kb, 0)

    local[2].wait()

    def gates(step, carry):
        for inner in range(4):
            at = aligned((step * 4 + inner) * DK, DK)
            for chain in range(2):
                scale[chain, :, at] = gain_in[0:1, at] * jax.nn.sigmoid(
                    gateb[chain, :, at].astype(F32)
                )
        return carry

    lax.fori_loop(0, H // 4, gates, 0)

    pass_on = []
    for chain in range(2):
        half = lb.at[chain, aligned(core * (SPAN // 2), SPAN // 2), :]
        arrived(LAT + chain, half)
        pass_on.append(
            pltpu.make_async_remote_copy(
                half, half, send.at[PASS + chain], recv.at[PASS + chain],
                device_id={"seq": seq + 1 - 2 * core}, device_id_type=MESH,
            )
        )
        pass_on[chain].start()
        if chain == 0:
            spread(1, k_in, kb, 1)
    spread(2, v_in, vb, 0)
    spread(3, v_in, vb, 1)
    spread(4, q_in, qb, 0)
    spread(5, q_in, qb, 1)

    eye = ri == ci
    strict = ri > ci
    lower = ri >= ci
    tri = lower.astype(BF16)
    tri2 = jnp.concatenate([tri, tri], axis=1)
    upper = (ri <= ci).astype(BF16)
    lane = lax.broadcasted_iota(jnp.int32, (8, C), 1)
    local[0].wait()
    local[1].wait()
    arrived(AUX, auxb)

    rate = -jnp.exp(jnp.full((1, DK), rate_in[me], F32))

    def small_rows(step, carry):
        for inner in range(4):
            j = step * 4 + inner
            one = auxb[2 * j].astype(F32)
            two = auxb[2 * j + 1].astype(F32)
            mine = stack(
                jnp.where(lane < TOK, one, pltpu.roll(two, TOK, 1)),
                jnp.where(lane < TOK, pltpu.roll(one, TOK, 1), two),
            )
            counts = dot(mine.astype(BF16), upper)
            cols[j] = stack(jax.nn.sigmoid(mine), counts, mine, jnp.zeros((C - 48, C), F32)).T
            rows[j] = counts
        return carry

    def decay_stage(chain, half_core):
        for inner in range(BLOCKS // 2):
            j = half_core * (BLOCKS // 2) + inner
            at = aligned(j * C, C)
            kind = cols[j, :, 34 + 8 * chain:35 + 8 * chain]
            pre = dot(lb[chain, at, :], upb[...]).astype(BF16).astype(F32)
            bias = jnp.where(kind > 0.5, biasb[1:2, :], biasb[0:1, :])
            dh, dl = halves(rate * softplus(pre + bias))
            total[chain, at, :] = dot(tri2, stack(dh, dl))

    lax.fori_loop(0, BLOCKS // 4, small_rows, 0)
    for chain in range(2):
        decay_stage(chain, core)
        pass_on[chain].wait()
        decay_stage(chain, 1 - core)

    near = ((ri // 16) == (ci // 16)).astype(BF16)
    eye_wide = eye.astype(F32)
    eye_low = eye.astype(BF16)
    parts = []
    for width in (16, 32, 64):
        same_pair = (ri // (2 * width)) == (ci // (2 * width))
        parts.append((same_pair & ((ri // width) != (ci // width))).astype(BF16))

    def key_stage(chain):
        def body(step, carry):
            todo = []
            for inner in range(KEY_STEP):
                j = step * KEY_STEP + inner
                at = aligned(j * C, C)
                beta = cols[j, :, 8 * chain:8 * chain + 1]
                count_col = cols[j, :, 17 + 8 * chain:18 + 8 * chain]
                count_row = rows[j, 8 * chain + 1:8 * chain + 2, :]
                count_last = count_row[:, C - 1:C]
                sums = total[chain, at, :]
                last = sums[C - 1:C, :]
                growth = jnp.exp(sums)
                grow[chain, at, :] = growth
                key = unit(kb[chain, at, :])
                key_grow = key * growth
                alive = (count_col < 0.5).astype(F32)
                keyg[chain, at, :] = key_grow * (alive * beta)
                shrunk = halves(key * jnp.exp(-sums))
                shrink[chain, at, :] = jnp.concatenate(shrunk, axis=1)
                mask = (count_col == count_last).astype(F32)
                moved_t = halves((key * jnp.exp(last - sums) * mask).T)
                tail[chain, at, :] = jnp.concatenate(moved_t, axis=1)
                gram = lax.dot_general(
                    key_grow.astype(BF16), shrunk[0],
                    (((1,), (1,)), ((), ())), preferred_element_type=F32,
                )
                low = jnp.where(strict & (count_col == count_row), gram, 0.0) * beta
                low = low.astype(BF16)
                todo.append(dict(at=at, low=low, d=low * near))
            for t in todo:
                t["d2"] = dot(t["d"], t["d"]).astype(BF16)
            for t in todo:
                start = eye_low - t["d"]
                both = dot(stack(start, t["d2"]), t["d2"])
                t["t"] = start.astype(F32) + both[:C]
                t["d4"] = both[C:].astype(BF16)
            for t in todo:
                both = dot(stack(t["t"].astype(BF16), t["d4"]), t["d4"])
                t["t"] = t["t"] + both[:C]
                t["d8"] = both[C:].astype(BF16)
            for t in todo:
                t["t"] = t["t"] + dot(t["t"].astype(BF16), t["d8"])
            for part in parts:
                for t in todo:
                    t["tb"] = t["t"].astype(BF16)
                    t["y"] = dot(t["low"] * part, t["tb"]).astype(BF16)
                for t in todo:
                    t["t"] = t["t"] - dot(t["tb"], t["y"])
            for t in todo:
                xb[chain, t["at"], :] = (t["t"] - eye_wide).astype(BF16)
            return carry

        lax.fori_loop(0, BLOCKS // KEY_STEP, body, 0)

    def value_stage(chain):
        maps[chain, :, 0:DK] = eye.astype(F32)
        maps[chain, :, DK:] = jnp.zeros((DK, DK), F32)

        def body(step, carry):
            todo = []
            for inner in range(8):
                j = step * 8 + inner
                at = aligned(j * C, C)
                beta = cols[j, :, 8 * chain:8 * chain + 1]
                count_last = rows[j, 8 * chain + 1:8 * chain + 2, C - 1:C]
                rhs = jnp.concatenate(
                    [keyg[chain, at, :], vb[chain, at, :].astype(F32) * beta], axis=1
                )
                wu = rhs + dot(xb[chain, at, :], rhs.astype(BF16))
                pair = halves(wu)
                wb[chain, at, :] = jnp.concatenate([pair[0][:, :C], pair[1][:, :C]], axis=1)
                ub[chain, at, :] = wu[:, C:]
                ts = tail[chain, at, :]
                both = dot(jnp.concatenate([ts, ts[:, :C]], axis=1), right_of(pair))
                carry_row = jnp.exp(total[chain, at, :][C - 1:C, :]) * (count_last < 0.5).astype(F32)
                move = jnp.where(eye, carry_row, 0.0) - both[:, :C]
                todo.append((at, move, both[:, C:]))

            def chained(move, offset, pair):
                both = fine(move, pair)
                return jnp.concatenate([both[:, :C], both[:, C:] + offset], axis=1)

            def keep(at, pair, offset):
                mcb[chain, at, :] = jnp.concatenate([pair[0][:, :C], pair[1][:, :C]], axis=1)
                ocb[chain, at, :] = offset

            past = []
            for four_of in (todo[:4], todo[4:]):
                one = halves(jnp.concatenate(four_of[0][1:], axis=1))
                two = chained(halves(four_of[1][1]), four_of[1][2], one)
                rest = chained(
                    halves(four_of[3][1]), four_of[3][2], halves(jnp.concatenate(four_of[2][1:], axis=1))
                )
                two_s = halves(two)
                three = chained(halves(four_of[2][1]), four_of[2][2], two_s)
                four = chained(halves(rest[:, :C]), rest[:, C:], two_s)
                four_m = halves(four[:, :C])
                keep(four_of[1][0], one, four_of[0][2])
                keep(four_of[2][0], two_s, two[:, C:])
                keep(four_of[3][0], halves(three[:, :C]), three[:, C:])
                keep(four_of[0][0], four_m, four[:, C:])
                past.append((four_m, four[:, C:]))
            held = maps[chain]
            for move, offset in past:
                held = chained(move, offset, halves(held))
            maps[chain] = held
            return carry

        lax.fori_loop(0, BLOCKS // 8, body, 0)

    def map_copy(chain, src_x, to):
        cut = pl.ds(DK, DK) if src_x == 0 else pl.ds(0, 2 * DK)
        return pltpu.make_async_remote_copy(
            maps_out.at[chain, :, cut], gathered.at[src_x, chain, :, cut],
            pre_send.at[chain, to - 1], pre_recv.at[chain, src_x],
            device_id={"seq": 2 * to + core}, device_id_type=MESH,
        )

    def map_sends(chain, wait):
        for src_x in range(3):

            @pl.when(x == src_x)
            def _():
                for to in range(src_x + 1, 4):
                    copy = map_copy(chain, src_x, to)
                    if wait:
                        copy.wait_send()
                    else:
                        copy.start()

    arrived(0, kb.at[0])
    key_stage(0)
    arrived(1, kb.at[1])
    key_stage(1)
    arrived(2, vb.at[0])
    value_stage(0)
    maps_out[0] = maps[0].astype(BF16)
    map_sends(0, False)
    arrived(3, vb.at[1])
    value_stage(1)
    maps_out[1] = maps[1].astype(BF16)
    map_sends(1, False)

    def query_parts(chain, j):
        at = aligned(j * C, C)
        count_col = cols[j, :, 17 + 8 * chain:18 + 8 * chain]
        count_row = rows[j, 8 * chain + 1:8 * chain + 2, :]
        query = unit(qb[chain, at, :]) * (DK ** -0.5) * grow[chain, at, :]
        sh = shrink[chain, at, :]
        gram = lax.dot_general(
            left_of(halves(query)), jnp.concatenate([sh[:, :C], sh], axis=1),
            (((1,), (1,)), ((), ())), preferred_element_type=F32,
        )
        mix = jnp.where(lower & (count_col == count_row), gram, 0.0)
        live = query * (count_col < 0.5).astype(F32)
        return halves(jnp.concatenate([live, mix], axis=1))

    def incoming_state(chain):
        @pl.when(x == 0)
        def _():
            first[chain] = jnp.zeros((DK, DK), F32)

        for src_x in range(3):

            @pl.when(x > src_x)
            def _():
                map_copy(chain, src_x, src_x + 1).wait_recv()
                if src_x == 0:
                    first[chain] = gathered[0, chain, :, DK:].astype(F32)
                else:
                    move = gathered[src_x, chain, :, 0:DK]
                    first[chain] = gathered[src_x, chain, :, DK:].astype(F32) + dot(
                        jnp.concatenate([move, move], axis=1), stack(*halves(first[chain]))
                    )

    def moved(chain, at, incoming):
        mc = mcb[chain, at, :]
        return ocb[chain, at, :] + dot(jnp.concatenate([mc, mc[:, :C]], axis=1), incoming)

    def state_stage(chain):
        now = first[chain]
        for four in range(BLOCKS // 4):
            incoming = right_of(halves(now))
            states[chain, four] = incoming
            if four < BLOCKS // 4 - 1:
                now = moved(chain, pl.ds(four * 4 * C, C), incoming)

        def body(step, carry):
            todo = []
            for inner in range(8):
                j = step * 8 + inner
                at = aligned(j * C, C)
                incoming = states[chain, step * 2 + inner // 4]
                if inner % 4 == 0:
                    todo.append((j, at, incoming))
                else:
                    todo.append((j, at, right_of(halves(moved(chain, at, incoming)))))
            for j, at, incoming in todo:
                ws = wb[chain, at, :]
                fresh = ub[chain, at, :] - dot(jnp.concatenate([ws, ws[:, :C]], axis=1), incoming)
                fh, fl = halves(fresh)
                right[chain, j] = stack(incoming[C:2 * C], fh, incoming[2 * C:], fl)
            return carry

        lax.fori_loop(0, BLOCKS // 8, body, 0)

    def output_stage(chain):
        def body(step, own):
            p = lax.rem(step + blk // 8, BLOCKS // 4)
            for inner in range(4):
                j = 4 * p + inner
                at = aligned(j * C, C)
                hold = right[chain, j]
                out = dot(left_of(query_parts(chain, j)), stack(hold[:2 * C], hold))
                core_buf[chain, at, :] = out.astype(BF16)
            for inner in range(8):
                b = 8 * p + lax.rem(blk + inner, 8)
                src = core_buf.at[chain, aligned(b * TOK, TOK), :]
                dst = back.at[chain, :, my_cols]
                if own and inner == 0:
                    pltpu.make_async_copy(src, dst, back_recv.at[chain, 0]).start()
                else:
                    pltpu.make_async_remote_copy(
                        src, dst, back_send.at[chain], back_recv.at[chain, step],
                        device_id={"head": lax.rem(b, GROUPS), "seq": seq - core + b // GROUPS},
                        device_id_type=MESH,
                    ).start()

        body(0, True)

        def others(step, carry):
            body(step, False)
            return carry

        lax.fori_loop(1, BLOCKS // 4, others, 0)

    incoming_state(0)
    state_stage(0)
    arrived(4, qb.at[0])
    output_stage(0)
    incoming_state(1)
    state_stage(1)
    arrived(5, qb.at[1])
    output_stage(1)

    for chain in range(2):

        def finish(step, carry, chain=chain):
            some = back.at[chain, :, pl.ds(0, 8 * DK)]
            pltpu.make_async_copy(some, some, back_recv.at[chain, step]).wait()
            q = lax.rem(blk // 8 + 4 - step, 4)
            base = lax.rem(q, 2) * 16 + q // 2
            for inner in range(8):
                at = aligned((base + 2 * inner) * DK, DK)
                wide = back[chain, :, at].astype(F32)
                norm = lax.rsqrt(jnp.mean(wide * wide, axis=-1, keepdims=True) + NORM_EPS)
                out_ref[chain, :, at] = (wide * norm * scale[chain, :, at]).astype(BF16)
            return carry

        lax.fori_loop(0, 4, finish, 0)

    map_sends(0, True)
    map_sends(1, True)

    many = (OWNERS - 1) * DK
    for slot in range(6):
        sent = k_in.at[0, :, pl.ds(0, many)]
        pltpu.make_async_copy(sent, sent, send.at[slot]).wait()
    for chain in range(2):
        sent = back.at[0, :, pl.ds(0, many)]
        pltpu.make_async_copy(sent, sent, back_send.at[chain]).wait()
    for chain in range(2):
        lat_sent = lb.at[chain, pl.ds(0, (GROUPS - 1) * TOK), :]
        pltpu.make_async_copy(lat_sent, lat_sent, send.at[LAT + chain]).wait()
    aux_sent = aux_src.at[pl.ds(0, OWNERS - 1)]
    pltpu.make_async_copy(aux_sent, aux_sent, send.at[AUX]).wait()


def per_device(
    query_rows, key_rows, value_rows, beta_raw, gate_latent, gate_up, dt_bias, decay_log,
    boundary, modality, out_gate, norm_gain,
):
    span = lambda width, dtype: pltpu.VMEM((2, SPAN, width), dtype)
    return pl.pallas_call(
        kernel,
        out_shape=pltpu.VMEM((2, TOK, H * DK), BF16),
        in_specs=[ANY, ANY, ANY, ANY, ANY, ANY, ANY, ANY, ANY, SM, ANY, ANY],
        out_specs=VM,
        scratch_shapes=[
            pltpu.VMEM((2, H, TOK), BF16),
            pltpu.VMEM((2, TOK), jnp.int32),
            pltpu.VMEM((2, TOK), jnp.int32),
            pltpu.VMEM((1, H * DK), F32),
            span(DK, BF16), span(DK, BF16), span(DK, BF16), span(DK, BF16),
            pltpu.VMEM((OWNERS, 8, C), BF16),
            pltpu.VMEM((OWNERS, 8, C), BF16),
            pltpu.VMEM((DK, DK), BF16),
            pltpu.VMEM((2, DK), F32),
            pltpu.VMEM((2, TOK, H * DK), BF16),
            pltpu.VMEM((2, TOK, H * DK), F32),
            span(DK, F32),
            span(DK, F32),
            span(2 * DK, BF16),
            span(DK, F32),
            span(2 * DK, BF16),
            span(DK, BF16),
            span(2 * DK, BF16),
            span(DK, F32),
            span(2 * DK, BF16),
            span(DK, F32),
            pltpu.VMEM((2, BLOCKS, 4 * C, DK), BF16),
            pltpu.VMEM((BLOCKS, C, C), F32),
            pltpu.VMEM((BLOCKS, 16, C), F32),
            pltpu.VMEM((2, DK, 2 * DK), F32),
            pltpu.VMEM((2, DK, DK), F32),
            pltpu.VMEM((2, DK, 2 * DK), BF16),
            pltpu.VMEM((3, 2, DK, 2 * DK), BF16),
            pltpu.VMEM((2, BLOCKS // 4, 3 * C, DK), BF16),
            span(DK, BF16),
            pltpu.VMEM((2, TOK, H * DK), BF16),
            pltpu.SemaphoreType.DMA((11,)),
            pltpu.SemaphoreType.DMA((11,)),
            pltpu.SemaphoreType.DMA((2, 3)),
            pltpu.SemaphoreType.DMA((2, 3)),
            pltpu.SemaphoreType.DMA((2,)),
            pltpu.SemaphoreType.DMA((2, 4)),
            pltpu.SemaphoreType.DMA((7,)),
        ],
        compiler_params=pltpu.CompilerParams(
            collective_id=0, has_side_effects=True, vmem_limit_bytes=60 * 1024 * 1024
        ),
        name="delta_attention",
    )(
        query_rows, key_rows, value_rows, beta_raw.transpose(0, 2, 1), boundary, modality, gate_latent, gate_up, dt_bias, decay_log,
        out_gate, norm_gain.reshape(1, -1),
    )


def solution(mesh):
    rows = P(None, ("seq", "head"), None)
    flat = P(None, ("seq", "head"))
    return jax.shard_map(
        per_device,
        mesh=mesh,
        in_specs=(rows, rows, rows, rows, rows, P(), P(), P(), flat, flat, rows, P()),
        out_specs=rows,
        check_vma=False,
    )
```
